256 devices in a mesh: section: 4 (over x_hi, core), tp: 2 (over x_lo), doc: 32 (over z, y).
Axes of the slice: x: 4 (x_hi: 2, x_lo: 2; x = x_hi * 2 + x_lo), y: 4, z: 8, core: 2. Of those that a mesh axis runs over, the one named last changes fastest.
Arguments:
- token_ids: int32 [64, 2, 32], P('doc'), may hold values from 0 to 16383
- seg_lengths: int32 [64, 2], P('doc'), may hold values from 1 to 32
- emb_table: bfloat16 [16384, 4096], P('section', 'tp'), may hold values from -6 to 6
- mem_init: bfloat16 [16, 4096], P(None, 'tp'), may hold values from -6 to 6
- norm_gain: float32 [4, 4096], P('section'), may hold values from 0.1 to 1.9
- w_query: bfloat16 [4, 4096, 2048], P('section', 'doc', 'tp'), may hold values from -0.09375 to 0.09375
- w_key: bfloat16 [4, 4096, 2048], P('section', 'doc', 'tp'), may hold values from -0.09375 to 0.09375
- w_value: bfloat16 [4, 4096, 2048], P('section', 'doc', 'tp'), may hold values from -0.09375 to 0.09375
- w_out: bfloat16 [4, 2048, 4096], P('section', None, 'tp'), may hold values from -0.125 to 0.125
- layer_mix: float32 [4], P('section'), may hold values from 0.5 to 4.5
Outputs:
- pooled: float32 [64, 4096], P(None, 'tp')
The draws below stay inside these ranges and needn't reach their ends.
All inputs are finite; a program needn't handle non-finite values.
Results may differ from the reference program's by a relative error of at most 0.013.
Values may be sent and summed in bfloat16 or wider, within the bound.
A program may use at most 192 MiB of HBM per device.

```python
import math
import jax
import jax.numpy as jnp
import numpy as np
from jax import lax

D = 4096
HD = 128
HEADS = 16
VOCAB = 16384
M = 16
L = 32
SEGS = 2
SECTIONS = 4
DOCS = 64


def draw_layer_mix(key, part):
    position = jnp.arange(SECTIONS).astype(jnp.float32)
    rising = 1.0 + 2.0 * position / max(SECTIONS - 1, 1)
    factor = jax.random.uniform(jax.random.fold_in(key, 31), (SECTIONS,), jnp.float32, 0.7, 1.3)
    return (rising * factor).astype(jnp.float32)


def set_ends(values, stream_key, low, largest):
    extent = values.shape
    index_at = [jax.random.randint(jax.random.fold_in(stream_key, axis), (), 0, extent[axis]) for axis in range(len(extent))]
    values = values.at[tuple(index_at)].set(low)
    longest = extent.index(max(extent))
    index_at[longest] = (index_at[longest] + 1) % extent[longest]
    return values.at[tuple(index_at)].set(largest)


def levels(own_key, dims, split, low, largest):
    factor_of = 1.0
    for dim, blocks in split:
        heights = jax.random.uniform(jax.random.fold_in(jax.random.fold_in(own_key, 6), dim), (blocks,), jnp.float32, low / len(split), largest / len(split))
        factor_of = factor_of * jnp.repeat(jnp.exp(heights), dims[dim] // blocks).reshape((-1,) + (1,) * (len(dims) - 1 - dim))
    return factor_of


def rank_bounds(number_of, slope):
    portions = [(1 << 20) // math.isqrt(rank ** slope) + 1 for rank in range(1, number_of + 1)]
    scale = 1 + sum(portions) // (1 << 30)
    return np.cumsum(np.array([max(1, weight // scale) for weight in portions]))


def ranked(stream_key, extent, number_of, slope):
    table = rank_bounds(number_of, slope)
    lot = jax.random.randint(jax.random.fold_in(stream_key, 1), extent, 0, int(table[number_of - 1]))
    grade = jnp.searchsorted(jnp.asarray(table, jnp.int32), lot, side="right")
    return jax.random.permutation(jax.random.fold_in(stream_key, 2), number_of)[grade].astype(jnp.int32)


def normal_values(rng, extent, spread, most, cuts=(), held_as=jnp.bfloat16):
    array = jax.random.normal(rng, extent, jnp.float32) * spread
    if len(cuts) > 0:
        array = levels(rng, extent, cuts, -0.22, 0.18) * array
    return jnp.clip(array, min=-most, max=most).astype(held_as)


def setup_inputs(seed: int = 0) -> dict:
    key_of = jax.random.split(jax.random.key(seed), 11)
    token_ids = set_ends(ranked(key_of[0], (DOCS, SEGS, L), VOCAB, 2), jax.random.fold_in(key_of[0], 3), 0, VOCAB - 1).astype(jnp.int32)
    seg_lengths = set_ends(jax.random.randint(key_of[1], (DOCS, SEGS), 1, L + 1), jax.random.fold_in(key_of[1], 1), 1, L).astype(jnp.int32)
    emb_table = normal_values(key_of[2], (VOCAB, D), 1.0, 6.0, ((0, 4), (1, 2)))
    mem_init = normal_values(key_of[3], (M, D), 1.0, 6.0, ((1, 2),))
    norm_gain = jnp.clip(1.0 + 0.18 * jax.random.normal(key_of[4], (SECTIONS, D), jnp.float32), 0.1, 1.9)
    w_query = normal_values(key_of[5], (SECTIONS, D, HEADS * HD), D ** -0.5, 0.09375, ((0, 4), (1, 32), (2, 2)))
    w_key = normal_values(key_of[6], (SECTIONS, D, HEADS * HD), D ** -0.5, 0.09375, ((0, 4), (1, 32), (2, 2)))
    w_value = normal_values(key_of[7], (SECTIONS, D, HEADS * HD), D ** -0.5, 0.09375, ((0, 4), (1, 32), (2, 2)))
    w_out = normal_values(key_of[8], (SECTIONS, HEADS * HD, D), (HEADS * HD) ** -0.5, 0.125, ((0, 4), (2, 2)))
    layer_mix = draw_layer_mix(jax.random.fold_in(key_of[10], 71), 0)
    return dict(token_ids=token_ids, seg_lengths=seg_lengths, emb_table=emb_table, mem_init=mem_init, norm_gain=norm_gain, w_query=w_query, w_key=w_key, w_value=w_value, w_out=w_out, layer_mix=layer_mix)


EPSILON = 1e-05
NEGATIVE = -1e+30

def visible_mask(row_count, lengths):
    position = jnp.arange(row_count)
    key_ok = (position[None, :] < M) | (position[None, :] - M < lengths[:, None])
    ordered = (position[None, :] < M) | (position[:, None] < M) | (position[None, :] <= position[:, None])
    return key_ok[:, None, None, :] & ordered[None, None, :, :]

def layer_apply(hidden, lengths, query_proj, key_proj, value_proj, out_proj, norm_row):
    doc_count, row_count, width = hidden.shape
    floats = hidden.astype(jnp.float32)
    mean_square = lax.optimization_barrier(jnp.mean(floats * floats, -1, keepdims=True))
    normed = (floats * lax.rsqrt(mean_square + EPSILON) * norm_row).astype(jnp.bfloat16)
    normed_wide = normed.astype(jnp.float32)
    queries = jnp.einsum('brd,dk->brk', normed_wide, query_proj.astype(jnp.float32)).astype(jnp.bfloat16)
    keys = jnp.einsum('brd,dk->brk', normed_wide, key_proj.astype(jnp.float32)).astype(jnp.bfloat16)
    values = jnp.einsum('brd,dk->brk', normed_wide, value_proj.astype(jnp.float32)).astype(jnp.bfloat16)
    head_shape = (doc_count, row_count, HEADS, HD)
    scores = jnp.einsum('bqhe,bkhe->bhqk', queries.reshape(head_shape).astype(jnp.float32), keys.reshape(head_shape).astype(jnp.float32)) * (1.0 / math.sqrt(HD))
    allowed = visible_mask(row_count, lengths)
    scores = jnp.where(allowed, scores, NEGATIVE)
    weights = jnp.where(allowed, jnp.exp(scores), 0.0)
    probs = (weights / lax.optimization_barrier(jnp.sum(weights, -1, keepdims=True))).astype(jnp.bfloat16)
    mixed = jnp.einsum('bhqk,bkhe->bqhe', probs.astype(jnp.float32), values.reshape(head_shape).astype(jnp.float32)).astype(jnp.bfloat16)
    update = jnp.einsum('brk,kd->brd', mixed.reshape(doc_count, row_count, HEADS * HD).astype(jnp.float32), out_proj.astype(jnp.float32))
    return (floats + update).astype(jnp.bfloat16)

def reference(token_ids, seg_lengths, emb_table, mem_init, norm_gain, w_query, w_key, w_value, w_out, layer_mix):
    embedded = jnp.take(emb_table, token_ids, axis=0)
    doc_count = token_ids.shape[0]
    memory = jnp.broadcast_to(mem_init, (doc_count, M, mem_init.shape[1]))
    position = jnp.arange(L)
    pooled_layers = None
    for segment in range(SEGS):
        hidden = jnp.concatenate([memory, embedded[:, segment]], 1)
        lengths = seg_lengths[:, segment]
        token_ok = position[None, :] < lengths[:, None]

        def layer_step(carried, params):
            query_proj, key_proj, value_proj, out_proj, norm_row, mixing = params
            result = layer_apply(carried, lengths, query_proj, key_proj, value_proj, out_proj, norm_row)
            summed = lax.optimization_barrier(jnp.sum(jnp.where(token_ok[:, :, None], result[:, M:].astype(jnp.float32), 0.0), 1))
            return (result, mixing * summed / lengths[:, None].astype(jnp.float32))
        hidden, pooled_layers = lax.scan(layer_step, hidden, (w_query, w_key, w_value, w_out, norm_gain, layer_mix))
        memory = hidden[:, :M]
    return lax.optimization_barrier(jnp.sum(pooled_layers, 0))
```

```python
import math

import jax
import jax.numpy as jnp
from jax import lax
from jax.experimental import pallas as pl
from jax.experimental.pallas import tpu as pltpu
from jax.sharding import PartitionSpec as P

HD = 128
M = 16
L = 32
SEGS = 2
ROWS = M + L
EPSILON = 1e-05
NEGATIVE = -1e30

NY = 4
NZ = 8
KEEP = 80
BOTH = 48
WAVES = 2
NSEC = 4


def kernel(
    tok_ref,
    mem_ref,
    gain_ref,
    len_ref,
    mix_ref,
    wq_ref,
    wk_ref,
    wv_ref,
    wo_ref,
    out_ref,
    weights,
    w_out,
    blocks,
    scaled,
    qkv,
    mixed,
    heads,
    result,
    parts,
    lens,
    lens_in,
    pool_row,
    pool,
    pool_in,
    total,
    cast,
    local_sem,
    y_send,
    y_recv,
    z_send,
    z_recv,
    f_send,
    f_recv,
    len_sem,
    part_send,
    part_recv,
    tok_send,
    tok_recv,
    x_send,
    x_recv,
    a_send,
    a_recv,
    pool_send,
    pool_recv,
    total_send,
    total_recv,
    cast_send,
    cast_recv,
    go_sem,
):
    sec = lax.axis_index("section")
    tp = lax.axis_index("tp")
    doc = lax.axis_index("doc")
    z = doc // NY
    y = doc % NY
    bit = y % 2
    y_mate = y + 1 - 2 * bit
    y_twin = NY - 1 - y
    y_far = NY - 1 - y_mate
    kind = ((y + 1) // 2) % 2
    width = blocks.shape[-1]
    per = w_out.shape[0] // 4
    depth = wq_ref.shape[0]
    slab = NY * depth
    pair = 2 * depth

    def where(section, t, d):
        return {"section": section, "tp": t, "doc": d}

    def remote(src, dst, send, recv, to):
        return pltpu.make_async_remote_copy(
            src_ref=src,
            dst_ref=dst,
            send_sem=send,
            recv_sem=recv,
            device_id=to,
            device_id_type=pl.DeviceIdType.MESH,
        )

    def at_y(other):
        return where(sec, tp, z * NY + other)

    def kind_of(other):
        return ((other + 1) // 2) % 2

    def column(which, other):
        start = pl.multiple_of(kind_of(other) * per, per)
        return pl.ds(start, per)

    sources = (wq_ref, wk_ref, wv_ref)
    own_row = pl.multiple_of(doc * depth, depth)
    both_from = (1 - bit) * KEEP

    own_copies = [
        pltpu.make_async_copy(
            ref.at[:, column(j, y)],
            weights.at[pl.ds(own_row, depth), pl.ds(j * per, per)],
            local_sem.at[j],
        )
        for j, ref in enumerate(sources)
    ]
    wo_copy = pltpu.make_async_copy(wo_ref, w_out, local_sem.at[3])

    def y_copy(n, j, other):
        ref = sources[j]
        if n == 0:
            src = ref.at[:, column(j, other)]
            dst = weights.at[pl.ds(own_row, depth), pl.ds(j * per, per)]
        else:
            first = pl.multiple_of(both_from, 16)
            src = ref.at[pl.ds(first, BOTH), column(j, other)]
            dst = weights.at[
                pl.ds(pl.multiple_of(own_row + both_from, 16), BOTH), pl.ds(j * per, per)
            ]
        return remote(src, dst, y_send.at[n, j], y_recv.at[n, j], at_y(other))

    y_copies = [
        y_copy(n, j, other) for n, other in enumerate((y_mate, y_twin, y_far)) for j in range(3)
    ]

    def rows_a(zz):
        return pl.ds(pl.multiple_of(zz * slab + (y // 2) * pair, pair), pair)

    def rows_b(zz):
        return pl.ds(
            pl.multiple_of(zz * slab + (1 - y // 2) * pair + KEEP, 16), 2 * BOTH
        )

    def chunk_of(way, step):
        return (z + NZ - step) % NZ if way == 0 else (z + step) % NZ

    def z_copy(way, step, part):
        zz = chunk_of(way, step)
        ref = weights.at[rows_a(zz) if part == 0 else rows_b(zz)]
        to = (z + 1) % NZ if way == 0 else (z + NZ - 1) % NZ
        return remote(
            ref,
            ref,
            z_send.at[way, step, part],
            z_recv.at[way, step, part],
            where(sec, tp, to * NY + y),
        )

    def z_sent(way, step, part):
        return step < 3 or (step == 3 and part == way)

    def z_arrival(way, step, part):
        zz = chunk_of(way, step + 1)
        ref = weights.at[rows_a(zz) if part == 0 else rows_b(zz)]
        return remote(
            ref,
            ref,
            z_send.at[way, step, part],
            z_recv.at[way, step, part],
            where(sec, tp, z * NY + y_twin),
        )

    def f_copies(slot, zz):
        base = zz * slab + (y // 2) * pair
        out = []
        for h, start in enumerate((base, base + pair - KEEP)):
            ref = weights.at[pl.ds(pl.multiple_of(start, 16), KEEP)]
            out.append(
                remote(ref, ref, f_send.at[slot, h], f_recv.at[slot, h], at_y(y_twin))
            )
        return out

    slot = tp * 2 + bit
    peers = [
        (tp, y_mate, tp * 2 + 1 - bit),
        (1 - tp, y, (1 - tp) * 2 + bit),
        (1 - tp, y_mate, (1 - tp) * 2 + 1 - bit),
    ]
    everyone = [(tp, y, slot)] + peers

    def first_copy(n, w):
        t, other, _ = peers[n]
        ref = blocks.at[w, tp, bit]
        return remote(
            ref, ref, tok_send.at[0, w, n], x_recv.at[w, slot], where(sec, t, z * NY + other)
        )

    def token_copy(n, w):
        t, other, _ = peers[n]
        ref = blocks.at[WAVES + w, tp, bit, pl.ds(M, L)]
        return remote(
            ref, ref, tok_send.at[1, w, n], tok_recv.at[w, slot], where(sec, t, z * NY + other)
        )

    def part_copy(s):
        index = jnp.maximum(sec - 1, 0)
        return remote(
            tok_ref.at[s], parts.at[index, s], part_send.at[s], part_recv.at[index, s], where(0, tp, doc)
        )

    len_copy = remote(lens, lens_in, len_sem.at[0], len_sem.at[1], at_y(y_mate))

    wo_copy.start()
    for copy in own_copies:
        copy.start()
    for copy in y_copies:
        copy.start()

    @pl.when(sec > 0)
    def _():
        for s in range(SEGS):
            part_copy(s).start()

    lane = lax.broadcasted_iota(jnp.int32, (1, 128), 1)
    mine = (lane >= bit * ROWS) & (lane < bit * ROWS + ROWS)
    for t in range(SEGS * WAVES):
        lens[t : t + 1, :] = jnp.where(mine, len_ref[t % WAVES, t // WAVES], 0)
    for t in range(SEGS * WAVES, 8):
        lens[t : t + 1, :] = jnp.zeros((1, 128), jnp.int32)
    len_copy.start()

    for copy in own_copies:
        copy.wait()
    for n in range(3):
        for j in range(3):
            y_copies[n * 3 + j].wait_recv()

    @pl.when(sec % 2 == 1)
    def _():
        pl.semaphore_wait(go_sem, 1)

    for part in range(2):
        for way in range(2):
            z_copy(way, 0, part).start()
    for copy in f_copies(0, z):
        copy.start()

    @pl.when(sec == 0)
    def _():
        for s in range(SEGS):
            for index in range(NSEC - 1):
                remote(
                    tok_ref.at[s],
                    parts.at[index, s],
                    part_send.at[s],
                    part_recv.at[index, s],
                    where(1, tp, doc),
                ).wait_recv()
            own = pltpu.make_async_copy(tok_ref.at[s], parts.at[NSEC - 1, s], local_sem.at[4 + s])
            own.start()
            own.wait()
            for w in range(WAVES):
                rows = parts[0, s, w] + parts[1, s, w] + parts[2, s, w] + parts[3, s, w]
                blocks[s * WAVES + w, tp, bit, M:, :] = rows
                if s == 0:
                    blocks[w, tp, bit, :M, :] = mem_ref[...]
            for w in range(WAVES):
                for n in range(3):
                    (first_copy if s == 0 else token_copy)(n, w).start()

    for step in range(4):
        for part in range(2):
            for way in range(2):
                if z_sent(way, step, part):
                    z_arrival(way, step, part).wait_recv()
                    if z_sent(way, step + 1, part) and step < 3:
                        z_copy(way, step + 1, part).start()
                    if part == 0:
                        for copy in f_copies(1 + step + 4 * way, chunk_of(way, step + 1)):
                            copy.start()

    for step in range(4):
        for part in range(2):
            for way in range(2):
                if z_sent(way, step, part):
                    z_copy(way, step, part).wait_send()

    @pl.when(sec % 2 == 0)
    def _():
        pl.semaphore_signal(
            go_sem, inc=1, device_id=where(sec + 1, tp, doc), device_id_type=pl.DeviceIdType.MESH
        )

    for k in range(8):
        for copy in f_copies(k, z):
            copy.wait()
    for copy in y_copies:
        copy.wait_send()
    wo_copy.wait()
    len_copy.wait()

    def b_copy(t, n):
        to_tp, other, _ = everyone[n]
        ref = result.at[t]
        dst = blocks.at[t, tp, bit]
        return remote(
            ref, dst, x_send.at[t, n], x_recv.at[t, slot], where((sec + 1) % NSEC, to_tp, z * NY + other)
        )

    def m_copy(t, n):
        to_tp, other, _ = everyone[n]
        return remote(
            result.at[t, pl.ds(0, M)],
            blocks.at[t + WAVES, tp, bit, pl.ds(0, M)],
            x_send.at[t, n],
            x_recv.at[t + WAVES, slot],
            where(0, to_tp, z * NY + other),
        )

    def arrival(t, source, rows, sem):
        ref = blocks.at[t, source // 2, source % 2, rows]
        return remote(ref, ref, x_send.at[0, 0], sem, at_y(y_mate))

    head_slot = tp * 2 + kind
    a_peers = [
        (1 - tp, y, bit, (1 - tp) * 2 + kind),
        (tp, y_mate, 1 - bit, tp * 2 + 1 - kind),
        (1 - tp, y_mate, 1 - bit, (1 - tp) * 2 + 1 - kind),
    ]

    def a_copy(t, n):
        to_tp, other, which, _ = a_peers[n]
        return remote(
            mixed.at[t, which],
            heads.at[t, head_slot],
            a_send.at[t, n],
            a_recv.at[t, head_slot],
            where(sec, to_tp, z * NY + other),
        )

    def a_arrival(t, n):
        source = a_peers[n][3]
        return remote(
            mixed.at[t, 0], heads.at[t, source], a_send.at[t, n], a_recv.at[t, source], at_y(y_mate)
        )

    def pool_copy(w):
        index = jnp.minimum(sec, NSEC - 2)
        return remote(
            pool.at[w], pool_in.at[index, w], pool_send.at[w], pool_recv.at[index, w], where(NSEC - 1, tp, doc)
        )

    def total_copy(w, to):
        return remote(
            total.at[w], cast, total_send.at[w, to // 2], total_recv, where(to, tp, doc)
        )

    all_rows = pl.ds(0, ROWS)
    scale = 1.0 / math.sqrt(HD)

    def task(t, carry):
        s = t // WAVES
        w = t % WAVES

        @pl.when((sec > 0))
        def _():
            for _, _, source in everyone:
                arrival(t, source, all_rows, x_recv.at[t, source]).wait_recv()

        @pl.when((sec == 0) & (s == 0))
        def _():
            for _, _, source in peers:
                arrival(t, source, all_rows, x_recv.at[t, source]).wait_recv()

        @pl.when((sec == 0) & (s == 1))
        def _():
            for _, _, source in peers:
                arrival(t, source, pl.ds(M, L), tok_recv.at[w, source]).wait_recv()
            for _, _, source in everyone:
                arrival(t, source, pl.ds(0, M), x_recv.at[t, source]).wait_recv()

        step = 256
        square = jnp.zeros((2 * ROWS, step), jnp.float32)
        for half in range(2):
            for c in range(0, width, step):
                x = blocks[t, half, :, :, c : c + step].reshape(2 * ROWS, step).astype(jnp.float32)
                square = square + x * x
                k = half * width + c
                scaled[:, k : k + step] = (x * gain_ref[:, k : k + step]).astype(jnp.bfloat16)
        mean_square = jnp.sum(square, -1, keepdims=True) * (1.0 / (2 * width))
        inverse = lax.rsqrt(mean_square + EPSILON)

        def project(j, carry):
            cols = pl.ds(pl.multiple_of(j * per, per), per)
            out = jnp.dot(scaled[...], weights[:, cols], preferred_element_type=jnp.float32)
            qkv[j] = (out * inverse).astype(jnp.bfloat16)
            return carry

        lax.fori_loop(0, 3, project, 0)

        lengths = (lens[pl.ds(t, 1), :] + lens_in[pl.ds(t, 1), :])[:, : 2 * ROWS]
        shape = (2 * ROWS, 2 * ROWS)
        row = lax.broadcasted_iota(jnp.int32, shape, 0)
        col = lax.broadcasted_iota(jnp.int32, shape, 1)
        row_doc = (row >= ROWS).astype(jnp.int32)
        col_doc = (col >= ROWS).astype(jnp.int32)
        i = row - ROWS * row_doc
        j = col - ROWS * col_doc
        allowed = (
            (row_doc == col_doc)
            & ((j < M) | (j - M < lengths))
            & ((j < M) | (i < M) | (j <= i))
        )
        for h in range(per // HD):
            cols = slice(h * HD, (h + 1) * HD)
            scores = (
                lax.dot_general(
                    qkv[0, :, cols],
                    qkv[1, :, cols],
                    (((1,), (1,)), ((), ())),
                    preferred_element_type=jnp.float32,
                )
                * scale
            )
            scores = jnp.where(allowed, scores, NEGATIVE)
            exps = jnp.where(allowed, jnp.exp(scores), 0.0)
            probs = (exps / jnp.sum(exps, -1, keepdims=True)).astype(jnp.bfloat16)
            out = jnp.dot(probs, qkv[2, :, cols], preferred_element_type=jnp.float32)
            mixed[t, :, :, cols] = out.astype(jnp.bfloat16).reshape(2, ROWS, HD)

        for n in range(3):
            a_copy(t, n).start()
        heads[t, head_slot] = mixed[t, bit]
        for n in range(3):
            a_arrival(t, n).wait_recv()

        length = len_ref[w, s]
        position = lax.broadcasted_iota(jnp.int32, (ROWS, 1), 0)
        token_ok = (position >= M) & (position - M < length)
        factor = mix_ref[0] / length.astype(jnp.float32)

        def finish(j, carry):
            cols = pl.ds(pl.multiple_of(j * 512, 512), 512)
            every = jnp.concatenate([heads[t, q] for q in range(4)], axis=1)
            update = jnp.dot(every, w_out[:, cols], preferred_element_type=jnp.float32)
            out = (blocks[t, tp, bit, :, cols].astype(jnp.float32) + update).astype(jnp.bfloat16)
            result[t, :, cols] = out
            summed = jnp.sum(jnp.where(token_ok, out.astype(jnp.float32), 0.0), 0, keepdims=True)
            pool_row[:, cols] = summed * factor
            return carry

        lax.fori_loop(0, width // 512, finish, 0)

        @pl.when(sec < NSEC - 1)
        def _():
            for n in range(4):
                b_copy(t, n).start()

        @pl.when((sec == NSEC - 1) & (s == 0))
        def _():
            for n in range(4):
                m_copy(t, n).start()

        @pl.when(s == 1)
        def _():
            for k in range(width // 128):
                pool[w, k : k + 1, :] = pool_row[:, k * 128 : (k + 1) * 128]

            @pl.when(sec < NSEC - 1)
            def _():
                pool_copy(w).start()

            @pl.when(sec == NSEC - 1)
            def _():
                for index in range(NSEC - 1):
                    remote(
                        pool.at[w],
                        pool_in.at[index, w],
                        pool_send.at[w],
                        pool_recv.at[index, w],
                        where(0, tp, doc),
                    ).wait_recv()
                summed = pool[w] + pool_in[0, w] + pool_in[1, w] + pool_in[2, w]
                total[w] = summed

                @pl.when(w == 0)
                def _():
                    total_copy(0, 0).start()
                    total_copy(0, 2).start()

                @pl.when(w == 1)
                def _():
                    total_copy(1, 1).start()
                    cast[...] = summed

        return carry

    lax.fori_loop(0, SEGS * WAVES, task, 0)

    core = sec % 2
    base = sec - core
    n_docs = NY * NZ

    @pl.when(sec < NSEC - 1)
    def _():
        remote(
            total.at[0], cast, total_send.at[0, 0], total_recv, where(NSEC - 1, tp, doc)
        ).wait_recv()

    def cast_copy(k, which):
        to = base + core if which == 0 else base + 1 - core
        return remote(
            cast,
            out_ref.at[2 * doc + core],
            cast_send.at[which, k],
            cast_recv.at[core, doc],
            where(to, tp, (doc + k) % n_docs),
        )

    cast_copy(0, 1).start()

    def send_row(k, carry):
        cast_copy(k, 0).start()
        cast_copy(k, 1).start()
        return carry

    lax.fori_loop(1, n_docs, send_row, 0)
    out_ref[2 * doc + core] = cast[...]

    def row_arrival(c, d):
        return remote(
            cast, out_ref.at[2 * d + c], cast_send.at[0, 0], cast_recv.at[c, d], where(base + 1 - core, tp, doc)
        )

    row_arrival(1 - core, doc).wait_recv()

    def take_row(k, carry):
        d = (doc + k) % n_docs
        row_arrival(core, d).wait_recv()
        row_arrival(1 - core, d).wait_recv()
        return carry

    lax.fori_loop(1, n_docs, take_row, 0)

    cast_copy(0, 1).wait_send()

    def sent_row(k, carry):
        cast_copy(k, 0).wait_send()
        cast_copy(k, 1).wait_send()
        return carry

    lax.fori_loop(1, n_docs, sent_row, 0)

    @pl.when(sec > 0)
    def _():
        for s in range(SEGS):
            part_copy(s).wait_send()

    @pl.when(sec == 0)
    def _():
        for w in range(WAVES):
            for n in range(3):
                first_copy(n, w).wait_send()
                token_copy(n, w).wait_send()

    def sent_task(t, carry):
        for n in range(3):
            a_copy(t, n).wait_send()

        @pl.when(sec < NSEC - 1)
        def _():
            for n in range(4):
                b_copy(t, n).wait_send()

        @pl.when((sec == NSEC - 1) & (t < WAVES))
        def _():
            for n in range(4):
                m_copy(t, n).wait_send()

        return carry

    lax.fori_loop(0, SEGS * WAVES, sent_task, 0)

    @pl.when(sec < NSEC - 1)
    def _():
        for w in range(WAVES):
            pool_copy(w).wait_send()

    @pl.when(sec == NSEC - 1)
    def _():
        total_copy(0, 0).wait_send()
        total_copy(0, 2).wait_send()
        total_copy(1, 1).wait_send()


def body(
    token_ids,
    seg_lengths,
    emb_table,
    mem_init,
    norm_gain,
    w_query,
    w_key,
    w_value,
    w_out,
    layer_mix,
):
    doc_local = token_ids.shape[0]
    vocab_rows, width = emb_table.shape
    flat_ids = jnp.transpose(token_ids, (1, 0, 2)).reshape(-1)
    local_ids = flat_ids - lax.axis_index("section") * vocab_rows
    owned = (local_ids >= 0) & (local_ids < vocab_rows)
    picked = jnp.take(emb_table, jnp.clip(local_ids, 0, vocab_rows - 1), axis=0)
    tokens = jnp.where(owned[:, None], picked, jnp.zeros((), picked.dtype))
    tokens = tokens.reshape(SEGS, doc_local, L, width)
    depth, head_cols = w_query.shape[1:]
    per = head_cols // 2
    n_tasks = SEGS * WAVES
    dma = pltpu.SemaphoreType.DMA
    bf16, f32 = jnp.bfloat16, jnp.float32
    any_space = pl.BlockSpec(memory_space=pl.ANY)
    vmem = pl.BlockSpec(memory_space=pltpu.VMEM)
    smem = pl.BlockSpec(memory_space=pltpu.SMEM)
    lanes = width // 128
    rows = pl.pallas_call(
        kernel,
        out_shape=jax.ShapeDtypeStruct((NY * NZ * WAVES, lanes, 128), f32),
        in_specs=[any_space, vmem, vmem, smem, smem, any_space, any_space, any_space, any_space],
        out_specs=vmem,
        scratch_shapes=[
            pltpu.VMEM((2 * width, 3 * per), bf16),
            pltpu.VMEM((2 * head_cols, width), bf16),
            pltpu.VMEM((n_tasks, 2, 2, ROWS, width), bf16),
            pltpu.VMEM((2 * ROWS, 2 * width), bf16),
            pltpu.VMEM((3, 2 * ROWS, per), bf16),
            pltpu.VMEM((n_tasks, 2, ROWS, per), bf16),
            pltpu.VMEM((n_tasks, 4, ROWS, per), bf16),
            pltpu.VMEM((n_tasks, ROWS, width), bf16),
            pltpu.VMEM((NSEC, SEGS, WAVES, L, width), bf16),
            pltpu.VMEM((8, 128), jnp.int32),
            pltpu.VMEM((8, 128), jnp.int32),
            pltpu.VMEM((1, width), f32),
            pltpu.VMEM((WAVES, lanes, 128), f32),
            pltpu.VMEM((NSEC - 1, WAVES, lanes, 128), f32),
            pltpu.VMEM((WAVES, lanes, 128), f32),
            pltpu.VMEM((lanes, 128), f32),
            dma((6,)),
            dma((3, 3)),
            dma((3, 3)),
            dma((2, 4, 2)),
            dma((2, 4, 2)),
            dma((8, 2)),
            dma((8, 2)),
            dma((2,)),
            dma((SEGS,)),
            dma((NSEC - 1, SEGS)),
            dma((SEGS, WAVES, 3)),
            dma((WAVES, 4)),
            dma((n_tasks, 4)),
            dma((n_tasks, 4)),
            dma((n_tasks, 3)),
            dma((n_tasks, 4)),
            dma((WAVES,)),
            dma((NSEC - 1, WAVES)),
            dma((WAVES, 2)),
            dma,
            dma((2, NY * NZ)),
            dma((2, NY * NZ)),
            pltpu.SemaphoreType.REGULAR,
        ],
        compiler_params=pltpu.CompilerParams(
            has_side_effects=True, vmem_limit_bytes=48 * 1024 * 1024
        ),
    )(
        tokens,
        mem_init,
        norm_gain,
        seg_lengths,
        layer_mix,
        w_query[0],
        w_key[0],
        w_value[0],
        w_out[0],
    )
    return rows.reshape(NY * NZ * WAVES, width)


def solution(mesh):
    return jax.shard_map(
        body,
        mesh=mesh,
        in_specs=(
            P("doc", None, None),
            P("doc", None),
            P("section", "tp"),
            P(None, "tp"),
            P("section", None),
            P("section", "doc", "tp"),
            P("section", "doc", "tp"),
            P("section", "doc", "tp"),
            P("section", None, "tp"),
            P("section"),
        ),
        out_specs=P(None, "tp"),
        check_vma=False,
    )
```

```python
import math

import jax
import jax.numpy as jnp
from jax import lax
from jax.experimental import pallas as pl
from jax.experimental.pallas import tpu as pltpu
from jax.sharding import PartitionSpec as P

HD = 128
M = 16
L = 32
SEGS = 2
ROWS = M + L
EPSILON = 1e-05
NEGATIVE = -1e30

NY = 4
NZ = 8
KEEP = 80
BOTH = 48
WAVES = 2
NSEC = 4


def kernel(
    ids_hbm,
    table_hbm,
    mem_hbm,
    gain_hbm,
    len_hbm,
    mix_hbm,
    wq_ref,
    wk_ref,
    wv_ref,
    wo_ref,
    out_ref,
    ids_ref,
    table,
    picks,
    mem_ref,
    gain_ref,
    len_ref,
    mix_ref,
    weights,
    w_out,
    blocks,
    scaled,
    qkv_sum,
    qkv,
    mixed,
    heads,
    result,
    parts,
    lens,
    lens_in,
    pool_row,
    pool,
    pool_in,
    total,
    cast,
    local_sem,
    y_send,
    y_recv,
    z_send,
    z_recv,
    f_send,
    f_recv,
    len_sem,
    part_send,
    part_recv,
    tok_send,
    tok_recv,
    x_send,
    x_recv,
    r_send,
    a_send,
    a_recv,
    pool_send,
    pool_recv,
    total_send,
    total_recv,
    cast_send,
    cast_recv,
    go_sem,
):
    sec = lax.axis_index("section")
    tp = lax.axis_index("tp")
    doc = lax.axis_index("doc")
    z = doc // NY
    y = doc % NY
    bit = y % 2
    y_mate = y + 1 - 2 * bit
    y_twin = NY - 1 - y
    y_far = NY - 1 - y_mate
    kind = ((y + 1) // 2) % 2
    width = blocks.shape[-1]
    per = w_out.shape[0] // 4
    depth = wq_ref.shape[0]
    slab = NY * depth
    pair = 2 * depth

    def where(section, t, d):
        return {"section": section, "tp": t, "doc": d}

    def remote(src, dst, send, recv, to):
        return pltpu.make_async_remote_copy(
            src_ref=src,
            dst_ref=dst,
            send_sem=send,
            recv_sem=recv,
            device_id=to,
            device_id_type=pl.DeviceIdType.MESH,
        )

    def at_y(other):
        return where(sec, tp, z * NY + other)

    def kind_of(other):
        return ((other + 1) // 2) % 2

    def column(which, other):
        start = pl.multiple_of(kind_of(other) * per, per)
        return pl.ds(start, per)

    sources = (wq_ref, wk_ref, wv_ref)
    own_row = pl.multiple_of(doc * depth, depth)
    both_from = (1 - bit) * KEEP

    own_copies = [
        pltpu.make_async_copy(
            ref.at[:, column(j, y)],
            weights.at[pl.ds(own_row, depth), pl.ds(j * per, per)],
            local_sem.at[j],
        )
        for j, ref in enumerate(sources)
    ]
    wo_copy = pltpu.make_async_copy(wo_ref, w_out, local_sem.at[3])

    def y_copy(n, j, other):
        ref = sources[j]
        if n == 0:
            src = ref.at[:, column(j, other)]
            dst = weights.at[pl.ds(own_row, depth), pl.ds(j * per, per)]
        else:
            first = pl.multiple_of(both_from, 16)
            src = ref.at[pl.ds(first, BOTH), column(j, other)]
            dst = weights.at[
                pl.ds(pl.multiple_of(own_row + both_from, 16), BOTH), pl.ds(j * per, per)
            ]
        return remote(src, dst, y_send.at[n, j], y_recv.at[n, j], at_y(other))

    y_copies = [
        y_copy(n, j, other) for n, other in enumerate((y_mate, y_twin, y_far)) for j in range(3)
    ]

    def rows_a(zz):
        return pl.ds(pl.multiple_of(zz * slab + (y // 2) * pair, pair), pair)

    def rows_b(zz):
        return pl.ds(
            pl.multiple_of(zz * slab + (1 - y // 2) * pair + KEEP, 16), 2 * BOTH
        )

    def chunk_of(way, step):
        return (z + NZ - step) % NZ if way == 0 else (z + step) % NZ

    def z_copy(way, step, part):
        zz = chunk_of(way, step)
        ref = weights.at[rows_a(zz) if part == 0 else rows_b(zz)]
        to = (z + 1) % NZ if way == 0 else (z + NZ - 1) % NZ
        return remote(
            ref,
            ref,
            z_send.at[way, step, part],
            z_recv.at[way, step, part],
            where(sec, tp, to * NY + y),
        )

    def z_sent(way, step, part):
        return step < 3 or (step == 3 and part == way)

    def z_arrival(way, step, part):
        zz = chunk_of(way, step + 1)
        ref = weights.at[rows_a(zz) if part == 0 else rows_b(zz)]
        return remote(
            ref,
            ref,
            z_send.at[way, step, part],
            z_recv.at[way, step, part],
            where(sec, tp, z * NY + y_twin),
        )

    def f_copies(slot, zz):
        base = zz * slab + (y // 2) * pair
        out = []
        for h, start in enumerate((base, base + pair - KEEP)):
            ref = weights.at[pl.ds(pl.multiple_of(start, 16), KEEP)]
            out.append(
                remote(ref, ref, f_send.at[slot, h], f_recv.at[slot, h], at_y(y_twin))
            )
        return out

    slot = tp * 2 + bit
    peers = [
        (tp, y_mate, tp * 2 + 1 - bit),
        (1 - tp, y, (1 - tp) * 2 + bit),
        (1 - tp, y_mate, (1 - tp) * 2 + 1 - bit),
    ]
    everyone = [(tp, y, slot)] + peers

    def first_copy(n, w):
        t, other, _ = peers[n]
        ref = blocks.at[w, tp, bit]
        return remote(
            ref, ref, tok_send.at[0, w, n], x_recv.at[w, slot], where(sec, t, z * NY + other)
        )

    def token_copy(n, w):
        t, other, _ = peers[n]
        ref = blocks.at[WAVES + w, tp, bit, pl.ds(M, L)]
        return remote(
            ref, ref, tok_send.at[1, w, n], tok_recv.at[w, slot], where(sec, t, z * NY + other)
        )

    def part_copy(s):
        index = jnp.maximum(sec - 1, 0)
        return remote(
            parts.at[NSEC - 1, s], parts.at[index, s], part_send.at[s], part_recv.at[index, s], where(0, tp, doc)
        )

    len_copy = remote(lens, lens_in, len_sem.at[0], len_sem.at[1], at_y(y_mate))

    small_copies = [
        pltpu.make_async_copy(len_hbm, len_ref, local_sem.at[4]),
        pltpu.make_async_copy(mix_hbm, mix_ref, local_sem.at[5]),
        pltpu.make_async_copy(ids_hbm, ids_ref, local_sem.at[6]),
        pltpu.make_async_copy(mem_hbm, mem_ref, local_sem.at[7]),
        pltpu.make_async_copy(gain_hbm.at[:, pl.ds(0, width)], gain_ref.at[0], local_sem.at[8]),
        pltpu.make_async_copy(gain_hbm.at[:, pl.ds(width, width)], gain_ref.at[1], local_sem.at[9]),
    ]
    table_copy = pltpu.make_async_copy(table_hbm, table, local_sem.at[10])
    for copy in small_copies + own_copies:
        copy.start()

    next_sec = (sec + 1) % NSEC
    last_sec = (sec + NSEC - 1) % NSEC
    greeted = [where(sec, tp, z * NY + other) for other in (y_mate, y_twin, y_far)]
    greeted += [where(sec, 1 - tp, z * NY + other) for other in (y, y_mate)]
    greeted += [where(sec, tp, (z + step) % NZ * NY + y) for step in (1, NZ - 1)]
    greeted += [
        where(to, t, z * NY + other)
        for to in (next_sec, last_sec)
        for t in (tp, 1 - tp)
        for other in (y, y_mate)
    ]
    greeted += [where((sec + 2) % NSEC, tp, doc)]
    barrier = pltpu.get_barrier_semaphore()
    for to in greeted:
        pl.semaphore_signal(barrier, inc=1, device_id=to, device_id_type=pl.DeviceIdType.MESH)
    pl.semaphore_wait(barrier, len(greeted))

    for copy in y_copies:
        copy.start()
    table_copy.start()
    wo_copy.start()
    for copy in small_copies:
        copy.wait()

    lane = lax.broadcasted_iota(jnp.int32, (1, 128), 1)
    mine = (lane >= bit * ROWS) & (lane < bit * ROWS + ROWS)
    for t in range(SEGS * WAVES):
        lens[t : t + 1, :] = jnp.where(mine, len_ref[t % WAVES, t // WAVES], 0)
    for t in range(SEGS * WAVES, 8):
        lens[t : t + 1, :] = jnp.zeros((1, 128), jnp.int32)
    len_copy.start()

    for copy in own_copies:
        copy.wait()
    for n in range(3):
        for j in range(3):
            y_copies[n * 3 + j].wait_recv()

    def start_z():
        for part in range(2):
            for way in range(2):
                z_copy(way, 0, part).start()
        for copy in f_copies(0, z):
            copy.start()

    @pl.when(sec % 2 == 0)
    def _():
        start_z()

    n_ids = SEGS * WAVES * L
    eye = lax.broadcasted_iota(jnp.int32, (L, L), 0) == lax.broadcasted_iota(jnp.int32, (L, L), 1)
    columns = [
        jnp.sum(
            jnp.where(eye, ids_ref[w, s : s + 1, :].astype(jnp.float32), 0.0), -1, keepdims=True
        )
        for s in range(SEGS)
        for w in range(WAVES)
    ]
    wanted = jnp.concatenate(columns, axis=0).astype(jnp.int32) - sec * table.shape[0]
    for k in range(0, table.shape[0], 512):
        place = lax.broadcasted_iota(jnp.int32, (n_ids, 512), 1) + k
        picks[:, k : k + 512] = jnp.where(place == wanted, 1.0, 0.0).astype(jnp.bfloat16)
    table_copy.wait()

    def pick(j, carry):
        cols = pl.ds(pl.multiple_of(j * 512, 512), 512)
        rows = jnp.dot(picks[...], table[:, cols], preferred_element_type=jnp.float32)
        parts[NSEC - 1, :, :, :, cols] = rows.astype(jnp.bfloat16).reshape(SEGS, WAVES, L, 512)
        return carry

    lax.fori_loop(0, width // 512, pick, 0)

    @pl.when(sec > 0)
    def _():
        for s in range(SEGS):
            part_copy(s).start()

    @pl.when(sec % 2 == 1)
    def _():
        pl.semaphore_wait(go_sem, 1)
        start_z()

    @pl.when(sec == 0)
    def _():
        for s in range(SEGS):
            for index in range(NSEC - 1):
                remote(
                    parts.at[NSEC - 1, s],
                    parts.at[index, s],
                    part_send.at[s],
                    part_recv.at[index, s],
                    where(1, tp, doc),
                ).wait_recv()
            for w in range(WAVES):
                rows = parts[0, s, w] + parts[1, s, w] + parts[2, s, w] + parts[3, s, w]
                blocks[s * WAVES + w, tp, bit, M:, :] = rows
                if s == 0:
                    blocks[w, tp, bit, :M, :] = mem_ref[...]
            for w in range(WAVES):
                for n in range(3):
                    (first_copy if s == 0 else token_copy)(n, w).start()

    for step in range(4):
        for part in range(2):
            for way in range(2):
                if z_sent(way, step, part):
                    z_arrival(way, step, part).wait_recv()
                    if z_sent(way, step + 1, part) and step < 3:
                        z_copy(way, step + 1, part).start()
                    if part == 0:
                        for copy in f_copies(1 + step + 4 * way, chunk_of(way, step + 1)):
                            copy.start()

    for step in range(4):
        for part in range(2):
            for way in range(2):
                if z_sent(way, step, part):
                    z_copy(way, step, part).wait_send()

    @pl.when(sec % 2 == 0)
    def _():
        pl.semaphore_signal(
            go_sem, inc=1, device_id=where(sec + 1, tp, doc), device_id_type=pl.DeviceIdType.MESH
        )

    for k in range(8):
        for copy in f_copies(k, z):
            copy.wait()
    for copy in y_copies:
        copy.wait_send()
    wo_copy.wait()
    len_copy.wait()

    near = sec % 2 == 0

    def b_copy(t, n):
        to_tp, other, _ = everyone[n]
        return remote(
            result.at[t],
            blocks.at[t, tp, bit],
            x_send.at[t, n],
            x_recv.at[t, slot],
            where((sec + 1) % NSEC, to_tp, z * NY + other),
        )

    hop = [y, y_mate]

    def h_copy(t, n):
        return remote(
            result.at[t],
            blocks.at[t, tp, bit],
            x_send.at[t, n],
            x_recv.at[t, slot],
            where((sec + 1) % NSEC, 1 - tp, z * NY + hop[n]),
        )

    def m_copy(t, n):
        return remote(
            result.at[t, pl.ds(0, M)],
            blocks.at[t + WAVES, tp, bit, pl.ds(0, M)],
            x_send.at[t, n],
            x_recv.at[t + WAVES, slot],
            where(0, 1 - tp, z * NY + hop[n]),
        )

    def forward(t, n, rows):
        which = bit if n == 0 else 1 - bit
        ref = blocks.at[t, 1 - tp, which, rows]
        return remote(
            ref, ref, r_send.at[t, n], x_recv.at[t, (1 - tp) * 2 + which], where(sec, 1 - tp, doc)
        )

    def arrival(t, source, rows, sem):
        ref = blocks.at[t, source // 2, source % 2, rows]
        return remote(ref, ref, x_send.at[0, 0], sem, at_y(y_mate))

    head_slot = tp * 2 + kind
    a_peers = [
        (1 - tp, y, bit, (1 - tp) * 2 + kind),
        (tp, y_mate, 1 - bit, tp * 2 + 1 - kind),
        (1 - tp, y_mate, 1 - bit, (1 - tp) * 2 + 1 - kind),
    ]

    def a_copy(t, n):
        to_tp, other, which, _ = a_peers[n]
        return remote(
            mixed.at[t, which],
            heads.at[t, head_slot],
            a_send.at[t, n],
            a_recv.at[t, head_slot],
            where(sec, to_tp, z * NY + other),
        )

    def a_arrival(t, n):
        source = a_peers[n][3]
        return remote(
            mixed.at[t, 0], heads.at[t, source], a_send.at[t, n], a_recv.at[t, source], at_y(y_mate)
        )

    def pool_copy(w):
        index = jnp.minimum(sec, NSEC - 2)
        return remote(
            pool.at[w], pool_in.at[index, w], pool_send.at[w], pool_recv.at[index, w], where(NSEC - 1, tp, doc)
        )

    def total_copy(w, to):
        return remote(
            total.at[w], cast, total_send.at[w, to // 2], total_recv, where(to, tp, doc)
        )

    all_rows = pl.ds(0, ROWS)
    scale = 1.0 / math.sqrt(HD)

    def task(t, carry):
        s = t // WAVES
        w = t % WAVES

        step = 256
        first = jnp.where(near & ((sec > 0) | (s == 1)), 1 - tp, tp)

        def take(half, rows, t):
            for d in (bit, 1 - bit):
                source = half * 2 + d
                arrival(t, source, rows, x_recv.at[t, source]).wait_recv()

        def wait_half(n):
            half = first if n == 0 else 1 - first

            @pl.when(sec % 2 == 1)
            def _():
                take(half, all_rows, t)

            @pl.when(sec == 2)
            def _():
                for k, d in enumerate((bit, 1 - bit)):
                    source = half * 2 + d
                    arrival(t, source, all_rows, x_recv.at[t, source]).wait_recv()
                    if n == 0:
                        forward(t, k, all_rows).start()

            @pl.when((sec == 0) & (s == 0))
            def _():
                source = half * 2 + 1 - bit
                arrival(t, source, all_rows, x_recv.at[t, source]).wait_recv()
                if n == 1:
                    source = half * 2 + bit
                    arrival(t, source, all_rows, x_recv.at[t, source]).wait_recv()

            @pl.when((sec == 0) & (s == 1))
            def _():
                source = half * 2 + 1 - bit
                arrival(t, source, pl.ds(M, L), tok_recv.at[w, source]).wait_recv()
                if n == 0:
                    source = half * 2 + bit
                    arrival(t, source, pl.ds(M, L), tok_recv.at[w, source]).wait_recv()
                for k, d in enumerate((bit, 1 - bit)):
                    source = half * 2 + d
                    arrival(t, source, pl.ds(0, M), x_recv.at[t, source]).wait_recv()
                    if n == 0:
                        forward(t, k, pl.ds(0, M)).start()

        square = jnp.zeros((2 * ROWS, step), jnp.float32)
        for n in range(2):
            half = first if n == 0 else 1 - first
            wait_half(n)
            for c in range(0, width, step):
                x = blocks[t, half, :, :, c : c + step].reshape(2 * ROWS, step).astype(jnp.float32)
                square = square + x * x
                scaled[:, c : c + step] = (x * gain_ref[half, :, c : c + step]).astype(jnp.bfloat16)
            if n == 1:
                mean_square = jnp.sum(square, -1, keepdims=True) * (1.0 / (2 * width))
                inverse = lax.rsqrt(mean_square + EPSILON)
            rows = pl.ds(pl.multiple_of(half * width, width), width)

            def project(j, carry):
                cols = pl.ds(pl.multiple_of(j * per, per), per)
                out = jnp.dot(scaled[...], weights[rows, cols], preferred_element_type=jnp.float32)
                if n == 0:
                    qkv_sum[j] = out
                else:
                    qkv[j] = ((qkv_sum[j] + out) * inverse).astype(jnp.bfloat16)
                return carry

            lax.fori_loop(0, 3, project, 0)

        lengths = (lens[pl.ds(t, 1), :] + lens_in[pl.ds(t, 1), :])[:, : 2 * ROWS]
        shape = (2 * ROWS, 2 * ROWS)
        row = lax.broadcasted_iota(jnp.int32, shape, 0)
        col = lax.broadcasted_iota(jnp.int32, shape, 1)
        row_doc = (row >= ROWS).astype(jnp.int32)
        col_doc = (col >= ROWS).astype(jnp.int32)
        i = row - ROWS * row_doc
        j = col - ROWS * col_doc
        allowed = (
            (row_doc == col_doc)
            & ((j < M) | (j - M < lengths))
            & ((j < M) | (i < M) | (j <= i))
        )
        for h in range(per // HD):
            cols = slice(h * HD, (h + 1) * HD)
            scores = (
                lax.dot_general(
                    qkv[0, :, cols],
                    qkv[1, :, cols],
                    (((1,), (1,)), ((), ())),
                    preferred_element_type=jnp.float32,
                )
                * scale
            )
            scores = jnp.where(allowed, scores, NEGATIVE)
            exps = jnp.where(allowed, jnp.exp(scores), 0.0)
            probs = (exps / jnp.sum(exps, -1, keepdims=True)).astype(jnp.bfloat16)
            out = jnp.dot(probs, qkv[2, :, cols], preferred_element_type=jnp.float32)
            mixed[t, :, :, cols] = out.astype(jnp.bfloat16).reshape(2, ROWS, HD)

        for n in range(3):
            a_copy(t, n).start()
        heads[t, head_slot] = mixed[t, bit]
        for n in range(3):
            a_arrival(t, n).wait_recv()

        length = len_ref[w, s]
        position = lax.broadcasted_iota(jnp.int32, (ROWS, 1), 0)
        token_ok = (position >= M) & (position - M < length)
        factor = mix_ref[0] / length.astype(jnp.float32)

        def finish(j, carry):
            cols = pl.ds(pl.multiple_of(j * 512, 512), 512)
            every = jnp.concatenate([heads[t, q] for q in range(4)], axis=1)
            update = jnp.dot(every, w_out[:, cols], preferred_element_type=jnp.float32)
            out = (blocks[t, tp, bit, :, cols].astype(jnp.float32) + update).astype(jnp.bfloat16)
            result[t, :, cols] = out
            summed = jnp.sum(jnp.where(token_ok, out.astype(jnp.float32), 0.0), 0, keepdims=True)
            pool_row[:, cols] = summed * factor
            return carry

        lax.fori_loop(0, width // 512, finish, 0)

        @pl.when(near)
        def _():
            for n in range(4):
                b_copy(t, n).start()

        @pl.when(sec == 1)
        def _():
            for n in range(2):
                h_copy(t, n).start()

        @pl.when((sec == NSEC - 1) & (s == 0))
        def _():
            for n in range(2):
                m_copy(t, n).start()

        @pl.when(s == 1)
        def _():
            for k in range(width // 128):
                pool[w, k : k + 1, :] = pool_row[:, k * 128 : (k + 1) * 128]

            @pl.when(sec < NSEC - 1)
            def _():
                pool_copy(w).start()

            @pl.when(sec == NSEC - 1)
            def _():
                for index in range(NSEC - 1):
                    remote(
                        pool.at[w],
                        pool_in.at[index, w],
                        pool_send.at[w],
                        pool_recv.at[index, w],
                        where(0, tp, doc),
                    ).wait_recv()
                summed = pool[w] + pool_in[0, w] + pool_in[1, w] + pool_in[2, w]
                total[w] = summed

                @pl.when(w == 0)
                def _():
                    total_copy(0, 0).start()
                    total_copy(0, 2).start()

                @pl.when(w == 1)
                def _():
                    total_copy(1, 1).start()
                    cast[...] = summed

        return carry

    lax.fori_loop(0, SEGS * WAVES, task, 0)

    core = sec % 2
    base = sec - core
    n_docs = NY * NZ

    @pl.when(sec < NSEC - 1)
    def _():
        remote(
            total.at[0], cast, total_send.at[0, 0], total_recv, where(NSEC - 1, tp, doc)
        ).wait_recv()

    def cast_copy(k, which):
        to = base + core if which == 0 else base + 1 - core
        return remote(
            cast,
            out_ref.at[2 * doc + core],
            cast_send.at[which, k],
            cast_recv.at[core, doc],
            where(to, tp, (doc + k) % n_docs),
        )

    cast_copy(0, 1).start()

    def send_row(k, carry):
        cast_copy(k, 0).start()
        cast_copy(k, 1).start()
        return carry

    lax.fori_loop(1, n_docs, send_row, 0)
    out_ref[2 * doc + core] = cast[...]

    def row_arrival(c, d):
        return remote(
            cast, out_ref.at[2 * d + c], cast_send.at[0, 0], cast_recv.at[c, d], where(base + 1 - core, tp, doc)
        )

    row_arrival(1 - core, doc).wait_recv()

    def take_row(k, carry):
        d = (doc + k) % n_docs
        row_arrival(core, d).wait_recv()
        row_arrival(1 - core, d).wait_recv()
        return carry

    lax.fori_loop(1, n_docs, take_row, 0)

    cast_copy(0, 1).wait_send()

    def sent_row(k, carry):
        cast_copy(k, 0).wait_send()
        cast_copy(k, 1).wait_send()
        return carry

    lax.fori_loop(1, n_docs, sent_row, 0)

    @pl.when(sec > 0)
    def _():
        for s in range(SEGS):
            part_copy(s).wait_send()

    @pl.when(sec == 0)
    def _():
        for w in range(WAVES):
            for n in range(3):
                first_copy(n, w).wait_send()
                token_copy(n, w).wait_send()

    def sent_task(t, carry):
        for n in range(3):
            a_copy(t, n).wait_send()

        @pl.when(near)
        def _():
            for n in range(4):
                b_copy(t, n).wait_send()

        @pl.when(sec == 1)
        def _():
            for n in range(2):
                h_copy(t, n).wait_send()

        @pl.when((sec == NSEC - 1) & (t < WAVES))
        def _():
            for n in range(2):
                m_copy(t, n).wait_send()

        @pl.when(sec == 2)
        def _():
            for n in range(2):
                forward(t, n, all_rows).wait_send()

        @pl.when((sec == 0) & (t >= WAVES))
        def _():
            for n in range(2):
                forward(t, n, pl.ds(0, M)).wait_send()

        return carry

    lax.fori_loop(0, SEGS * WAVES, sent_task, 0)

    @pl.when(sec < NSEC - 1)
    def _():
        for w in range(WAVES):
            pool_copy(w).wait_send()

    @pl.when(sec == NSEC - 1)
    def _():
        total_copy(0, 0).wait_send()
        total_copy(0, 2).wait_send()
        total_copy(1, 1).wait_send()


def body(
    token_ids,
    seg_lengths,
    emb_table,
    mem_init,
    norm_gain,
    w_query,
    w_key,
    w_value,
    w_out,
    layer_mix,
):
    doc_local = token_ids.shape[0]
    vocab_rows, width = emb_table.shape
    depth, head_cols = w_query.shape[1:]
    per = head_cols // 2
    n_tasks = SEGS * WAVES
    dma = pltpu.SemaphoreType.DMA
    bf16, f32 = jnp.bfloat16, jnp.float32
    any_space = pl.BlockSpec(memory_space=pl.ANY)
    vmem = pl.BlockSpec(memory_space=pltpu.VMEM)
    lanes = width // 128
    rows = pl.pallas_call(
        kernel,
        out_shape=jax.ShapeDtypeStruct((NY * NZ * WAVES, lanes, 128), f32),
        in_specs=[any_space] * 10,
        out_specs=vmem,
        scratch_shapes=[
            pltpu.VMEM((WAVES, SEGS, L), jnp.int32),
            pltpu.VMEM((vocab_rows, width), bf16),
            pltpu.VMEM((n_tasks * L, vocab_rows), bf16),
            pltpu.VMEM((M, width), bf16),
            pltpu.VMEM((2, 1, width), f32),
            pltpu.SMEM((doc_local, SEGS), jnp.int32),
            pltpu.SMEM((1,), f32),
            pltpu.VMEM((2 * width, 3 * per), bf16),
            pltpu.VMEM((2 * head_cols, width), bf16),
            pltpu.VMEM((n_tasks, 2, 2, ROWS, width), bf16),
            pltpu.VMEM((2 * ROWS, width), bf16),
            pltpu.VMEM((3, 2 * ROWS, per), f32),
            pltpu.VMEM((3, 2 * ROWS, per), bf16),
            pltpu.VMEM((n_tasks, 2, ROWS, per), bf16),
            pltpu.VMEM((n_tasks, 4, ROWS, per), bf16),
            pltpu.VMEM((n_tasks, ROWS, width), bf16),
            pltpu.VMEM((NSEC, SEGS, WAVES, L, width), bf16),
            pltpu.VMEM((8, 128), jnp.int32),
            pltpu.VMEM((8, 128), jnp.int32),
            pltpu.VMEM((1, width), f32),
            pltpu.VMEM((WAVES, lanes, 128), f32),
            pltpu.VMEM((NSEC - 1, WAVES, lanes, 128), f32),
            pltpu.VMEM((WAVES, lanes, 128), f32),
            pltpu.VMEM((lanes, 128), f32),
            dma((11,)),
            dma((3, 3)),
            dma((3, 3)),
            dma((2, 4, 2)),
            dma((2, 4, 2)),
            dma((8, 2)),
            dma((8, 2)),
            dma((2,)),
            dma((SEGS,)),
            dma((NSEC - 1, SEGS)),
            dma((SEGS, WAVES, 3)),
            dma((WAVES, 4)),
            dma((n_tasks, 4)),
            dma((n_tasks, 4)),
            dma((n_tasks, 2)),
            dma((n_tasks, 3)),
            dma((n_tasks, 4)),
            dma((WAVES,)),
            dma((NSEC - 1, WAVES)),
            dma((WAVES, 2)),
            dma,
            dma((2, NY * NZ)),
            dma((2, NY * NZ)),
            pltpu.SemaphoreType.REGULAR,
        ],
        compiler_params=pltpu.CompilerParams(
            has_side_effects=True, collective_id=0, vmem_limit_bytes=60 * 1024 * 1024
        ),
    )(
        token_ids,
        emb_table,
        mem_init,
        norm_gain,
        seg_lengths,
        layer_mix,
        w_query[0],
        w_key[0],
        w_value[0],
        w_out[0],
    )
    return rows.reshape(NY * NZ * WAVES, width)


def solution(mesh):
    return jax.shard_map(
        body,
        mesh=mesh,
        in_specs=(
            P("doc", None, None),
            P("doc", None),
            P("section", "tp"),
            P(None, "tp"),
            P("section", None),
            P("section", "doc", "tp"),
            P("section", "doc", "tp"),
            P("section", "doc", "tp"),
            P("section", None, "tp"),
            P("section"),
        ),
        out_specs=P(None, "tp"),
        check_vma=False,
    )
```

```python
import math

import jax
import jax.numpy as jnp
from jax import lax
from jax.experimental import pallas as pl
from jax.experimental.pallas import tpu as pltpu
from jax.sharding import PartitionSpec as P

HD = 128
M = 16
L = 32
SEGS = 2
ROWS = M + L
EPSILON = 1e-05
NEGATIVE = -1e30

NY = 4
NZ = 8
KEEP = 80
BOTH = 48
WAVES = 2
NSEC = 4


def kernel(
    ids_hbm,
    table_hbm,
    mem_hbm,
    gain_hbm,
    len_hbm,
    mix_hbm,
    wq_ref,
    wk_ref,
    wv_ref,
    wo_ref,
    out_ref,
    ids_ref,
    table,
    picks,
    mem_ref,
    gain_ref,
    len_ref,
    mix_ref,
    weights2,
    weights4,
    w_out,
    blocks,
    scaled,
    sum2,
    sum4,
    qkv2,
    qkv4,
    mixed2,
    mixed4,
    heads,
    result,
    parts,
    lens,
    pool_row,
    pool,
    pool_in,
    total,
    cast,
    local_sem,
    y_send,
    y_recv,
    z_send,
    z_recv,
    f_send,
    f_recv,
    len_send,
    len_recv,
    part_send,
    part_recv,
    tok_send,
    tok_recv,
    x_send,
    x_recv,
    r_send,
    a_send,
    a_recv,
    pool_send,
    pool_recv,
    total_send,
    total_recv,
    cast_send,
    cast_recv,
    go_sem,
):
    sec = lax.axis_index("section")
    tp = lax.axis_index("tp")
    doc = lax.axis_index("doc")
    z = doc // NY
    y = doc % NY
    bit = y % 2
    y_mate = y + 1 - 2 * bit
    y_twin = NY - 1 - y
    y_far = NY - 1 - y_mate
    kind = ((y + 1) // 2) % 2
    width = blocks.shape[-1]
    depth = wq_ref.shape[0]
    slab = NY * depth
    pair = 2 * depth
    heads_cols = wq_ref.shape[1]

    def where(section, t, d):
        return {"section": section, "tp": t, "doc": d}

    def remote(src, dst, send, recv, to):
        return pltpu.make_async_remote_copy(
            src_ref=src,
            dst_ref=dst,
            send_sem=send,
            recv_sem=recv,
            device_id=to,
            device_id_type=pl.DeviceIdType.MESH,
        )

    def at_y(other):
        return where(sec, tp, z * NY + other)

    wide = sec < 2
    ring = [y, y_mate, y_twin, y_far]
    sources = (wq_ref, wk_ref, wv_ref)
    own_row = pl.multiple_of(doc * depth, depth)
    both_from = (1 - bit) * KEEP

    class Weights:
        def __init__(self, size):
            self.size = size
            self.per = heads_cols // size
            self.ref = weights4 if size == 4 else weights2

        def kind(self, other):
            return other if self.size == 4 else ((other + 1) // 2) % 2

        def column(self, other):
            return pl.ds(pl.multiple_of(self.kind(other) * self.per, self.per), self.per)

        def own_copies(self):
            return [
                pltpu.make_async_copy(
                    ref.at[:, self.column(y)],
                    self.ref.at[pl.ds(own_row, depth), pl.ds(j * self.per, self.per)],
                    local_sem.at[j],
                )
                for j, ref in enumerate(sources)
            ]

        def y_copies(self):
            out = []
            for n, other in enumerate(ring[1:]):
                for j, ref in enumerate(sources):
                    first, rows = 0, depth
                    if self.size == 2 and n > 0:
                        first, rows = pl.multiple_of(both_from, 16), BOTH
                    src = ref.at[pl.ds(first, rows), self.column(other)]
                    dst = self.ref.at[
                        pl.ds(pl.multiple_of(own_row + first, 16), rows),
                        pl.ds(j * self.per, self.per),
                    ]
                    out.append(remote(src, dst, y_send.at[n, j], y_recv.at[n, j], at_y(other)))
            return out

        def rows(self, zz, part):
            if self.size == 4:
                return pl.ds(pl.multiple_of(zz * slab + part * pair, pair), pair)
            if part == 0:
                return pl.ds(pl.multiple_of(zz * slab + (y // 2) * pair, pair), pair)
            return pl.ds(pl.multiple_of(zz * slab + (1 - y // 2) * pair + KEEP, 16), 2 * BOTH)

        def z_copy(self, way, step, part, arrival=False):
            ahead = step + 1 if arrival else step
            zz = (z + NZ - ahead) % NZ if way == 0 else (z + ahead) % NZ
            ref = self.ref.at[self.rows(zz, part)]
            to = (z + 1) % NZ if way == 0 else (z + NZ - 1) % NZ
            return remote(
                ref,
                ref,
                z_send.at[way, step, part],
                z_recv.at[way, step, part],
                where(sec, tp, to * NY + y),
            )

        def f_copies(self, slot, zz):
            if self.size == 4:
                return []
            base = zz * slab + (y // 2) * pair
            out = []
            for h, start in enumerate((base, base + pair - KEEP)):
                ref = self.ref.at[pl.ds(pl.multiple_of(start, 16), KEEP)]
                out.append(
                    remote(ref, ref, f_send.at[slot, h], f_recv.at[slot, h], at_y(y_twin))
                )
            return out

        def start_y(self):
            for copy in self.y_copies():
                copy.start()

        def start_z(self):
            for copy in self.own_copies():
                copy.wait()
            for copy in self.y_copies():
                copy.wait_recv()
            for part in range(2):
                for way in range(2):
                    self.z_copy(way, 0, part).start()
            for copy in self.f_copies(0, z):
                copy.start()

        def relay(self, step):
            for part in range(2):
                for way in range(2):
                    if z_sent(way, step, part):
                        self.z_copy(way, step, part, arrival=True).wait_recv()
                        if z_sent(way, step + 1, part):
                            self.z_copy(way, step + 1, part).start()
                        if part == 0:
                            ahead = step + 1
                            zz = (z + NZ - ahead) % NZ if way == 0 else (z + ahead) % NZ
                            for copy in self.f_copies(1 + step + 4 * way, zz):
                                copy.start()

        def finish(self):
            for step in range(4):
                for part in range(2):
                    for way in range(2):
                        if z_sent(way, step, part):
                            self.z_copy(way, step, part).wait_send()
            for k in range(8):
                for copy in self.f_copies(k, z):
                    copy.wait()
            for copy in self.y_copies():
                copy.wait_send()

    def z_sent(way, step, part):
        return step < 3 or (step == 3 and part == way)

    def each(condition, action):
        @pl.when(condition & wide)
        def _():
            action(Weights(4))

        @pl.when(condition & (sec >= 2))
        def _():
            action(Weights(2))

    slot = tp * NY + y
    peers = [(t, other) for t in (tp, 1 - tp) for other in ring][1:]

    def first_copy(n, w):
        t, other = peers[n]
        ref = blocks.at[w, tp, y]
        return remote(
            ref, ref, tok_send.at[0, w, n], x_recv.at[w, slot], where(sec, t, z * NY + other)
        )

    def token_copy(n, w):
        t, other = peers[n]
        ref = blocks.at[WAVES + w, tp, y, pl.ds(M, L)]
        return remote(
            ref, ref, tok_send.at[1, w, n], tok_recv.at[w, slot], where(sec, t, z * NY + other)
        )

    def part_copy(s):
        index = jnp.maximum(sec - 1, 0)
        return remote(
            parts.at[NSEC - 1, s], parts.at[index, s], part_send.at[s], part_recv.at[index, s], where(0, tp, doc)
        )

    def len_copy(n, arrival=False):
        index = ring[n + 1] if arrival else y
        ref = lens.at[index]
        return remote(ref, ref, len_send.at[n], len_recv.at[n], at_y(ring[n + 1]))


    small_copies = [
        pltpu.make_async_copy(len_hbm, len_ref, local_sem.at[4]),
        pltpu.make_async_copy(mix_hbm, mix_ref, local_sem.at[5]),
        pltpu.make_async_copy(ids_hbm, ids_ref, local_sem.at[6]),
        pltpu.make_async_copy(mem_hbm, mem_ref, local_sem.at[7]),
        pltpu.make_async_copy(gain_hbm.at[:, pl.ds(0, width)], gain_ref.at[0], local_sem.at[8]),
        pltpu.make_async_copy(gain_hbm.at[:, pl.ds(width, width)], gain_ref.at[1], local_sem.at[9]),
    ]
    table_copy = pltpu.make_async_copy(table_hbm, table, local_sem.at[10])
    wo_copy = pltpu.make_async_copy(wo_ref, w_out, local_sem.at[3])
    for copy in small_copies:
        copy.start()
    for group in (Weights(4), Weights(2)):

        @pl.when(wide if group.size == 4 else sec >= 2)
        def _():
            for copy in group.own_copies():
                copy.start()


    next_sec = (sec + 1) % NSEC
    last_sec = (sec + NSEC - 1) % NSEC
    greeted = [where(sec, t, z * NY + other) for t, other in peers]
    greeted += [where(sec, tp, (z + step) % NZ * NY + y) for step in (1, NZ - 1)]
    greeted += [
        where(to, t, z * NY + other)
        for to in (next_sec, last_sec)
        for t in (tp, 1 - tp)
        for other in ring
    ]
    greeted += [where((sec + 2) % NSEC, tp, doc)]
    barrier = pltpu.get_barrier_semaphore()
    for to in greeted:
        pl.semaphore_signal(barrier, inc=1, device_id=to, device_id_type=pl.DeviceIdType.MESH)
    pl.semaphore_wait(barrier, len(greeted))

    each(sec >= 0, Weights.start_y)
    table_copy.start()
    wo_copy.start()
    for copy in small_copies:
        copy.wait()

    lane = lax.broadcasted_iota(jnp.int32, (1, 128), 1)
    mine = (lane >= bit * ROWS) & (lane < bit * ROWS + ROWS)
    for t in range(SEGS * WAVES):
        lens[y, t : t + 1, :] = jnp.where(mine, len_ref[t % WAVES, t // WAVES], 0)
    for t in range(SEGS * WAVES, 8):
        lens[y, t : t + 1, :] = jnp.zeros((1, 128), jnp.int32)
    for n in range(3):
        len_copy(n).start()

    even = sec % 2 == 0
    odd = sec % 2 == 1
    each(even, Weights.start_z)

    n_ids = SEGS * WAVES * L
    eye = lax.broadcasted_iota(jnp.int32, (L, L), 0) == lax.broadcasted_iota(jnp.int32, (L, L), 1)
    columns = [
        jnp.sum(
            jnp.where(eye, ids_ref[w, s : s + 1, :].astype(jnp.float32), 0.0), -1, keepdims=True
        )
        for s in range(SEGS)
        for w in range(WAVES)
    ]
    wanted = jnp.concatenate(columns, axis=0).astype(jnp.int32) - sec * table.shape[0]
    for k in range(0, table.shape[0], 512):
        place = lax.broadcasted_iota(jnp.int32, (n_ids, 512), 1) + k
        picks[:, k : k + 512] = jnp.where(place == wanted, 1.0, 0.0).astype(jnp.bfloat16)
    each(even, lambda group: group.relay(0))
    table_copy.wait()

    def pick(j, carry):
        cols = pl.ds(pl.multiple_of(j * 512, 512), 512)
        rows = jnp.dot(picks[...], table[:, cols], preferred_element_type=jnp.float32)
        parts[NSEC - 1, :, :, :, cols] = rows.astype(jnp.bfloat16).reshape(SEGS, WAVES, L, 512)
        return carry

    lax.fori_loop(0, width // 1024, pick, 0)
    each(even, lambda group: group.relay(1))
    lax.fori_loop(width // 1024, width // 512, pick, 0)

    @pl.when(sec > 0)
    def _():
        for s in range(SEGS):
            part_copy(s).start()

    each(even, lambda group: group.relay(2))

    @pl.when(even)
    def _():
        pl.semaphore_signal(
            go_sem, inc=1, device_id=where(sec + 1, tp, doc), device_id_type=pl.DeviceIdType.MESH
        )

    @pl.when(sec == 0)
    def _():
        for s in range(SEGS):
            for index in range(NSEC - 1):
                remote(
                    parts.at[NSEC - 1, s],
                    parts.at[index, s],
                    part_send.at[s],
                    part_recv.at[index, s],
                    where(1, tp, doc),
                ).wait_recv()
            for w in range(WAVES):
                rows = parts[0, s, w] + parts[1, s, w] + parts[2, s, w] + parts[3, s, w]
                blocks[s * WAVES + w, tp, y, M:, :] = rows
                if s == 0:
                    blocks[w, tp, y, :M, :] = mem_ref[...]
            for w in range(WAVES):
                for n in range(7):
                    (first_copy if s == 0 else token_copy)(n, w).start()

    @pl.when(odd)
    def _():
        pl.semaphore_wait(go_sem, 1)

    def late(group):
        group.start_z()
        for step in range(3):
            group.relay(step)

    each(odd, late)
    each(sec >= 0, lambda group: group.relay(3))
    each(sec >= 0, Weights.finish)
    wo_copy.wait()
    for n in range(3):
        len_copy(n).wait_send()
        len_copy(n, arrival=True).wait_recv()

    near = sec % 2 == 0

    def members(size):
        return ring if size == 4 else ring[:2]

    def b_copy(t, n, size):
        to_tp = tp if n < size else 1 - tp
        other = members(size)[n % size]
        return remote(
            result.at[t],
            blocks.at[t, tp, y],
            x_send.at[t, n],
            x_recv.at[t, slot],
            where((sec + 1) % NSEC, to_tp, z * NY + other),
        )

    def h_copy(t, n):
        return remote(
            result.at[t],
            blocks.at[t, tp, y],
            x_send.at[t, n],
            x_recv.at[t, slot],
            where((sec + 1) % NSEC, 1 - tp, z * NY + ring[n]),
        )

    def m_copy(t, n):
        return remote(
            result.at[t, pl.ds(0, M)],
            blocks.at[t + WAVES, tp, y, pl.ds(0, M)],
            x_send.at[t, n],
            x_recv.at[t + WAVES, slot],
            where(0, 1 - tp, z * NY + ring[n]),
        )

    def forward(t, n, rows):
        ref = blocks.at[t, 1 - tp, ring[n], rows]
        return remote(
            ref, ref, r_send.at[t, n], x_recv.at[t, (1 - tp) * NY + ring[n]], where(sec, 1 - tp, doc)
        )

    def arrival(t, half, other, rows, tokens=False):
        ref = blocks.at[t, half, other, rows]
        source = half * NY + other
        sem = tok_recv.at[t - WAVES, source] if tokens else x_recv.at[t, source]
        return remote(ref, ref, x_send.at[0, 0], sem, at_y(y_mate))

    def head_cols(size, t, other):
        per = heads_cols // size
        start = t * heads_cols + Weights(size).kind(other) * per
        return pl.ds(pl.multiple_of(start, per), per)

    def a_peers(size):
        return [(t, other) for t in (tp, 1 - tp) for other in members(size)][1:]

    def mixed_rows(size, t, other):
        return mixed4.at[t, other] if size == 4 else mixed2.at[t, other % 2]

    def a_copy(t, n, size):
        to_tp, other = a_peers(size)[n]
        return remote(
            mixed_rows(size, t, other),
            heads.at[t, :, head_cols(size, tp, y)],
            a_send.at[t, n],
            a_recv.at[t, slot],
            where(sec, to_tp, z * NY + other),
        )

    def a_arrival(t, n, size):
        from_tp, other = a_peers(size)[n]
        return remote(
            mixed_rows(size, t, other),
            heads.at[t, :, head_cols(size, from_tp, other)],
            a_send.at[t, n],
            a_recv.at[t, from_tp * NY + other],
            at_y(y_mate),
        )

    def pool_copy(w):
        index = jnp.minimum(sec, NSEC - 2)
        return remote(
            pool.at[w], pool_in.at[index, w], pool_send.at[w], pool_recv.at[index, w], where(NSEC - 1, tp, doc)
        )

    def total_copy(w, to):
        return remote(
            total.at[w], cast, total_send.at[w, to // 2], total_recv, where(to, tp, doc)
        )

    all_rows = pl.ds(0, ROWS)
    scale = 1.0 / math.sqrt(HD)

    def attend(t, size):
        s = t // WAVES
        per = heads_cols // size
        docs = members(size)
        n_rows = size * ROWS
        group = Weights(size)
        far = near & ((sec > 0) | (s == 1))
        first = jnp.where(far, 1 - tp, tp)

        def wait_half(n):
            half = first if n == 0 else 1 - first

            @pl.when(odd)
            def _():
                for other in docs:
                    arrival(t, half, other, all_rows).wait_recv()

            if size == 2:

                @pl.when(even)
                def _():
                    for k, other in enumerate(docs):
                        arrival(t, half, other, all_rows).wait_recv()
                        if n == 0:
                            forward(t, k, all_rows).start()

                return

            @pl.when(even & (s == 0))
            def _():
                for other in docs[1 - n :]:
                    arrival(t, half, other, all_rows).wait_recv()

            @pl.when(even & (s == 1))
            def _():
                for other in docs[n:]:
                    arrival(t, half, other, pl.ds(M, L), tokens=True).wait_recv()
                for k, other in enumerate(docs):
                    arrival(t, half, other, pl.ds(0, M)).wait_recv()
                    if n == 0:
                        forward(t, k, pl.ds(0, M)).start()

        step = 128
        total_sum = sum2 if size == 2 else sum4
        qkv = qkv2 if size == 2 else qkv4
        base = pl.multiple_of(y // 2 * 2, 2) if size == 2 else 0
        square = jnp.zeros((n_rows, step), jnp.float32)
        for n in range(2):
            half = first if n == 0 else 1 - first
            wait_half(n)
            for c in range(0, width, step):
                x = blocks[t, half, pl.ds(base, size), :, c : c + step]
                x = x.reshape(n_rows, step).astype(jnp.float32)
                square = square + x * x
                scaled[:n_rows, c : c + step] = (x * gain_ref[half, :, c : c + step]).astype(
                    jnp.bfloat16
                )
            if n == 1:
                mean_square = jnp.sum(square, -1, keepdims=True) * (1.0 / (2 * width))
                inverse = lax.rsqrt(mean_square + EPSILON)
            rows = pl.ds(pl.multiple_of(half * width, width), width)

            def project(j, carry):
                cols = pl.ds(pl.multiple_of(j * per, per), per)
                out = jnp.dot(
                    scaled[:n_rows, :], group.ref[rows, cols], preferred_element_type=jnp.float32
                )
                if n == 0:
                    total_sum[j] = out
                else:
                    qkv[j] = ((total_sum[j] + out) * inverse).astype(jnp.bfloat16)
                return carry

            lax.fori_loop(0, 3, project, 0)

        shape = (2 * ROWS, 2 * ROWS)
        row = lax.broadcasted_iota(jnp.int32, shape, 0)
        col = lax.broadcasted_iota(jnp.int32, shape, 1)
        row_doc = (row >= ROWS).astype(jnp.int32)
        col_doc = (col >= ROWS).astype(jnp.int32)
        i = row - ROWS * row_doc
        j = col - ROWS * col_doc
        ordered = (row_doc == col_doc) & ((j < M) | (i < M) | (j <= i))
        for p in range(size // 2):
            d = base + 2 * p
            lengths = (lens[d, pl.ds(t, 1), :] + lens[d + 1, pl.ds(t, 1), :])[:, : 2 * ROWS]
            allowed = ordered & ((j < M) | (j - M < lengths))
            own = slice(p * 2 * ROWS, (p + 1) * 2 * ROWS)
            for h in range(per // HD):
                cols = slice(h * HD, (h + 1) * HD)
                scores = (
                    lax.dot_general(
                        qkv[0, own, cols],
                        qkv[1, own, cols],
                        (((1,), (1,)), ((), ())),
                        preferred_element_type=jnp.float32,
                    )
                    * scale
                )
                scores = jnp.where(allowed, scores, NEGATIVE)
                exps = jnp.where(allowed, jnp.exp(scores), 0.0)
                probs = (exps / jnp.sum(exps, -1, keepdims=True)).astype(jnp.bfloat16)
                out = jnp.dot(probs, qkv[2, own, cols], preferred_element_type=jnp.float32)
                out = out.astype(jnp.bfloat16).reshape(2, ROWS, HD)
                if size == 4:
                    mixed4[t, 2 * p : 2 * p + 2, :, cols] = out
                else:
                    mixed2[t, :, :, cols] = out

        count = 2 * size - 1
        for n in range(count):
            a_copy(t, n, size).start()
        heads[t, :, head_cols(size, tp, y)] = mixed4[t, y] if size == 4 else mixed2[t, bit]
        for n in range(count):
            a_arrival(t, n, size).wait_recv()

    def task(t, carry):
        s = t // WAVES
        w = t % WAVES

        @pl.when(wide)
        def _():
            attend(t, 4)

        @pl.when(sec >= 2)
        def _():
            attend(t, 2)

        length = len_ref[w, s]
        position = lax.broadcasted_iota(jnp.int32, (ROWS, 1), 0)
        token_ok = (position >= M) & (position - M < length)
        factor = mix_ref[0] / length.astype(jnp.float32)

        def finish(j, carry):
            cols = pl.ds(pl.multiple_of(j * 512, 512), 512)
            update = jnp.dot(heads[t], w_out[:, cols], preferred_element_type=jnp.float32)
            out = (blocks[t, tp, y, :, cols].astype(jnp.float32) + update).astype(jnp.bfloat16)
            result[t, :, cols] = out
            summed = jnp.sum(jnp.where(token_ok, out.astype(jnp.float32), 0.0), 0, keepdims=True)
            pool_row[:, cols] = summed * factor
            return carry

        lax.fori_loop(0, width // 512, finish, 0)

        @pl.when(sec == 0)
        def _():
            for n in range(8):
                b_copy(t, n, 4).start()

        @pl.when(sec == 2)
        def _():
            for n in range(4):
                b_copy(t, n, 2).start()

        @pl.when(sec == 1)
        def _():
            for n in range(2):
                h_copy(t, n).start()

        @pl.when((sec == NSEC - 1) & (s == 0))
        def _():
            for n in range(4):
                m_copy(t, n).start()

        @pl.when(s == 1)
        def _():
            for k in range(width // 128):
                pool[w, k : k + 1, :] = pool_row[:, k * 128 : (k + 1) * 128]

            @pl.when(sec < NSEC - 1)
            def _():
                pool_copy(w).start()

            @pl.when(sec == NSEC - 1)
            def _():
                for index in range(NSEC - 1):
                    remote(
                        pool.at[w],
                        pool_in.at[index, w],
                        pool_send.at[w],
                        pool_recv.at[index, w],
                        where(0, tp, doc),
                    ).wait_recv()
                summed = pool[w] + pool_in[0, w] + pool_in[1, w] + pool_in[2, w]
                total[w] = summed

                @pl.when(w == 0)
                def _():
                    total_copy(0, 0).start()
                    total_copy(0, 2).start()

                @pl.when(w == 1)
                def _():
                    total_copy(1, 1).start()
                    cast[...] = summed

        return carry

    lax.fori_loop(0, SEGS * WAVES, task, 0)

    core = sec % 2
    base = sec - core
    n_docs = NY * NZ

    @pl.when(sec < NSEC - 1)
    def _():
        remote(
            total.at[0], cast, total_send.at[0, 0], total_recv, where(NSEC - 1, tp, doc)
        ).wait_recv()

    def cast_copy(k, which):
        to = base + core if which == 0 else base + 1 - core
        return remote(
            cast,
            out_ref.at[2 * doc + core],
            cast_send.at[which, k],
            cast_recv.at[core, doc],
            where(to, tp, (doc + k) % n_docs),
        )

    cast_copy(0, 1).start()

    def send_row(k, carry):
        cast_copy(k, 0).start()
        cast_copy(k, 1).start()
        return carry

    lax.fori_loop(1, n_docs, send_row, 0)
    out_ref[2 * doc + core] = cast[...]

    def row_arrival(c, d):
        return remote(
            cast, out_ref.at[2 * d + c], cast_send.at[0, 0], cast_recv.at[c, d], where(base + 1 - core, tp, doc)
        )

    row_arrival(1 - core, doc).wait_recv()

    def take_row(k, carry):
        d = (doc + k) % n_docs
        row_arrival(core, d).wait_recv()
        row_arrival(1 - core, d).wait_recv()
        return carry

    lax.fori_loop(1, n_docs, take_row, 0)

    cast_copy(0, 1).wait_send()

    def sent_row(k, carry):
        cast_copy(k, 0).wait_send()
        cast_copy(k, 1).wait_send()
        return carry

    lax.fori_loop(1, n_docs, sent_row, 0)

    @pl.when(sec > 0)
    def _():
        for s in range(SEGS):
            part_copy(s).wait_send()

    @pl.when(sec == 0)
    def _():
        for w in range(WAVES):
            for n in range(7):
                first_copy(n, w).wait_send()
                token_copy(n, w).wait_send()

    def sent_task(t, carry):
        @pl.when(wide)
        def _():
            for n in range(7):
                a_copy(t, n, 4).wait_send()

        @pl.when(sec >= 2)
        def _():
            for n in range(3):
                a_copy(t, n, 2).wait_send()

        @pl.when(sec == 0)
        def _():
            for n in range(8):
                b_copy(t, n, 4).wait_send()

        @pl.when(sec == 2)
        def _():
            for n in range(4):
                b_copy(t, n, 2).wait_send()

        @pl.when(sec == 1)
        def _():
            for n in range(2):
                h_copy(t, n).wait_send()

        @pl.when((sec == NSEC - 1) & (t < WAVES))
        def _():
            for n in range(4):
                m_copy(t, n).wait_send()

        @pl.when(sec == 2)
        def _():
            for n in range(2):
                forward(t, n, all_rows).wait_send()

        @pl.when((sec == 0) & (t >= WAVES))
        def _():
            for n in range(4):
                forward(t, n, pl.ds(0, M)).wait_send()

        return carry

    lax.fori_loop(0, SEGS * WAVES, sent_task, 0)

    @pl.when(sec < NSEC - 1)
    def _():
        for w in range(WAVES):
            pool_copy(w).wait_send()

    @pl.when(sec == NSEC - 1)
    def _():
        total_copy(0, 0).wait_send()
        total_copy(0, 2).wait_send()
        total_copy(1, 1).wait_send()


def body(
    token_ids,
    seg_lengths,
    emb_table,
    mem_init,
    norm_gain,
    w_query,
    w_key,
    w_value,
    w_out,
    layer_mix,
):
    doc_local = token_ids.shape[0]
    vocab_rows, width = emb_table.shape
    depth, head_cols = w_query.shape[1:]
    half, quarter = head_cols // 2, head_cols // 4
    n_tasks = SEGS * WAVES
    dma = pltpu.SemaphoreType.DMA
    bf16, f32 = jnp.bfloat16, jnp.float32
    any_space = pl.BlockSpec(memory_space=pl.ANY)
    vmem = pl.BlockSpec(memory_space=pltpu.VMEM)
    lanes = width // 128
    rows = pl.pallas_call(
        kernel,
        out_shape=jax.ShapeDtypeStruct((NY * NZ * WAVES, lanes, 128), f32),
        in_specs=[any_space] * 10,
        out_specs=vmem,
        scratch_shapes=[
            pltpu.VMEM((WAVES, SEGS, L), jnp.int32),
            pltpu.VMEM((vocab_rows, width), bf16),
            pltpu.VMEM((n_tasks * L, vocab_rows), bf16),
            pltpu.VMEM((M, width), bf16),
            pltpu.VMEM((2, 1, width), f32),
            pltpu.SMEM((doc_local, SEGS), jnp.int32),
            pltpu.SMEM((1,), f32),
            pltpu.VMEM((2 * width, 3 * half), bf16),
            pltpu.VMEM((2 * width, 3 * quarter), bf16),
            pltpu.VMEM((2 * head_cols, width), bf16),
            pltpu.VMEM((n_tasks, 2, NY, ROWS, width), bf16),
            pltpu.VMEM((4 * ROWS, width), bf16),
            pltpu.VMEM((3, 2 * ROWS, half), f32),
            pltpu.VMEM((3, 4 * ROWS, quarter), f32),
            pltpu.VMEM((3, 2 * ROWS, half), bf16),
            pltpu.VMEM((3, 4 * ROWS, quarter), bf16),
            pltpu.VMEM((n_tasks, 2, ROWS, half), bf16),
            pltpu.VMEM((n_tasks, 4, ROWS, quarter), bf16),
            pltpu.VMEM((n_tasks, ROWS, 2 * head_cols), bf16),
            pltpu.VMEM((n_tasks, ROWS, width), bf16),
            pltpu.VMEM((NSEC, SEGS, WAVES, L, width), bf16),
            pltpu.VMEM((NY, 8, 128), jnp.int32),
            pltpu.VMEM((1, width), f32),
            pltpu.VMEM((WAVES, lanes, 128), f32),
            pltpu.VMEM((NSEC - 1, WAVES, lanes, 128), f32),
            pltpu.VMEM((WAVES, lanes, 128), f32),
            pltpu.VMEM((lanes, 128), f32),
            dma((11,)),
            dma((3, 3)),
            dma((3, 3)),
            dma((2, 4, 2)),
            dma((2, 4, 2)),
            dma((8, 2)),
            dma((8, 2)),
            dma((3,)),
            dma((3,)),
            dma((SEGS,)),
            dma((NSEC - 1, SEGS)),
            dma((SEGS, WAVES, 7)),
            dma((WAVES, 8)),
            dma((n_tasks, 8)),
            dma((n_tasks, 8)),
            dma((n_tasks, 4)),
            dma((n_tasks, 7)),
            dma((n_tasks, 8)),
            dma((WAVES,)),
            dma((NSEC - 1, WAVES)),
            dma((WAVES, 2)),
            dma,
            dma((2, NY * NZ)),
            dma((2, NY * NZ)),
            pltpu.SemaphoreType.REGULAR,
        ],
        compiler_params=pltpu.CompilerParams(
            has_side_effects=True, collective_id=0, vmem_limit_bytes=67000000
        ),
    )(
        token_ids,
        emb_table,
        mem_init,
        norm_gain,
        seg_lengths,
        layer_mix,
        w_query[0],
        w_key[0],
        w_value[0],
        w_out[0],
    )
    return rows.reshape(NY * NZ * WAVES, width)


def solution(mesh):
    return jax.shard_map(
        body,
        mesh=mesh,
        in_specs=(
            P("doc", None, None),
            P("doc", None),
            P("section", "tp"),
            P(None, "tp"),
            P("section", None),
            P("section", "doc", "tp"),
            P("section", "doc", "tp"),
            P("section", "doc", "tp"),
            P("section", None, "tp"),
            P("section"),
        ),
        out_specs=P(None, "tp"),
        check_vma=False,
    )
```

```python
import math

import jax
import jax.numpy as jnp
from jax import lax
from jax.experimental import pallas as pl
from jax.experimental.pallas import tpu as pltpu
from jax.sharding import PartitionSpec as P

HD = 128
M = 16
L = 32
SEGS = 2
ROWS = M + L
EPSILON = 1e-05
NEGATIVE = -1e30

NY = 4
NZ = 8
KEEP_EARLY = 112
KEEP_LATE = 80
WAVES = 2
NSEC = 4


def kernel(
    ids_hbm,
    table_hbm,
    mem_hbm,
    gain_hbm,
    len_hbm,
    mix_hbm,
    wq_ref,
    wk_ref,
    wv_ref,
    wo_ref,
    out_ref,
    ids_ref,
    table,
    picks,
    mem_ref,
    gain_ref,
    len_ref,
    mix_ref,
    weights2,
    weights4,
    w_out,
    blocks,
    scaled,
    sum2,
    sum4,
    qkv2,
    qkv4,
    mixed2,
    mixed4,
    heads,
    result,
    parts,
    lens,
    pool_row,
    pool,
    pool_in,
    total,
    cast,
    local_sem,
    y_send,
    y_recv,
    z_send,
    z_recv,
    f_send,
    f_recv,
    len_send,
    len_recv,
    part_send,
    part_recv,
    tok_send,
    tok_recv,
    x_send,
    x_recv,
    r_send,
    a_send,
    a_recv,
    pool_send,
    pool_recv,
    total_send,
    total_recv,
    cast_send,
    cast_recv,
    go_sem,
):
    sec = lax.axis_index("section")
    tp = lax.axis_index("tp")
    doc = lax.axis_index("doc")
    z = doc // NY
    y = doc % NY
    bit = y % 2
    y_mate = y + 1 - 2 * bit
    y_twin = NY - 1 - y
    y_far = NY - 1 - y_mate
    kind = ((y + 1) // 2) % 2
    width = blocks.shape[-1]
    depth = wq_ref.shape[0]
    slab = NY * depth
    pair = 2 * depth
    heads_cols = wq_ref.shape[1]

    def where(section, t, d):
        return {"section": section, "tp": t, "doc": d}

    def remote(src, dst, send, recv, to):
        return pltpu.make_async_remote_copy(
            src_ref=src,
            dst_ref=dst,
            send_sem=send,
            recv_sem=recv,
            device_id=to,
            device_id_type=pl.DeviceIdType.MESH,
        )

    def at_y(other):
        return where(sec, tp, z * NY + other)

    wide = sec == 0
    ring = [y, y_mate, y_twin, y_far]
    sources = (wq_ref, wk_ref, wv_ref)
    own_row = pl.multiple_of(doc * depth, depth)

    class Weights:
        def __init__(self, size, keep=KEEP_LATE):
            self.size = size
            self.keep = keep
            self.both = depth - keep
            self.per = heads_cols // size
            self.ref = weights4 if size == 4 else weights2

        def kind(self, other):
            return other if self.size == 4 else ((other + 1) // 2) % 2

        def column(self, other):
            return pl.ds(pl.multiple_of(self.kind(other) * self.per, self.per), self.per)

        def own_copies(self):
            return [
                pltpu.make_async_copy(
                    ref.at[:, self.column(y)],
                    self.ref.at[pl.ds(own_row, depth), pl.ds(j * self.per, self.per)],
                    local_sem.at[j],
                )
                for j, ref in enumerate(sources)
            ]

        def y_copies(self):
            out = []
            for n, other in enumerate(ring[1:]):
                for j, ref in enumerate(sources):
                    first, rows = 0, depth
                    if self.size == 2 and n > 0:
                        first, rows = pl.multiple_of((1 - bit) * self.keep, 16), self.both
                    src = ref.at[pl.ds(first, rows), self.column(other)]
                    dst = self.ref.at[
                        pl.ds(pl.multiple_of(own_row + first, 16), rows),
                        pl.ds(j * self.per, self.per),
                    ]
                    out.append(remote(src, dst, y_send.at[n, j], y_recv.at[n, j], at_y(other)))
            return out

        def rows(self, zz, part):
            if self.size == 4:
                return pl.ds(pl.multiple_of(zz * slab + part * pair, pair), pair)
            if part == 0:
                return pl.ds(pl.multiple_of(zz * slab + (y // 2) * pair, pair), pair)
            return pl.ds(pl.multiple_of(zz * slab + (1 - y // 2) * pair + self.keep, 16), 2 * self.both)

        def z_copy(self, way, step, part, arrival=False):
            ahead = step + 1 if arrival else step
            zz = (z + NZ - ahead) % NZ if way == 0 else (z + ahead) % NZ
            ref = self.ref.at[self.rows(zz, part)]
            to = (z + 1) % NZ if way == 0 else (z + NZ - 1) % NZ
            return remote(
                ref,
                ref,
                z_send.at[way, step, part],
                z_recv.at[way, step, part],
                where(sec, tp, to * NY + y),
            )

        def f_copies(self, slot, zz):
            if self.size == 4:
                return []
            base = zz * slab + (y // 2) * pair
            out = []
            for h, start in enumerate((base, base + pair - self.keep)):
                ref = self.ref.at[pl.ds(pl.multiple_of(start, 16), self.keep)]
                out.append(
                    remote(ref, ref, f_send.at[slot, h], f_recv.at[slot, h], at_y(y_twin))
                )
            return out

        def start_y(self):
            for copy in self.y_copies():
                copy.start()

        def start_z(self):
            for copy in self.own_copies():
                copy.wait()
            for copy in self.y_copies():
                copy.wait_recv()
            for part in range(2):
                for way in range(2):
                    self.z_copy(way, 0, part).start()
            for copy in self.f_copies(0, z):
                copy.start()

        def relay(self, step):
            for part in range(2):
                for way in range(2):
                    if z_sent(way, step, part):
                        self.z_copy(way, step, part, arrival=True).wait_recv()
                        if z_sent(way, step + 1, part):
                            self.z_copy(way, step + 1, part).start()
                        if part == 0:
                            ahead = step + 1
                            zz = (z + NZ - ahead) % NZ if way == 0 else (z + ahead) % NZ
                            for copy in self.f_copies(1 + step + 4 * way, zz):
                                copy.start()

        def finish(self):
            for step in range(4):
                for part in range(2):
                    for way in range(2):
                        if z_sent(way, step, part):
                            self.z_copy(way, step, part).wait_send()
            for k in range(8):
                for copy in self.f_copies(k, z):
                    copy.wait()
            for copy in self.y_copies():
                copy.wait_send()

    def z_sent(way, step, part):
        return step < 3 or (step == 3 and part == way)

    def each(condition, action):
        @pl.when(condition & wide)
        def _():
            action(Weights(4))

        @pl.when(condition & (sec == 1))
        def _():
            action(Weights(2, KEEP_EARLY))

        @pl.when(condition & (sec >= 2))
        def _():
            action(Weights(2))

    slot = tp * NY + y
    peers = [(t, other) for t in (tp, 1 - tp) for other in ring][1:]

    def first_copy(n, w):
        t, other = peers[n]
        ref = blocks.at[w, tp, y]
        return remote(
            ref, ref, tok_send.at[0, w, n], x_recv.at[w, slot], where(sec, t, z * NY + other)
        )

    def token_copy(n, w):
        t, other = peers[n]
        ref = blocks.at[WAVES + w, tp, y, pl.ds(M, L)]
        return remote(
            ref, ref, tok_send.at[1, w, n], tok_recv.at[w, slot], where(sec, t, z * NY + other)
        )

    def part_copy(s):
        index = jnp.maximum(sec - 1, 0)
        return remote(
            parts.at[NSEC - 1, s], parts.at[index, s], part_send.at[s], part_recv.at[index, s], where(0, tp, doc)
        )

    def len_copy(n, arrival=False):
        index = ring[n + 1] if arrival else y
        ref = lens.at[index]
        return remote(ref, ref, len_send.at[n], len_recv.at[n], at_y(ring[n + 1]))


    small_copies = [
        pltpu.make_async_copy(len_hbm, len_ref, local_sem.at[4]),
        pltpu.make_async_copy(mix_hbm, mix_ref, local_sem.at[5]),
        pltpu.make_async_copy(ids_hbm, ids_ref, local_sem.at[6]),
        pltpu.make_async_copy(mem_hbm, mem_ref, local_sem.at[7]),
        pltpu.make_async_copy(gain_hbm.at[:, pl.ds(0, width)], gain_ref.at[0], local_sem.at[8]),
        pltpu.make_async_copy(gain_hbm.at[:, pl.ds(width, width)], gain_ref.at[1], local_sem.at[9]),
    ]
    table_copy = pltpu.make_async_copy(table_hbm, table, local_sem.at[10])
    wo_copy = pltpu.make_async_copy(wo_ref, w_out, local_sem.at[3])
    for copy in small_copies:
        copy.start()
    for group in (Weights(4), Weights(2)):

        @pl.when(wide if group.size == 4 else sec >= 1)
        def _():
            for copy in group.own_copies():
                copy.start()


    next_sec = (sec + 1) % NSEC
    last_sec = (sec + NSEC - 1) % NSEC
    greeted = [where(sec, t, z * NY + other) for t, other in peers]
    greeted += [where(sec, tp, (z + step) % NZ * NY + y) for step in (1, NZ - 1)]
    greeted += [
        where(to, t, z * NY + other)
        for to in (next_sec, last_sec)
        for t in (tp, 1 - tp)
        for other in ring
    ]
    greeted += [where((sec + 2) % NSEC, tp, doc)]
    barrier = pltpu.get_barrier_semaphore()
    for to in greeted:
        pl.semaphore_signal(barrier, inc=1, device_id=to, device_id_type=pl.DeviceIdType.MESH)
    pl.semaphore_wait(barrier, len(greeted))

    each(sec >= 0, Weights.start_y)
    table_copy.start()
    wo_copy.start()
    for copy in small_copies:
        copy.wait()

    lane = lax.broadcasted_iota(jnp.int32, (1, 128), 1)
    mine = (lane >= bit * ROWS) & (lane < bit * ROWS + ROWS)
    for t in range(SEGS * WAVES):
        lens[y, t : t + 1, :] = jnp.where(mine, len_ref[t % WAVES, t // WAVES], 0)
    for t in range(SEGS * WAVES, 8):
        lens[y, t : t + 1, :] = jnp.zeros((1, 128), jnp.int32)
    for n in range(3):
        len_copy(n).start()

    even = sec % 2 == 0
    odd = sec % 2 == 1
    urgent = sec == 0
    each(even, Weights.start_z)

    n_ids = SEGS * WAVES * L
    eye = lax.broadcasted_iota(jnp.int32, (L, L), 0) == lax.broadcasted_iota(jnp.int32, (L, L), 1)
    columns = [
        jnp.sum(
            jnp.where(eye, ids_ref[w, s : s + 1, :].astype(jnp.float32), 0.0), -1, keepdims=True
        )
        for s in range(SEGS)
        for w in range(WAVES)
    ]
    wanted = jnp.concatenate(columns, axis=0).astype(jnp.int32) - sec * table.shape[0]
    for k in range(0, table.shape[0], 512):
        place = lax.broadcasted_iota(jnp.int32, (n_ids, 512), 1) + k
        picks[:, k : k + 512] = jnp.where(place == wanted, 1.0, 0.0).astype(jnp.bfloat16)
    each(urgent, lambda group: group.relay(0))

    def let_go():
        pl.semaphore_signal(
            go_sem, inc=1, device_id=where(sec + 1, tp, doc), device_id_type=pl.DeviceIdType.MESH
        )

    pl.when(urgent)(let_go)
    table_copy.wait()

    def pick(j, carry):
        cols = pl.ds(pl.multiple_of(j * 512, 512), 512)
        rows = jnp.dot(picks[...], table[:, cols], preferred_element_type=jnp.float32)
        parts[NSEC - 1, :, :, :, cols] = rows.astype(jnp.bfloat16).reshape(SEGS, WAVES, L, 512)
        return carry

    lax.fori_loop(0, width // 1024, pick, 0)
    each(urgent, lambda group: group.relay(1))
    lax.fori_loop(width // 1024, width // 512, pick, 0)

    @pl.when(sec > 0)
    def _():
        for s in range(SEGS):
            part_copy(s).start()

    @pl.when(sec == 0)
    def _():
        for s in range(SEGS):
            for index in range(NSEC - 1):
                remote(
                    parts.at[NSEC - 1, s],
                    parts.at[index, s],
                    part_send.at[s],
                    part_recv.at[index, s],
                    where(1, tp, doc),
                ).wait_recv()
            for w in range(WAVES):
                rows = parts[0, s, w] + parts[1, s, w] + parts[2, s, w] + parts[3, s, w]
                blocks[s * WAVES + w, tp, y, M:, :] = rows
                if s == 0:
                    blocks[w, tp, y, :M, :] = mem_ref[...]
            for w in range(WAVES):
                for n in range(7):
                    (first_copy if s == 0 else token_copy)(n, w).start()

    each(urgent, lambda group: group.relay(2))

    @pl.when(sec == 2)
    def _():
        group = Weights(2)
        for step in range(3):
            group.relay(step)
        let_go()

    @pl.when(odd)
    def _():
        pl.semaphore_wait(go_sem, 1)

    def late(group):
        group.start_z()
        for step in range(3):
            group.relay(step)

    each(odd, late)
    each(sec >= 0, lambda group: group.relay(3))
    each(sec >= 0, Weights.finish)
    wo_copy.wait()
    for n in range(3):
        len_copy(n).wait_send()
        len_copy(n, arrival=True).wait_recv()

    near = sec % 2 == 0

    def members(size):
        return ring if size == 4 else ring[:2]

    def b_copy(t, n, size):
        to_tp = tp if n < size else 1 - tp
        other = members(size)[n % size]
        return remote(
            result.at[t],
            blocks.at[t, tp, y],
            x_send.at[t, n],
            x_recv.at[t, slot],
            where((sec + 1) % NSEC, to_tp, z * NY + other),
        )

    def h_copy(t, n):
        return remote(
            result.at[t],
            blocks.at[t, tp, y],
            x_send.at[t, n],
            x_recv.at[t, slot],
            where((sec + 1) % NSEC, 1 - tp, z * NY + ring[n]),
        )

    def m_copy(t, n):
        return remote(
            result.at[t, pl.ds(0, M)],
            blocks.at[t + WAVES, tp, y, pl.ds(0, M)],
            x_send.at[t, n],
            x_recv.at[t + WAVES, slot],
            where(0, 1 - tp, z * NY + ring[n]),
        )

    def forward(t, n, rows):
        ref = blocks.at[t, 1 - tp, ring[n], rows]
        return remote(
            ref, ref, r_send.at[t, n], x_recv.at[t, (1 - tp) * NY + ring[n]], where(sec, 1 - tp, doc)
        )

    def arrival(t, half, other, rows, tokens=False):
        ref = blocks.at[t, half, other, rows]
        source = half * NY + other
        sem = tok_recv.at[t - WAVES, source] if tokens else x_recv.at[t, source]
        return remote(ref, ref, x_send.at[0, 0], sem, at_y(y_mate))

    def head_cols(size, t, other):
        per = heads_cols // size
        start = t * heads_cols + Weights(size).kind(other) * per
        return pl.ds(pl.multiple_of(start, per), per)

    def a_peers(size):
        return [(t, other) for t in (tp, 1 - tp) for other in members(size)][1:]

    def mixed_rows(size, t, other):
        return mixed4.at[t, other] if size == 4 else mixed2.at[t, other % 2]

    def a_copy(t, n, size):
        to_tp, other = a_peers(size)[n]
        return remote(
            mixed_rows(size, t, other),
            heads.at[t, :, head_cols(size, tp, y)],
            a_send.at[t, n],
            a_recv.at[t, slot],
            where(sec, to_tp, z * NY + other),
        )

    def a_arrival(t, n, size):
        from_tp, other = a_peers(size)[n]
        return remote(
            mixed_rows(size, t, other),
            heads.at[t, :, head_cols(size, from_tp, other)],
            a_send.at[t, n],
            a_recv.at[t, from_tp * NY + other],
            at_y(y_mate),
        )

    def pool_copy(w):
        index = jnp.minimum(sec, NSEC - 2)
        return remote(
            pool.at[w], pool_in.at[index, w], pool_send.at[w], pool_recv.at[index, w], where(NSEC - 1, tp, doc)
        )

    def total_copy(w, to):
        return remote(
            total.at[w], cast, total_send.at[w, to // 2], total_recv, where(to, tp, doc)
        )

    all_rows = pl.ds(0, ROWS)
    scale = 1.0 / math.sqrt(HD)

    def attend(t, size):
        s = t // WAVES
        per = heads_cols // size
        docs = members(size)
        n_rows = size * ROWS
        group = Weights(size)
        far = near & ((sec > 0) | (s == 1))
        first = jnp.where(far, 1 - tp, tp)

        def wait_half(n):
            half = first if n == 0 else 1 - first

            @pl.when(odd)
            def _():
                for other in docs:
                    arrival(t, half, other, all_rows).wait_recv()

            if size == 2:

                @pl.when(even)
                def _():
                    for k, other in enumerate(docs):
                        arrival(t, half, other, all_rows).wait_recv()
                        if n == 0:
                            forward(t, k, all_rows).start()

                return

            @pl.when(even & (s == 0))
            def _():
                for other in docs[1 - n :]:
                    arrival(t, half, other, all_rows).wait_recv()

            @pl.when(even & (s == 1))
            def _():
                for other in docs[n:]:
                    arrival(t, half, other, pl.ds(M, L), tokens=True).wait_recv()
                for k, other in enumerate(docs):
                    arrival(t, half, other, pl.ds(0, M)).wait_recv()
                    if n == 0:
                        forward(t, k, pl.ds(0, M)).start()

        step = 128
        total_sum = sum2 if size == 2 else sum4
        qkv = qkv2 if size == 2 else qkv4
        base = pl.multiple_of(y // 2 * 2, 2) if size == 2 else 0
        square = jnp.zeros((n_rows, step), jnp.float32)
        for n in range(2):
            half = first if n == 0 else 1 - first
            wait_half(n)
            for c in range(0, width, step):
                x = blocks[t, half, pl.ds(base, size), :, c : c + step]
                x = x.reshape(n_rows, step).astype(jnp.float32)
                square = square + x * x
                scaled[:n_rows, c : c + step] = (x * gain_ref[half, :, c : c + step]).astype(
                    jnp.bfloat16
                )
            if n == 1:
                mean_square = jnp.sum(square, -1, keepdims=True) * (1.0 / (2 * width))
                inverse = lax.rsqrt(mean_square + EPSILON)
            rows = pl.ds(pl.multiple_of(half * width, width), width)

            for j in range(3):
                cols = slice(j * per, (j + 1) * per)
                out = jnp.dot(
                    scaled[:n_rows, :], group.ref[rows, cols], preferred_element_type=jnp.float32
                )
                if n == 0:
                    total_sum[j] = out
                else:
                    qkv[j] = ((total_sum[j] + out) * inverse).astype(jnp.bfloat16)

        shape = (2 * ROWS, 2 * ROWS)
        row = lax.broadcasted_iota(jnp.int32, shape, 0)
        col = lax.broadcasted_iota(jnp.int32, shape, 1)
        row_doc = (row >= ROWS).astype(jnp.int32)
        col_doc = (col >= ROWS).astype(jnp.int32)
        i = row - ROWS * row_doc
        j = col - ROWS * col_doc
        ordered = (row_doc == col_doc) & ((j < M) | (i < M) | (j <= i))
        for p in range(size // 2):
            d = base + 2 * p
            lengths = (lens[d, pl.ds(t, 1), :] + lens[d + 1, pl.ds(t, 1), :])[:, : 2 * ROWS]
            allowed = ordered & ((j < M) | (j - M < lengths))
            own = slice(p * 2 * ROWS, (p + 1) * 2 * ROWS)
            for h in range(per // HD):
                cols = slice(h * HD, (h + 1) * HD)
                scores = (
                    lax.dot_general(
                        qkv[0, own, cols],
                        qkv[1, own, cols],
                        (((1,), (1,)), ((), ())),
                        preferred_element_type=jnp.float32,
                    )
                    * scale
                )
                scores = jnp.where(allowed, scores, NEGATIVE)
                exps = jnp.where(allowed, jnp.exp(scores), 0.0)
                probs = (exps / jnp.sum(exps, -1, keepdims=True)).astype(jnp.bfloat16)
                out = jnp.dot(probs, qkv[2, own, cols], preferred_element_type=jnp.float32)
                out = out.astype(jnp.bfloat16).reshape(2, ROWS, HD)
                if size == 4:
                    mixed4[t, 2 * p : 2 * p + 2, :, cols] = out
                else:
                    mixed2[t, :, :, cols] = out

        count = 2 * size - 1
        for n in range(count):
            a_copy(t, n, size).start()
        heads[t, :, head_cols(size, tp, y)] = mixed4[t, y] if size == 4 else mixed2[t, bit]
        for n in range(count):
            a_arrival(t, n, size).wait_recv()

    def task(t, carry):
        s = t // WAVES
        w = t % WAVES

        @pl.when(wide)
        def _():
            attend(t, 4)

        @pl.when(sec >= 1)
        def _():
            attend(t, 2)

        length = len_ref[w, s]
        position = lax.broadcasted_iota(jnp.int32, (ROWS, 1), 0)
        token_ok = (position >= M) & (position - M < length)
        factor = mix_ref[0] / length.astype(jnp.float32)

        for j in range(width // 512):
            cols = slice(j * 512, (j + 1) * 512)
            update = jnp.dot(heads[t], w_out[:, cols], preferred_element_type=jnp.float32)
            out = (blocks[t, tp, y, :, cols].astype(jnp.float32) + update).astype(jnp.bfloat16)
            result[t, :, cols] = out
            summed = jnp.sum(jnp.where(token_ok, out.astype(jnp.float32), 0.0), 0, keepdims=True)
            pool_row[:, cols] = summed * factor

        @pl.when(near)
        def _():
            for n in range(4):
                b_copy(t, n, 2).start()

        @pl.when(sec == 1)
        def _():
            for n in range(2):
                h_copy(t, n).start()

        @pl.when((sec == NSEC - 1) & (s == 0))
        def _():
            for n in range(4):
                m_copy(t, n).start()

        @pl.when(s == 1)
        def _():
            for k in range(width // 128):
                pool[w, k : k + 1, :] = pool_row[:, k * 128 : (k + 1) * 128]

            @pl.when(sec < NSEC - 1)
            def _():
                pool_copy(w).start()

            @pl.when(sec == NSEC - 1)
            def _():
                for index in range(NSEC - 1):
                    remote(
                        pool.at[w],
                        pool_in.at[index, w],
                        pool_send.at[w],
                        pool_recv.at[index, w],
                        where(0, tp, doc),
                    ).wait_recv()
                summed = pool[w] + pool_in[0, w] + pool_in[1, w] + pool_in[2, w]
                total[w] = summed

                @pl.when(w == 0)
                def _():
                    total_copy(0, 0).start()
                    total_copy(0, 2).start()

                @pl.when(w == 1)
                def _():
                    total_copy(1, 1).start()
                    cast[...] = summed

        return carry

    lax.fori_loop(0, SEGS * WAVES, task, 0)

    core = sec % 2
    base = sec - core
    n_docs = NY * NZ

    @pl.when(sec < NSEC - 1)
    def _():
        remote(
            total.at[0], cast, total_send.at[0, 0], total_recv, where(NSEC - 1, tp, doc)
        ).wait_recv()

    def cast_copy(k, which):
        to = base + core if which == 0 else base + 1 - core
        return remote(
            cast,
            out_ref.at[2 * doc + core],
            cast_send.at[which, k],
            cast_recv.at[core, doc],
            where(to, tp, (doc + k) % n_docs),
        )

    cast_copy(0, 1).start()

    def send_row(k, carry):
        cast_copy(k, 0).start()
        cast_copy(k, 1).start()
        return carry

    lax.fori_loop(1, n_docs, send_row, 0)
    out_ref[2 * doc + core] = cast[...]

    def row_arrival(c, d):
        return remote(
            cast, out_ref.at[2 * d + c], cast_send.at[0, 0], cast_recv.at[c, d], where(base + 1 - core, tp, doc)
        )

    row_arrival(1 - core, doc).wait_recv()

    def take_row(k, carry):
        d = (doc + k) % n_docs
        row_arrival(core, d).wait_recv()
        row_arrival(1 - core, d).wait_recv()
        return carry

    lax.fori_loop(1, n_docs, take_row, 0)

    cast_copy(0, 1).wait_send()

    def sent_row(k, carry):
        cast_copy(k, 0).wait_send()
        cast_copy(k, 1).wait_send()
        return carry

    lax.fori_loop(1, n_docs, sent_row, 0)

    @pl.when(sec > 0)
    def _():
        for s in range(SEGS):
            part_copy(s).wait_send()

    @pl.when(sec == 0)
    def _():
        for w in range(WAVES):
            for n in range(7):
                first_copy(n, w).wait_send()
                token_copy(n, w).wait_send()

    def sent_task(t, carry):
        @pl.when(wide)
        def _():
            for n in range(7):
                a_copy(t, n, 4).wait_send()

        @pl.when(sec >= 1)
        def _():
            for n in range(3):
                a_copy(t, n, 2).wait_send()

        @pl.when(near)
        def _():
            for n in range(4):
                b_copy(t, n, 2).wait_send()

        @pl.when(sec == 1)
        def _():
            for n in range(2):
                h_copy(t, n).wait_send()

        @pl.when((sec == NSEC - 1) & (t < WAVES))
        def _():
            for n in range(4):
                m_copy(t, n).wait_send()

        @pl.when(sec == 2)
        def _():
            for n in range(2):
                forward(t, n, all_rows).wait_send()

        @pl.when((sec == 0) & (t >= WAVES))
        def _():
            for n in range(4):
                forward(t, n, pl.ds(0, M)).wait_send()

        return carry

    lax.fori_loop(0, SEGS * WAVES, sent_task, 0)

    @pl.when(sec < NSEC - 1)
    def _():
        for w in range(WAVES):
            pool_copy(w).wait_send()

    @pl.when(sec == NSEC - 1)
    def _():
        total_copy(0, 0).wait_send()
        total_copy(0, 2).wait_send()
        total_copy(1, 1).wait_send()


def body(
    token_ids,
    seg_lengths,
    emb_table,
    mem_init,
    norm_gain,
    w_query,
    w_key,
    w_value,
    w_out,
    layer_mix,
):
    doc_local = token_ids.shape[0]
    vocab_rows, width = emb_table.shape
    depth, head_cols = w_query.shape[1:]
    half, quarter = head_cols // 2, head_cols // 4
    n_tasks = SEGS * WAVES
    dma = pltpu.SemaphoreType.DMA
    bf16, f32 = jnp.bfloat16, jnp.float32
    any_space = pl.BlockSpec(memory_space=pl.ANY)
    vmem = pl.BlockSpec(memory_space=pltpu.VMEM)
    lanes = width // 128
    rows = pl.pallas_call(
        kernel,
        out_shape=jax.ShapeDtypeStruct((NY * NZ * WAVES, lanes, 128), f32),
        in_specs=[any_space] * 10,
        out_specs=vmem,
        scratch_shapes=[
            pltpu.VMEM((WAVES, SEGS, L), jnp.int32),
            pltpu.VMEM((vocab_rows, width), bf16),
            pltpu.VMEM((n_tasks * L, vocab_rows), bf16),
            pltpu.VMEM((M, width), bf16),
            pltpu.VMEM((2, 1, width), f32),
            pltpu.SMEM((doc_local, SEGS), jnp.int32),
            pltpu.SMEM((1,), f32),
            pltpu.VMEM((2 * width, 3 * half), bf16),
            pltpu.VMEM((2 * width, 3 * quarter), bf16),
            pltpu.VMEM((2 * head_cols, width), bf16),
            pltpu.VMEM((n_tasks, 2, NY, ROWS, width), bf16),
            pltpu.VMEM((4 * ROWS, width), bf16),
            pltpu.VMEM((3, 2 * ROWS, half), f32),
            pltpu.VMEM((3, 4 * ROWS, quarter), f32),
            pltpu.VMEM((3, 2 * ROWS, half), bf16),
            pltpu.VMEM((3, 4 * ROWS, quarter), bf16),
            pltpu.VMEM((n_tasks, 2, ROWS, half), bf16),
            pltpu.VMEM((n_tasks, 4, ROWS, quarter), bf16),
            pltpu.VMEM((n_tasks, ROWS, 2 * head_cols), bf16),
            pltpu.VMEM((n_tasks, ROWS, width), bf16),
            pltpu.VMEM((NSEC, SEGS, WAVES, L, width), bf16),
            pltpu.VMEM((NY, 8, 128), jnp.int32),
            pltpu.VMEM((1, width), f32),
            pltpu.VMEM((WAVES, lanes, 128), f32),
            pltpu.VMEM((NSEC - 1, WAVES, lanes, 128), f32),
            pltpu.VMEM((WAVES, lanes, 128), f32),
            pltpu.VMEM((lanes, 128), f32),
            dma((11,)),
            dma((3, 3)),
            dma((3, 3)),
            dma((2, 4, 2)),
            dma((2, 4, 2)),
            dma((8, 2)),
            dma((8, 2)),
            dma((3,)),
            dma((3,)),
            dma((SEGS,)),
            dma((NSEC - 1, SEGS)),
            dma((SEGS, WAVES, 7)),
            dma((WAVES, 8)),
            dma((n_tasks, 8)),
            dma((n_tasks, 8)),
            dma((n_tasks, 4)),
            dma((n_tasks, 7)),
            dma((n_tasks, 8)),
            dma((WAVES,)),
            dma((NSEC - 1, WAVES)),
            dma((WAVES, 2)),
            dma,
            dma((2, NY * NZ)),
            dma((2, NY * NZ)),
            pltpu.SemaphoreType.REGULAR,
        ],
        compiler_params=pltpu.CompilerParams(
            has_side_effects=True, collective_id=0, vmem_limit_bytes=67000000
        ),
    )(
        token_ids,
        emb_table,
        mem_init,
        norm_gain,
        seg_lengths,
        layer_mix,
        w_query[0],
        w_key[0],
        w_value[0],
        w_out[0],
    )
    return rows.reshape(NY * NZ * WAVES, width)


def solution(mesh):
    return jax.shard_map(
        body,
        mesh=mesh,
        in_specs=(
            P("doc", None, None),
            P("doc", None),
            P("section", "tp"),
            P(None, "tp"),
            P("section", None),
            P("section", "doc", "tp"),
            P("section", "doc", "tp"),
            P("section", "doc", "tp"),
            P("section", None, "tp"),
            P("section"),
        ),
        out_specs=P(None, "tp"),
        check_vma=False,
    )
```

```python
import math

import jax
import jax.numpy as jnp
from jax import lax
from jax.experimental import pallas as pl
from jax.experimental.pallas import tpu as pltpu
from jax.sharding import PartitionSpec as P

HD = 128
M = 16
L = 32
SEGS = 2
ROWS = M + L
EPSILON = 1e-05
NEGATIVE = -1e30

NY = 4
NZ = 8
KEEP_EARLY = 96
KEEP_LATE = 80
WAVES = 2
NSEC = 4


def kernel(
    ids_hbm,
    table_hbm,
    mem_hbm,
    gain_hbm,
    len_hbm,
    mix_hbm,
    wq_ref,
    wk_ref,
    wv_ref,
    wo_ref,
    out_ref,
    ids_ref,
    table,
    picks,
    mem_ref,
    gain_ref,
    len_ref,
    mix_ref,
    weights2,
    weights4,
    w_out,
    blocks,
    scaled,
    sum2,
    sum4,
    qkv2,
    qkv4,
    mixed2,
    mixed4,
    heads,
    update,
    result,
    parts,
    lens,
    pool_row,
    pool,
    pool_in,
    total,
    cast,
    local_sem,
    y_send,
    y_recv,
    z_send,
    z_recv,
    f_send,
    f_recv,
    len_send,
    len_recv,
    part_send,
    part_recv,
    first_send,
    tok_send,
    tok_recv,
    x_send,
    x_recv,
    r_send,
    a_send,
    a_recv,
    pool_send,
    pool_recv,
    total_send,
    total_recv,
    cast_send,
    cast_recv,
    go_sem,
):
    sec = lax.axis_index("section")
    tp = lax.axis_index("tp")
    doc = lax.axis_index("doc")
    z = doc // NY
    y = doc % NY
    bit = y % 2
    y_mate = y + 1 - 2 * bit
    y_twin = NY - 1 - y
    y_far = NY - 1 - y_mate
    kind = ((y + 1) // 2) % 2
    width = blocks.shape[-1]
    depth = wq_ref.shape[0]
    slab = NY * depth
    pair = 2 * depth
    heads_cols = wq_ref.shape[1]

    def where(section, t, d):
        return {"section": section, "tp": t, "doc": d}

    def remote(src, dst, send, recv, to):
        return pltpu.make_async_remote_copy(
            src_ref=src,
            dst_ref=dst,
            send_sem=send,
            recv_sem=recv,
            device_id=to,
            device_id_type=pl.DeviceIdType.MESH,
        )

    def at_y(other):
        return where(sec, tp, z * NY + other)

    wide = sec == 0
    ring = [y, y_mate, y_twin, y_far]
    sources = (wq_ref, wk_ref, wv_ref)
    own_row = pl.multiple_of(doc * depth, depth)

    class Weights:
        def __init__(self, size, keep=KEEP_LATE):
            self.size = size
            self.keep = keep
            self.both = depth - keep
            self.per = heads_cols // size
            self.ref = weights4 if size == 4 else weights2

        def kind(self, other):
            return other if self.size == 4 else ((other + 1) // 2) % 2

        def column(self, other):
            return pl.ds(pl.multiple_of(self.kind(other) * self.per, self.per), self.per)

        def own_copies(self):
            return [
                pltpu.make_async_copy(
                    ref.at[:, self.column(y)],
                    self.ref.at[pl.ds(own_row, depth), pl.ds(j * self.per, self.per)],
                    local_sem.at[j],
                )
                for j, ref in enumerate(sources)
            ]

        def y_copies(self):
            out = []
            for n, other in enumerate(ring[1:]):
                for j, ref in enumerate(sources):
                    first, rows = 0, depth
                    if self.size == 2 and n > 0:
                        first, rows = pl.multiple_of((1 - bit) * self.keep, 16), self.both
                    src = ref.at[pl.ds(first, rows), self.column(other)]
                    dst = self.ref.at[
                        pl.ds(pl.multiple_of(own_row + first, 16), rows),
                        pl.ds(j * self.per, self.per),
                    ]
                    out.append(remote(src, dst, y_send.at[n, j], y_recv.at[n, j], at_y(other)))
            return out

        def rows(self, zz, part):
            if self.size == 4:
                return pl.ds(pl.multiple_of(zz * slab + part * pair, pair), pair)
            if part == 0:
                return pl.ds(pl.multiple_of(zz * slab + (y // 2) * pair, pair), pair)
            return pl.ds(pl.multiple_of(zz * slab + (1 - y // 2) * pair + self.keep, 16), 2 * self.both)

        def z_copy(self, way, step, part, arrival=False):
            ahead = step + 1 if arrival else step
            zz = (z + NZ - ahead) % NZ if way == 0 else (z + ahead) % NZ
            ref = self.ref.at[self.rows(zz, part)]
            to = (z + 1) % NZ if way == 0 else (z + NZ - 1) % NZ
            return remote(
                ref,
                ref,
                z_send.at[way, step, part],
                z_recv.at[way, step, part],
                where(sec, tp, to * NY + y),
            )

        def f_copies(self, slot, zz):
            if self.size == 4:
                return []
            base = zz * slab + (y // 2) * pair
            out = []
            for h, start in enumerate((base, base + pair - self.keep)):
                ref = self.ref.at[pl.ds(pl.multiple_of(start, 16), self.keep)]
                out.append(
                    remote(ref, ref, f_send.at[slot, h], f_recv.at[slot, h], at_y(y_twin))
                )
            return out

        def start_y(self):
            for copy in self.y_copies():
                copy.start()

        def start_z(self):
            for copy in self.own_copies():
                copy.wait()
            for copy in self.y_copies():
                copy.wait_recv()
            for part in range(2):
                for way in range(2):
                    self.z_copy(way, 0, part).start()
            for copy in self.f_copies(0, z):
                copy.start()

        def relay(self, step):
            for part in range(2):
                for way in range(2):
                    if z_sent(way, step, part):
                        self.z_copy(way, step, part, arrival=True).wait_recv()
                        if z_sent(way, step + 1, part):
                            self.z_copy(way, step + 1, part).start()
                        if part == 0:
                            ahead = step + 1
                            zz = (z + NZ - ahead) % NZ if way == 0 else (z + ahead) % NZ
                            for copy in self.f_copies(1 + step + 4 * way, zz):
                                copy.start()

        def finish(self):
            for step in range(4):
                for part in range(2):
                    for way in range(2):
                        if z_sent(way, step, part):
                            self.z_copy(way, step, part).wait_send()
            for k in range(8):
                for copy in self.f_copies(k, z):
                    copy.wait()
            for copy in self.y_copies():
                copy.wait_send()

    def z_sent(way, step, part):
        return step < 3 or (step == 3 and part == way)

    def each(condition, action):
        @pl.when(condition & wide)
        def _():
            action(Weights(4))

        @pl.when(condition & (sec == 1))
        def _():
            action(Weights(2, KEEP_EARLY))

        @pl.when(condition & (sec >= 2))
        def _():
            action(Weights(2))

    slot = tp * NY + y
    peers = [(t, other) for t in (tp, 1 - tp) for other in ring][1:]

    part_width = width // 2

    def part_cols(c):
        return pl.ds(c * part_width, part_width)

    def first_copy(n, w, c):
        t, other = peers[n]
        ref = blocks.at[w, tp, y, :, part_cols(c)]
        return remote(
            ref, ref, first_send.at[w, n, c], x_recv.at[w, slot, c], where(sec, t, z * NY + other)
        )

    def token_copy(n, w):
        t, other = peers[n]
        ref = blocks.at[WAVES + w, tp, y, pl.ds(M, L)]
        return remote(
            ref, ref, tok_send.at[w, n], tok_recv.at[w, slot], where(sec, t, z * NY + other)
        )

    def part_copy(s):
        index = jnp.maximum(sec - 1, 0)
        return remote(
            parts.at[NSEC - 1, s], parts.at[index, s], part_send.at[s], part_recv.at[index, s], where(0, tp, doc)
        )

    def len_copy(n, arrival=False):
        index = ring[n + 1] if arrival else y
        ref = lens.at[index]
        return remote(ref, ref, len_send.at[n], len_recv.at[n], at_y(ring[n + 1]))


    small_copies = [
        pltpu.make_async_copy(len_hbm, len_ref, local_sem.at[4]),
        pltpu.make_async_copy(mix_hbm, mix_ref, local_sem.at[5]),
        pltpu.make_async_copy(ids_hbm, ids_ref, local_sem.at[6]),
        pltpu.make_async_copy(mem_hbm, mem_ref, local_sem.at[7]),
        pltpu.make_async_copy(gain_hbm.at[:, pl.ds(0, width)], gain_ref.at[0], local_sem.at[8]),
        pltpu.make_async_copy(gain_hbm.at[:, pl.ds(width, width)], gain_ref.at[1], local_sem.at[9]),
    ]
    table_copy = pltpu.make_async_copy(table_hbm, table, local_sem.at[10])
    wo_copy = pltpu.make_async_copy(wo_ref, w_out, local_sem.at[3])
    for copy in small_copies:
        copy.start()
    for group in (Weights(4), Weights(2)):

        @pl.when(wide if group.size == 4 else sec >= 1)
        def _():
            for copy in group.own_copies():
                copy.start()


    next_sec = (sec + 1) % NSEC
    last_sec = (sec + NSEC - 1) % NSEC
    greeted = [where(sec, t, z * NY + other) for t, other in peers]
    greeted += [where(sec, tp, (z + step) % NZ * NY + y) for step in (1, NZ - 1)]
    greeted += [
        where(to, t, z * NY + other)
        for to in (next_sec, last_sec)
        for t in (tp, 1 - tp)
        for other in ring
    ]
    greeted += [where((sec + 2) % NSEC, tp, doc)]
    barrier = pltpu.get_barrier_semaphore()
    for to in greeted:
        pl.semaphore_signal(barrier, inc=1, device_id=to, device_id_type=pl.DeviceIdType.MESH)
    pl.semaphore_wait(barrier, len(greeted))

    each(sec >= 0, Weights.start_y)
    table_copy.start()
    wo_copy.start()
    for copy in small_copies:
        copy.wait()

    lane = lax.broadcasted_iota(jnp.int32, (1, 128), 1)
    mine = (lane >= bit * ROWS) & (lane < bit * ROWS + ROWS)
    for t in range(SEGS * WAVES):
        lens[y, t : t + 1, :] = jnp.where(mine, len_ref[t % WAVES, t // WAVES], 0)
    for t in range(SEGS * WAVES, 8):
        lens[y, t : t + 1, :] = jnp.zeros((1, 128), jnp.int32)
    for n in range(3):
        len_copy(n).start()

    even = sec % 2 == 0
    odd = sec % 2 == 1
    urgent = sec < 2
    each(sec <= 2, Weights.start_z)

    n_ids = SEGS * WAVES * L
    eye = lax.broadcasted_iota(jnp.int32, (L, L), 0) == lax.broadcasted_iota(jnp.int32, (L, L), 1)
    columns = [
        jnp.sum(
            jnp.where(eye, ids_ref[w, s : s + 1, :].astype(jnp.float32), 0.0), -1, keepdims=True
        )
        for s in range(SEGS)
        for w in range(WAVES)
    ]
    wanted = jnp.concatenate(columns, axis=0).astype(jnp.int32) - sec * table.shape[0]
    for k in range(0, table.shape[0], 512):
        place = lax.broadcasted_iota(jnp.int32, (n_ids, 512), 1) + k
        picks[:, k : k + 512] = jnp.where(place == wanted, 1.0, 0.0).astype(jnp.bfloat16)
    def let_go():
        pl.semaphore_signal(
            go_sem, inc=1, device_id=where(sec + 1, tp, doc), device_id_type=pl.DeviceIdType.MESH
        )

    each(urgent, lambda group: group.relay(0))
    table_copy.wait()

    def pick(j, carry):
        cols = pl.ds(pl.multiple_of(j * 512, 512), 512)
        rows = jnp.dot(picks[...], table[:, cols], preferred_element_type=jnp.float32)
        parts[NSEC - 1, :, :, :, cols] = rows.astype(jnp.bfloat16).reshape(SEGS, WAVES, L, 512)
        return carry

    lax.fori_loop(0, width // 1024, pick, 0)
    each(urgent, lambda group: group.relay(1))
    lax.fori_loop(width // 1024, width // 512, pick, 0)

    @pl.when(sec > 0)
    def _():
        for s in range(SEGS):
            part_copy(s).start()

    @pl.when(sec == 0)
    def _():
        for s in range(SEGS):
            for index in range(NSEC - 1):
                remote(
                    parts.at[NSEC - 1, s],
                    parts.at[index, s],
                    part_send.at[s],
                    part_recv.at[index, s],
                    where(1, tp, doc),
                ).wait_recv()
            for w in range(WAVES):
                rows = parts[0, s, w] + parts[1, s, w] + parts[2, s, w] + parts[3, s, w]
                blocks[s * WAVES + w, tp, y, M:, :] = rows
                if s == 0:
                    blocks[w, tp, y, :M, :] = mem_ref[...]
            for w in range(WAVES):
                for n in range(7):
                    if s == 0:
                        first_copy(n, w, 0).start()
                        first_copy(n, w, 1).start()
                    else:
                        token_copy(n, w).start()

    @pl.when(sec == 0)
    def _():
        Weights(4).relay(2)

    @pl.when(sec == 2)
    def _():
        group = Weights(2)
        for step in range(3):
            group.relay(step)
        let_go()

    @pl.when(sec == 1)
    def _():
        Weights(2, KEEP_EARLY).relay(2)

    @pl.when(sec == 3)
    def _():
        pl.semaphore_wait(go_sem, 1)
        group = Weights(2)
        group.start_z()
        for step in range(3):
            group.relay(step)

    each(sec >= 0, lambda group: group.relay(3))
    each(sec >= 0, Weights.finish)
    wo_copy.wait()
    for n in range(3):
        len_copy(n).wait_send()
        len_copy(n, arrival=True).wait_recv()

    near = sec % 2 == 0

    def members(size):
        return ring if size == 4 else ring[:2]

    def b_copy(t, n, c):
        to_tp = tp if n < 2 else 1 - tp
        return remote(
            result.at[t, :, part_cols(c)],
            blocks.at[t, tp, y, :, part_cols(c)],
            x_send.at[t, n, c],
            x_recv.at[t, slot, c],
            where((sec + 1) % NSEC, to_tp, z * NY + ring[n % 2]),
        )

    def h_copy(t, n, c):
        return remote(
            result.at[t, :, part_cols(c)],
            blocks.at[t, tp, y, :, part_cols(c)],
            x_send.at[t, n, c],
            x_recv.at[t, slot, c],
            where((sec + 1) % NSEC, 1 - tp, z * NY + ring[n]),
        )

    def m_copy(t, n, c):
        return remote(
            result.at[t, pl.ds(0, M), part_cols(c)],
            blocks.at[t + WAVES, tp, y, pl.ds(0, M), part_cols(c)],
            x_send.at[t, n, c],
            x_recv.at[t + WAVES, slot, c],
            where(0, 1 - tp, z * NY + ring[n]),
        )

    def forward(t, n, rows, c):
        ref = blocks.at[t, 1 - tp, ring[n], rows, part_cols(c)]
        return remote(
            ref,
            ref,
            r_send.at[t, n, c],
            x_recv.at[t, (1 - tp) * NY + ring[n], c],
            where(sec, 1 - tp, doc),
        )

    def arrival(t, half, other, rows, c):
        ref = blocks.at[t, half, other, rows, part_cols(c)]
        sem = x_recv.at[t, half * NY + other, c]
        return remote(ref, ref, x_send.at[0, 0, 0], sem, at_y(y_mate))

    def token_arrival(t, half, other):
        ref = blocks.at[t, half, other, pl.ds(M, L)]
        sem = tok_recv.at[t - WAVES, half * NY + other]
        return remote(ref, ref, x_send.at[0, 0, 0], sem, at_y(y_mate))

    def head_cols(size, t, other):
        per = heads_cols // size
        start = t * heads_cols + Weights(size).kind(other) * per
        return pl.ds(pl.multiple_of(start, per), per)

    def a_peers(size):
        return [(t, other) for t in (tp, 1 - tp) for other in members(size)][1:]

    def mixed_rows(size, t, other):
        return mixed4.at[t, other] if size == 4 else mixed2.at[t, other % 2]

    def a_copy(t, n, size):
        to_tp, other = a_peers(size)[n]
        return remote(
            mixed_rows(size, t, other),
            heads.at[t, :, head_cols(size, tp, y)],
            a_send.at[t, n],
            a_recv.at[t, slot],
            where(sec, to_tp, z * NY + other),
        )

    def a_arrival(t, n, size):
        from_tp, other = a_peers(size)[n]
        return remote(
            mixed_rows(size, t, other),
            heads.at[t, :, head_cols(size, from_tp, other)],
            a_send.at[t, n],
            a_recv.at[t, from_tp * NY + other],
            at_y(y_mate),
        )

    def pool_copy(w):
        index = jnp.minimum(sec, NSEC - 2)
        return remote(
            pool.at[w], pool_in.at[index, w], pool_send.at[w], pool_recv.at[index, w], where(NSEC - 1, tp, doc)
        )

    def total_copy(w, to):
        return remote(
            total.at[w], cast, total_send.at[w, to // 2], total_recv, where(to, tp, doc)
        )

    all_rows = pl.ds(0, ROWS)
    scale = 1.0 / math.sqrt(HD)

    def attend(t, size):
        s = t // WAVES
        per = heads_cols // size
        docs = members(size)
        n_rows = size * ROWS
        group = Weights(size)
        far = near & ((sec > 0) | (s == 1))
        first = jnp.where(far, 1 - tp, tp)

        def wait_half(n):
            half = first if n == 0 else 1 - first

            def take(others, rows, onward):
                for c in range(2):
                    for k, other in enumerate(others):
                        arrival(t, half, other, rows, c).wait_recv()
                        if onward:
                            forward(t, k, rows, c).start()

            @pl.when(odd)
            def _():
                take(docs, all_rows, False)

            if size == 2:

                @pl.when(even)
                def _():
                    take(docs, all_rows, n == 0)

                return

            @pl.when(even & (s == 0))
            def _():
                take(docs[1 - n :], all_rows, False)

            @pl.when(even & (s == 1))
            def _():
                for other in docs[n:]:
                    token_arrival(t, half, other).wait_recv()
                take(docs, pl.ds(0, M), n == 0)

        step = 128
        total_sum = sum2 if size == 2 else sum4
        qkv = qkv2 if size == 2 else qkv4
        base = pl.multiple_of(y // 2 * 2, 2) if size == 2 else 0
        square = jnp.zeros((n_rows, step), jnp.float32)
        for n in range(2):
            half = first if n == 0 else 1 - first
            wait_half(n)
            for c in range(0, width, step):
                x = blocks[t, half, pl.ds(base, size), :, c : c + step]
                x = x.reshape(n_rows, step).astype(jnp.float32)
                square = square + x * x
                scaled[:n_rows, c : c + step] = (x * gain_ref[half, :, c : c + step]).astype(
                    jnp.bfloat16
                )
            if n == 1:
                mean_square = jnp.sum(square, -1, keepdims=True) * (1.0 / (2 * width))
                inverse = lax.rsqrt(mean_square + EPSILON)
            rows = pl.ds(pl.multiple_of(half * width, width), width)

            for j in range(3):
                cols = slice(j * per, (j + 1) * per)
                out = jnp.dot(
                    scaled[:n_rows, :], group.ref[rows, cols], preferred_element_type=jnp.float32
                )
                if n == 0:
                    total_sum[j] = out
                else:
                    qkv[j] = ((total_sum[j] + out) * inverse).astype(jnp.bfloat16)

        shape = (2 * ROWS, 2 * ROWS)
        row = lax.broadcasted_iota(jnp.int32, shape, 0)
        col = lax.broadcasted_iota(jnp.int32, shape, 1)
        row_doc = (row >= ROWS).astype(jnp.int32)
        col_doc = (col >= ROWS).astype(jnp.int32)
        i = row - ROWS * row_doc
        j = col - ROWS * col_doc
        ordered = (row_doc == col_doc) & ((j < M) | (i < M) | (j <= i))
        for p in range(size // 2):
            d = base + 2 * p
            lengths = (lens[d, pl.ds(t, 1), :] + lens[d + 1, pl.ds(t, 1), :])[:, : 2 * ROWS]
            allowed = ordered & ((j < M) | (j - M < lengths))
            own = slice(p * 2 * ROWS, (p + 1) * 2 * ROWS)
            for h in range(per // HD):
                cols = slice(h * HD, (h + 1) * HD)
                scores = (
                    lax.dot_general(
                        qkv[0, own, cols],
                        qkv[1, own, cols],
                        (((1,), (1,)), ((), ())),
                        preferred_element_type=jnp.float32,
                    )
                    * scale
                )
                scores = jnp.where(allowed, scores, NEGATIVE)
                exps = jnp.where(allowed, jnp.exp(scores), 0.0)
                probs = (exps / jnp.sum(exps, -1, keepdims=True)).astype(jnp.bfloat16)
                out = jnp.dot(probs, qkv[2, own, cols], preferred_element_type=jnp.float32)
                out = out.astype(jnp.bfloat16).reshape(2, ROWS, HD)
                if size == 4:
                    mixed4[t, 2 * p : 2 * p + 2, :, cols] = out
                else:
                    mixed2[t, :, :, cols] = out

        count = 2 * size - 1
        for n in range(count):
            a_copy(t, n, size).start()
        heads[t, :, head_cols(size, tp, y)] = mixed4[t, y] if size == 4 else mixed2[t, bit]
        update[...] = jnp.zeros_like(update)
        where_from = [(tp, y)] + a_peers(size)
        for n in range(count):
            own = head_cols(size, *where_from[n])
            update[...] += jnp.dot(
                heads[t, :, own], w_out[own, :], preferred_element_type=jnp.float32
            )
            a_arrival(t, n, size).wait_recv()
        last = head_cols(size, *where_from[count])

        w = t % WAVES
        length = len_ref[w, s]
        position = lax.broadcasted_iota(jnp.int32, (ROWS, 1), 0)
        token_ok = (position >= M) & (position - M < length)
        factor = mix_ref[0] / length.astype(jnp.float32)

        for c in range(2):
            for k in range(0, part_width, 512):
                cols = slice(c * part_width + k, c * part_width + k + 512)
                out = update[:, cols] + jnp.dot(
                    heads[t, :, last], w_out[last, cols], preferred_element_type=jnp.float32
                )
                out = (blocks[t, tp, y, :, cols].astype(jnp.float32) + out).astype(jnp.bfloat16)
                result[t, :, cols] = out
                summed = jnp.where(token_ok, out.astype(jnp.float32), 0.0)
                pool_row[:, cols] = jnp.sum(summed, 0, keepdims=True) * factor

            @pl.when(near)
            def _():
                for n in range(4):
                    b_copy(t, n, c).start()

            if size == 2:

                @pl.when(sec == 1)
                def _():
                    for n in range(2):
                        h_copy(t, n, c).start()

                @pl.when((sec == NSEC - 1) & (s == 0))
                def _():
                    for n in range(4):
                        m_copy(t, n, c).start()

    def task(t, carry):
        s = t // WAVES
        w = t % WAVES

        @pl.when(wide)
        def _():
            attend(t, 4)

        @pl.when(sec >= 1)
        def _():
            attend(t, 2)

        @pl.when(s == 1)
        def _():
            for k in range(width // 128):
                pool[w, k : k + 1, :] = pool_row[:, k * 128 : (k + 1) * 128]

            @pl.when(sec < NSEC - 1)
            def _():
                pool_copy(w).start()

            @pl.when(sec == NSEC - 1)
            def _():
                for index in range(NSEC - 1):
                    remote(
                        pool.at[w],
                        pool_in.at[index, w],
                        pool_send.at[w],
                        pool_recv.at[index, w],
                        where(0, tp, doc),
                    ).wait_recv()
                summed = pool[w] + pool_in[0, w] + pool_in[1, w] + pool_in[2, w]
                total[w] = summed

                @pl.when(w == 0)
                def _():
                    total_copy(0, 0).start()
                    total_copy(0, 2).start()

                @pl.when(w == 1)
                def _():
                    total_copy(1, 1).start()
                    cast[...] = summed

        return carry

    lax.fori_loop(0, SEGS * WAVES, task, 0)

    core = sec % 2
    base = sec - core
    n_docs = NY * NZ

    @pl.when(sec < NSEC - 1)
    def _():
        remote(
            total.at[0], cast, total_send.at[0, 0], total_recv, where(NSEC - 1, tp, doc)
        ).wait_recv()

    def cast_copy(k, which):
        to = base + core if which == 0 else base + 1 - core
        return remote(
            cast,
            out_ref.at[2 * doc + core],
            cast_send.at[which, k],
            cast_recv.at[core, doc],
            where(to, tp, (doc + k) % n_docs),
        )

    cast_copy(0, 1).start()

    def send_row(k, carry):
        cast_copy(k, 0).start()
        cast_copy(k, 1).start()
        return carry

    lax.fori_loop(1, n_docs, send_row, 0)
    out_ref[2 * doc + core] = cast[...]

    def row_arrival(c, d):
        return remote(
            cast, out_ref.at[2 * d + c], cast_send.at[0, 0], cast_recv.at[c, d], where(base + 1 - core, tp, doc)
        )

    row_arrival(1 - core, doc).wait_recv()

    def take_row(k, carry):
        d = (doc + k) % n_docs
        row_arrival(core, d).wait_recv()
        row_arrival(1 - core, d).wait_recv()
        return carry

    lax.fori_loop(1, n_docs, take_row, 0)

    cast_copy(0, 1).wait_send()

    def sent_row(k, carry):
        cast_copy(k, 0).wait_send()
        cast_copy(k, 1).wait_send()
        return carry

    lax.fori_loop(1, n_docs, sent_row, 0)

    @pl.when(sec > 0)
    def _():
        for s in range(SEGS):
            part_copy(s).wait_send()

    @pl.when(sec == 0)
    def _():
        for w in range(WAVES):
            for n in range(7):
                first_copy(n, w, 0).wait_send()
                first_copy(n, w, 1).wait_send()
                token_copy(n, w).wait_send()

    def sent_task(t, carry):
        @pl.when(wide)
        def _():
            for n in range(7):
                a_copy(t, n, 4).wait_send()

        @pl.when(sec >= 1)
        def _():
            for n in range(3):
                a_copy(t, n, 2).wait_send()

        @pl.when(near)
        def _():
            for n in range(4):
                b_copy(t, n, 0).wait_send()
                b_copy(t, n, 1).wait_send()

        @pl.when(sec == 1)
        def _():
            for n in range(2):
                h_copy(t, n, 0).wait_send()
                h_copy(t, n, 1).wait_send()

        @pl.when((sec == NSEC - 1) & (t < WAVES))
        def _():
            for n in range(4):
                m_copy(t, n, 0).wait_send()
                m_copy(t, n, 1).wait_send()

        @pl.when(sec == 2)
        def _():
            for n in range(2):
                forward(t, n, all_rows, 0).wait_send()
                forward(t, n, all_rows, 1).wait_send()

        @pl.when((sec == 0) & (t >= WAVES))
        def _():
            for n in range(4):
                forward(t, n, pl.ds(0, M), 0).wait_send()
                forward(t, n, pl.ds(0, M), 1).wait_send()

        return carry

    lax.fori_loop(0, SEGS * WAVES, sent_task, 0)

    @pl.when(sec < NSEC - 1)
    def _():
        for w in range(WAVES):
            pool_copy(w).wait_send()

    @pl.when(sec == NSEC - 1)
    def _():
        total_copy(0, 0).wait_send()
        total_copy(0, 2).wait_send()
        total_copy(1, 1).wait_send()


def body(
    token_ids,
    seg_lengths,
    emb_table,
    mem_init,
    norm_gain,
    w_query,
    w_key,
    w_value,
    w_out,
    layer_mix,
):
    doc_local = token_ids.shape[0]
    vocab_rows, width = emb_table.shape
    depth, head_cols = w_query.shape[1:]
    half, quarter = head_cols // 2, head_cols // 4
    n_tasks = SEGS * WAVES
    dma = pltpu.SemaphoreType.DMA
    bf16, f32 = jnp.bfloat16, jnp.float32
    any_space = pl.BlockSpec(memory_space=pl.ANY)
    vmem = pl.BlockSpec(memory_space=pltpu.VMEM)
    lanes = width // 128
    rows = pl.pallas_call(
        kernel,
        out_shape=jax.ShapeDtypeStruct((NY * NZ * WAVES, lanes, 128), f32),
        in_specs=[any_space] * 10,
        out_specs=vmem,
        scratch_shapes=[
            pltpu.VMEM((WAVES, SEGS, L), jnp.int32),
            pltpu.VMEM((vocab_rows, width), bf16),
            pltpu.VMEM((n_tasks * L, vocab_rows), bf16),
            pltpu.VMEM((M, width), bf16),
            pltpu.VMEM((2, 1, width), f32),
            pltpu.SMEM((doc_local, SEGS), jnp.int32),
            pltpu.SMEM((1,), f32),
            pltpu.VMEM((2 * width, 3 * half), bf16),
            pltpu.VMEM((2 * width, 3 * quarter), bf16),
            pltpu.VMEM((2 * head_cols, width), bf16),
            pltpu.VMEM((n_tasks, 2, NY, ROWS, width), bf16),
            pltpu.VMEM((4 * ROWS, width), bf16),
            pltpu.VMEM((3, 2 * ROWS, half), f32),
            pltpu.VMEM((3, 4 * ROWS, quarter), f32),
            pltpu.VMEM((3, 2 * ROWS, half), bf16),
            pltpu.VMEM((3, 4 * ROWS, quarter), bf16),
            pltpu.VMEM((n_tasks, 2, ROWS, half), bf16),
            pltpu.VMEM((n_tasks, 4, ROWS, quarter), bf16),
            pltpu.VMEM((n_tasks, ROWS, 2 * head_cols), bf16),
            pltpu.VMEM((ROWS, width), f32),
            pltpu.VMEM((n_tasks, ROWS, width), bf16),
            pltpu.VMEM((NSEC, SEGS, WAVES, L, width), bf16),
            pltpu.VMEM((NY, 8, 128), jnp.int32),
            pltpu.VMEM((1, width), f32),
            pltpu.VMEM((WAVES, lanes, 128), f32),
            pltpu.VMEM((NSEC - 1, WAVES, lanes, 128), f32),
            pltpu.VMEM((WAVES, lanes, 128), f32),
            pltpu.VMEM((lanes, 128), f32),
            dma((11,)),
            dma((3, 3)),
            dma((3, 3)),
            dma((2, 4, 2)),
            dma((2, 4, 2)),
            dma((8, 2)),
            dma((8, 2)),
            dma((3,)),
            dma((3,)),
            dma((SEGS,)),
            dma((NSEC - 1, SEGS)),
            dma((WAVES, 7, 2)),
            dma((WAVES, 7)),
            dma((WAVES, 8)),
            dma((n_tasks, 4, 2)),
            dma((n_tasks, 8, 2)),
            dma((n_tasks, 4, 2)),
            dma((n_tasks, 7)),
            dma((n_tasks, 8)),
            dma((WAVES,)),
            dma((NSEC - 1, WAVES)),
            dma((WAVES, 2)),
            dma,
            dma((2, NY * NZ)),
            dma((2, NY * NZ)),
            pltpu.SemaphoreType.REGULAR,
        ],
        compiler_params=pltpu.CompilerParams(
            has_side_effects=True, collective_id=0, vmem_limit_bytes=67000000
        ),
    )(
        token_ids,
        emb_table,
        mem_init,
        norm_gain,
        seg_lengths,
        layer_mix,
        w_query[0],
        w_key[0],
        w_value[0],
        w_out[0],
    )
    return rows.reshape(NY * NZ * WAVES, width)


def solution(mesh):
    return jax.shard_map(
        body,
        mesh=mesh,
        in_specs=(
            P("doc", None, None),
            P("doc", None),
            P("section", "tp"),
            P(None, "tp"),
            P("section", None),
            P("section", "doc", "tp"),
            P("section", "doc", "tp"),
            P("section", "doc", "tp"),
            P("section", None, "tp"),
            P("section"),
        ),
        out_specs=P(None, "tp"),
        check_vma=False,
    )
```

```python
import math

import jax
import jax.numpy as jnp
from jax import lax
from jax.experimental import pallas as pl
from jax.experimental.pallas import tpu as pltpu
from jax.sharding import PartitionSpec as P

HD = 128
M = 16
L = 32
SEGS = 2
ROWS = M + L
EPSILON = 1e-05
NEGATIVE = -1e30

NY = 4
NZ = 8
KEEP_EARLY = 96
KEEP_LATE = 80
WAVES = 2
NSEC = 4


def kernel(
    ids_hbm,
    table_hbm,
    mem_hbm,
    gain_hbm,
    len_hbm,
    mix_hbm,
    wq_ref,
    wk_ref,
    wv_ref,
    wo_ref,
    out_ref,
    ids_ref,
    table,
    picks,
    mem_ref,
    gain_ref,
    len_ref,
    mix_ref,
    weights2,
    weights4,
    w_out,
    blocks,
    scaled,
    sum2,
    sum4,
    qkv2,
    qkv4,
    mixed2,
    mixed4,
    heads,
    update,
    result,
    parts,
    lens,
    pool_row,
    pool,
    pool_in,
    total,
    cast,
    local_sem,
    y_send,
    y_recv,
    z_send,
    z_recv,
    f_send,
    f_recv,
    len_send,
    len_recv,
    part_send,
    part_recv,
    first_send,
    tok_send,
    tok_recv,
    x_send,
    x_recv,
    r_send,
    a_send,
    a_recv,
    pool_send,
    pool_recv,
    total_send,
    total_recv,
    cast_send,
    cast_recv,
    go_sem,
):
    sec = lax.axis_index("section")
    tp = lax.axis_index("tp")
    doc = lax.axis_index("doc")
    z = doc // NY
    y = doc % NY
    bit = y % 2
    y_mate = y + 1 - 2 * bit
    y_twin = NY - 1 - y
    y_far = NY - 1 - y_mate
    kind = ((y + 1) // 2) % 2
    width = blocks.shape[-1]
    depth = wq_ref.shape[0]
    slab = NY * depth
    pair = 2 * depth
    heads_cols = wq_ref.shape[1]

    def where(section, t, d):
        return {"section": section, "tp": t, "doc": d}

    def remote(src, dst, send, recv, to):
        return pltpu.make_async_remote_copy(
            src_ref=src,
            dst_ref=dst,
            send_sem=send,
            recv_sem=recv,
            device_id=to,
            device_id_type=pl.DeviceIdType.MESH,
        )

    def at_y(other):
        return where(sec, tp, z * NY + other)

    wide = sec == 0
    ring = [y, y_mate, y_twin, y_far]
    sources = (wq_ref, wk_ref, wv_ref)
    own_row = pl.multiple_of(doc * depth, depth)

    class Weights:
        def __init__(self, size, keep=KEEP_LATE):
            self.size = size
            self.keep = keep
            self.both = depth - keep
            self.per = heads_cols // size
            self.ref = weights4 if size == 4 else weights2

        def kind(self, other):
            return other if self.size == 4 else ((other + 1) // 2) % 2

        def column(self, other):
            return pl.ds(pl.multiple_of(self.kind(other) * self.per, self.per), self.per)

        def own_copies(self):
            return [
                pltpu.make_async_copy(
                    ref.at[:, self.column(y)],
                    self.ref.at[pl.ds(own_row, depth), pl.ds(j * self.per, self.per)],
                    local_sem.at[j],
                )
                for j, ref in enumerate(sources)
            ]

        def y_copies(self):
            out = []
            for n, other in enumerate(ring[1:]):
                for j, ref in enumerate(sources):
                    first, rows = 0, depth
                    if self.size == 2 and n > 0:
                        first, rows = pl.multiple_of((1 - bit) * self.keep, 16), self.both
                    src = ref.at[pl.ds(first, rows), self.column(other)]
                    dst = self.ref.at[
                        pl.ds(pl.multiple_of(own_row + first, 16), rows),
                        pl.ds(j * self.per, self.per),
                    ]
                    out.append(remote(src, dst, y_send.at[n, j], y_recv.at[n, j], at_y(other)))
            return out

        def rows(self, zz, part):
            if self.size == 4:
                return pl.ds(pl.multiple_of(zz * slab + part * pair, pair), pair)
            if part == 0:
                return pl.ds(pl.multiple_of(zz * slab + (y // 2) * pair, pair), pair)
            return pl.ds(pl.multiple_of(zz * slab + (1 - y // 2) * pair + self.keep, 16), 2 * self.both)

        def z_copy(self, way, step, part, arrival=False):
            ahead = step + 1 if arrival else step
            zz = (z + NZ - ahead) % NZ if way == 0 else (z + ahead) % NZ
            ref = self.ref.at[self.rows(zz, part)]
            to = (z + 1) % NZ if way == 0 else (z + NZ - 1) % NZ
            return remote(
                ref,
                ref,
                z_send.at[way, step, part],
                z_recv.at[way, step, part],
                where(sec, tp, to * NY + y),
            )

        def f_copies(self, slot, zz):
            if self.size == 4:
                return []
            base = zz * slab + (y // 2) * pair
            out = []
            for h, start in enumerate((base, base + pair - self.keep)):
                ref = self.ref.at[pl.ds(pl.multiple_of(start, 16), self.keep)]
                out.append(
                    remote(ref, ref, f_send.at[slot, h], f_recv.at[slot, h], at_y(y_twin))
                )
            return out

        def start_y(self):
            for copy in self.y_copies():
                copy.start()

        def start_z(self):
            for copy in self.own_copies():
                copy.wait()
            for copy in self.y_copies():
                copy.wait_recv()
            for part in range(2):
                for way in range(2):
                    self.z_copy(way, 0, part).start()
            for copy in self.f_copies(0, z):
                copy.start()

        def relay(self, step):
            for part in range(2):
                for way in range(2):
                    if z_sent(way, step, part):
                        self.z_copy(way, step, part, arrival=True).wait_recv()
                        if z_sent(way, step + 1, part):
                            self.z_copy(way, step + 1, part).start()
                        if part == 0:
                            ahead = step + 1
                            zz = (z + NZ - ahead) % NZ if way == 0 else (z + ahead) % NZ
                            for copy in self.f_copies(1 + step + 4 * way, zz):
                                copy.start()

        def finish(self):
            for step in range(4):
                for part in range(2):
                    for way in range(2):
                        if z_sent(way, step, part):
                            self.z_copy(way, step, part).wait_send()
            for k in range(8):
                for copy in self.f_copies(k, z):
                    copy.wait()
            for copy in self.y_copies():
                copy.wait_send()

    def z_sent(way, step, part):
        return step < 3 or (step == 3 and part == way)

    def each(condition, action):
        @pl.when(condition & wide)
        def _():
            action(Weights(4))

        @pl.when(condition & (sec == 1))
        def _():
            action(Weights(2, KEEP_EARLY))

        @pl.when(condition & (sec >= 2))
        def _():
            action(Weights(2))

    slot = tp * NY + y
    peers = [(t, other) for t in (tp, 1 - tp) for other in ring][1:]

    part_width = width // 2

    def part_cols(c):
        return pl.ds(c * part_width, part_width)

    def first_copy(n, w, c):
        t, other = peers[n]
        ref = blocks.at[w, tp, y, :, part_cols(c)]
        return remote(
            ref, ref, first_send.at[w, n, c], x_recv.at[w, slot, c], where(sec, t, z * NY + other)
        )

    def token_copy(n, w):
        t, other = peers[n]
        ref = blocks.at[WAVES + w, tp, y, pl.ds(M, L)]
        return remote(
            ref, ref, tok_send.at[w, n], tok_recv.at[w, slot], where(sec, t, z * NY + other)
        )

    def part_copy(s):
        index = jnp.maximum(sec - 1, 0)
        return remote(
            parts.at[NSEC - 1, s], parts.at[index, s], part_send.at[s], part_recv.at[index, s], where(0, tp, doc)
        )

    def len_copy(n, arrival=False):
        index = ring[n + 1] if arrival else y
        ref = lens.at[index]
        return remote(ref, ref, len_send.at[n], len_recv.at[n], at_y(ring[n + 1]))


    small_copies = [
        pltpu.make_async_copy(len_hbm, len_ref, local_sem.at[4]),
        pltpu.make_async_copy(mix_hbm, mix_ref, local_sem.at[5]),
        pltpu.make_async_copy(ids_hbm, ids_ref, local_sem.at[6]),
        pltpu.make_async_copy(mem_hbm, mem_ref, local_sem.at[7]),
        pltpu.make_async_copy(gain_hbm.at[:, pl.ds(0, width)], gain_ref.at[0], local_sem.at[8]),
        pltpu.make_async_copy(gain_hbm.at[:, pl.ds(width, width)], gain_ref.at[1], local_sem.at[9]),
    ]
    table_copy = pltpu.make_async_copy(table_hbm, table, local_sem.at[10])
    wo_copy = pltpu.make_async_copy(wo_ref, w_out, local_sem.at[3])
    for copy in small_copies:
        copy.start()
    for group in (Weights(4), Weights(2)):

        @pl.when(wide if group.size == 4 else sec >= 1)
        def _():
            for copy in group.own_copies():
                copy.start()


    next_sec = (sec + 1) % NSEC
    last_sec = (sec + NSEC - 1) % NSEC
    greeted = [where(sec, t, z * NY + other) for t, other in peers]
    greeted += [where(sec, tp, (z + step) % NZ * NY + y) for step in (1, NZ - 1)]
    greeted += [
        where(to, t, z * NY + other)
        for to in (next_sec, last_sec)
        for t in (tp, 1 - tp)
        for other in ring
    ]
    greeted += [where((sec + 2) % NSEC, tp, doc)]
    barrier = pltpu.get_barrier_semaphore()
    for to in greeted:
        pl.semaphore_signal(barrier, inc=1, device_id=to, device_id_type=pl.DeviceIdType.MESH)
    pl.semaphore_wait(barrier, len(greeted))

    each(sec >= 0, Weights.start_y)
    table_copy.start()
    for copy in small_copies:
        copy.wait()

    lane = lax.broadcasted_iota(jnp.int32, (1, 128), 1)
    mine = (lane >= bit * ROWS) & (lane < bit * ROWS + ROWS)
    for t in range(SEGS * WAVES):
        lens[y, t : t + 1, :] = jnp.where(mine, len_ref[t % WAVES, t // WAVES], 0)
    for t in range(SEGS * WAVES, 8):
        lens[y, t : t + 1, :] = jnp.zeros((1, 128), jnp.int32)
    for n in range(3):
        len_copy(n).start()

    even = sec % 2 == 0
    odd = sec % 2 == 1
    urgent = sec < 2
    each(sec <= 2, Weights.start_z)

    n_ids = SEGS * WAVES * L
    eye = lax.broadcasted_iota(jnp.int32, (L, L), 0) == lax.broadcasted_iota(jnp.int32, (L, L), 1)
    columns = [
        jnp.sum(
            jnp.where(eye, ids_ref[w, s : s + 1, :].astype(jnp.float32), 0.0), -1, keepdims=True
        )
        for s in range(SEGS)
        for w in range(WAVES)
    ]
    wanted = jnp.concatenate(columns, axis=0).astype(jnp.int32) - sec * table.shape[0]
    for k in range(0, table.shape[0], 512):
        place = lax.broadcasted_iota(jnp.int32, (n_ids, 512), 1) + k
        picks[:, k : k + 512] = jnp.where(place == wanted, 1.0, 0.0).astype(jnp.bfloat16)
    def let_go():
        pl.semaphore_signal(
            go_sem, inc=1, device_id=where(sec + 1, tp, doc), device_id_type=pl.DeviceIdType.MESH
        )

    each(urgent, lambda group: group.relay(0))
    table_copy.wait()
    wo_copy.start()

    def pick(j, carry):
        cols = pl.ds(pl.multiple_of(j * 512, 512), 512)
        rows = jnp.dot(picks[...], table[:, cols], preferred_element_type=jnp.float32)
        parts[NSEC - 1, :, :, :, cols] = rows.astype(jnp.bfloat16).reshape(SEGS, WAVES, L, 512)
        return carry

    lax.fori_loop(0, width // 1024, pick, 0)
    each(urgent, lambda group: group.relay(1))
    lax.fori_loop(width // 1024, width // 512, pick, 0)

    @pl.when(sec > 0)
    def _():
        for s in range(SEGS):
            part_copy(s).start()

    @pl.when(sec == 0)
    def _():
        for s in range(SEGS):
            for index in range(NSEC - 1):
                remote(
                    parts.at[NSEC - 1, s],
                    parts.at[index, s],
                    part_send.at[s],
                    part_recv.at[index, s],
                    where(1, tp, doc),
                ).wait_recv()
            for w in range(WAVES):
                rows = parts[0, s, w] + parts[1, s, w] + parts[2, s, w] + parts[3, s, w]
                blocks[s * WAVES + w, tp, y, M:, :] = rows
                if s == 0:
                    blocks[w, tp, y, :M, :] = mem_ref[...]
            for w in range(WAVES):
                for n in range(7):
                    if s == 0:
                        first_copy(n, w, 0).start()
                        first_copy(n, w, 1).start()

    @pl.when(sec == 0)
    def _():
        Weights(4).relay(2)

    @pl.when(sec == 2)
    def _():
        group = Weights(2)
        for step in range(3):
            group.relay(step)
        let_go()

    @pl.when(sec == 1)
    def _():
        Weights(2, KEEP_EARLY).relay(2)

    @pl.when(sec == 3)
    def _():
        pl.semaphore_wait(go_sem, 1)
        group = Weights(2)
        group.start_z()
        for step in range(3):
            group.relay(step)

    each(sec >= 0, lambda group: group.relay(3))
    each(sec >= 0, Weights.finish)
    wo_copy.wait()
    for n in range(3):
        len_copy(n).wait_send()
        len_copy(n, arrival=True).wait_recv()

    near = sec % 2 == 0

    def members(size):
        return ring if size == 4 else ring[:2]

    def b_copy(t, n, c):
        to_tp = tp if n < 2 else 1 - tp
        return remote(
            result.at[t, :, part_cols(c)],
            blocks.at[t, tp, y, :, part_cols(c)],
            x_send.at[t, n, c],
            x_recv.at[t, slot, c],
            where((sec + 1) % NSEC, to_tp, z * NY + ring[n % 2]),
        )

    def h_copy(t, n, c):
        return remote(
            result.at[t, :, part_cols(c)],
            blocks.at[t, tp, y, :, part_cols(c)],
            x_send.at[t, n, c],
            x_recv.at[t, slot, c],
            where((sec + 1) % NSEC, 1 - tp, z * NY + ring[n]),
        )

    def m_copy(t, n, c):
        return remote(
            result.at[t, pl.ds(0, M), part_cols(c)],
            blocks.at[t + WAVES, tp, y, pl.ds(0, M), part_cols(c)],
            x_send.at[t, n, c],
            x_recv.at[t + WAVES, slot, c],
            where(0, 1 - tp, z * NY + ring[n]),
        )

    def forward(t, n, rows, c):
        ref = blocks.at[t, 1 - tp, ring[n], rows, part_cols(c)]
        return remote(
            ref,
            ref,
            r_send.at[t, n, c],
            x_recv.at[t, (1 - tp) * NY + ring[n], c],
            where(sec, 1 - tp, doc),
        )

    def arrival(t, half, other, rows, c):
        ref = blocks.at[t, half, other, rows, part_cols(c)]
        sem = x_recv.at[t, half * NY + other, c]
        return remote(ref, ref, x_send.at[0, 0, 0], sem, at_y(y_mate))

    def token_arrival(t, half, other):
        ref = blocks.at[t, half, other, pl.ds(M, L)]
        sem = tok_recv.at[t - WAVES, half * NY + other]
        return remote(ref, ref, x_send.at[0, 0, 0], sem, at_y(y_mate))

    def head_cols(size, t, other):
        per = heads_cols // size
        start = t * heads_cols + Weights(size).kind(other) * per
        return pl.ds(pl.multiple_of(start, per), per)

    def a_peers(size):
        return [(t, other) for t in (tp, 1 - tp) for other in members(size)][1:]

    def mixed_rows(size, t, other):
        return mixed4.at[t, other] if size == 4 else mixed2.at[t, other % 2]

    def a_copy(t, n, size):
        to_tp, other = a_peers(size)[n]
        return remote(
            mixed_rows(size, t, other),
            heads.at[t, :, head_cols(size, tp, y)],
            a_send.at[t, n],
            a_recv.at[t, slot],
            where(sec, to_tp, z * NY + other),
        )

    def a_arrival(t, n, size):
        from_tp, other = a_peers(size)[n]
        return remote(
            mixed_rows(size, t, other),
            heads.at[t, :, head_cols(size, from_tp, other)],
            a_send.at[t, n],
            a_recv.at[t, from_tp * NY + other],
            at_y(y_mate),
        )

    def pool_copy(w):
        index = jnp.minimum(sec, NSEC - 2)
        return remote(
            pool.at[w], pool_in.at[index, w], pool_send.at[w], pool_recv.at[index, w], where(NSEC - 1, tp, doc)
        )

    def total_copy(w, to):
        return remote(
            total.at[w], cast, total_send.at[w, to // 2], total_recv, where(to, tp, doc)
        )

    all_rows = pl.ds(0, ROWS)
    scale = 1.0 / math.sqrt(HD)

    def attend(t, size):
        s = t // WAVES
        per = heads_cols // size
        docs = members(size)
        n_rows = size * ROWS
        group = Weights(size)
        far = near & ((sec > 0) | (s == 1))
        first = jnp.where(far, 1 - tp, tp)

        def wait_half(n):
            half = first if n == 0 else 1 - first

            def take(others, rows, onward):
                for c in range(2):
                    for k, other in enumerate(others):
                        arrival(t, half, other, rows, c).wait_recv()
                        if onward:
                            forward(t, k, rows, c).start()

            @pl.when(odd)
            def _():
                take(docs, all_rows, False)

            if size == 2:

                @pl.when(even)
                def _():
                    take(docs, all_rows, n == 0)

                return

            @pl.when(even & (s == 0))
            def _():
                take(docs[1 - n :], all_rows, False)

            @pl.when(even & (s == 1))
            def _():
                for other in docs[n:]:
                    token_arrival(t, half, other).wait_recv()
                take(docs, pl.ds(0, M), n == 0)

        step = 128
        total_sum = sum2 if size == 2 else sum4
        qkv = qkv2 if size == 2 else qkv4
        base = pl.multiple_of(y // 2 * 2, 2) if size == 2 else 0
        square = jnp.zeros((n_rows, step), jnp.float32)
        for n in range(2):
            half = first if n == 0 else 1 - first
            wait_half(n)
            for c in range(0, width, step):
                x = blocks[t, half, pl.ds(base, size), :, c : c + step]
                x = x.reshape(n_rows, step).astype(jnp.float32)
                square = square + x * x
                scaled[:n_rows, c : c + step] = (x * gain_ref[half, :, c : c + step]).astype(
                    jnp.bfloat16
                )
            if n == 1:
                mean_square = jnp.sum(square, -1, keepdims=True) * (1.0 / (2 * width))
                inverse = lax.rsqrt(mean_square + EPSILON)
            rows = pl.ds(pl.multiple_of(half * width, width), width)

            for j in range(3):
                cols = slice(j * per, (j + 1) * per)
                out = jnp.dot(
                    scaled[:n_rows, :], group.ref[rows, cols], preferred_element_type=jnp.float32
                )
                if n == 0:
                    total_sum[j] = out
                else:
                    qkv[j] = ((total_sum[j] + out) * inverse).astype(jnp.bfloat16)

        shape = (2 * ROWS, 2 * ROWS)
        row = lax.broadcasted_iota(jnp.int32, shape, 0)
        col = lax.broadcasted_iota(jnp.int32, shape, 1)
        row_doc = (row >= ROWS).astype(jnp.int32)
        col_doc = (col >= ROWS).astype(jnp.int32)
        i = row - ROWS * row_doc
        j = col - ROWS * col_doc
        ordered = (row_doc == col_doc) & ((j < M) | (i < M) | (j <= i))
        for p in range(size // 2):
            d = base + 2 * p
            lengths = (lens[d, pl.ds(t, 1), :] + lens[d + 1, pl.ds(t, 1), :])[:, : 2 * ROWS]
            allowed = ordered & ((j < M) | (j - M < lengths))
            own = slice(p * 2 * ROWS, (p + 1) * 2 * ROWS)
            for h in range(per // HD):
                cols = slice(h * HD, (h + 1) * HD)
                scores = (
                    lax.dot_general(
                        qkv[0, own, cols],
                        qkv[1, own, cols],
                        (((1,), (1,)), ((), ())),
                        preferred_element_type=jnp.float32,
                    )
                    * scale
                )
                scores = jnp.where(allowed, scores, NEGATIVE)
                exps = jnp.where(allowed, jnp.exp(scores), 0.0)
                probs = (exps / jnp.sum(exps, -1, keepdims=True)).astype(jnp.bfloat16)
                out = jnp.dot(probs, qkv[2, own, cols], preferred_element_type=jnp.float32)
                out = out.astype(jnp.bfloat16).reshape(2, ROWS, HD)
                if size == 4:
                    mixed4[t, 2 * p : 2 * p + 2, :, cols] = out
                else:
                    mixed2[t, :, :, cols] = out

        count = 2 * size - 1
        for n in reversed(range(count)):
            a_copy(t, n, size).start()
        heads[t, :, head_cols(size, tp, y)] = mixed4[t, y] if size == 4 else mixed2[t, bit]
        update[...] = jnp.zeros_like(update)
        where_from = [(tp, y)] + a_peers(size)
        for n in range(count):
            own = head_cols(size, *where_from[n])
            update[...] += jnp.dot(
                heads[t, :, own], w_out[own, :], preferred_element_type=jnp.float32
            )
            a_arrival(t, n, size).wait_recv()
        last = head_cols(size, *where_from[count])

        w = t % WAVES
        length = len_ref[w, s]
        position = lax.broadcasted_iota(jnp.int32, (ROWS, 1), 0)
        token_ok = (position >= M) & (position - M < length)
        factor = mix_ref[0] / length.astype(jnp.float32)

        for c in range(2):
            for k in range(0, part_width, 512):
                cols = slice(c * part_width + k, c * part_width + k + 512)
                out = update[:, cols] + jnp.dot(
                    heads[t, :, last], w_out[last, cols], preferred_element_type=jnp.float32
                )
                out = (blocks[t, tp, y, :, cols].astype(jnp.float32) + out).astype(jnp.bfloat16)
                result[t, :, cols] = out
                summed = jnp.where(token_ok, out.astype(jnp.float32), 0.0)
                pool_row[:, cols] = jnp.sum(summed, 0, keepdims=True) * factor

            @pl.when(near)
            def _():
                for n in (3, 2, 1, 0):
                    b_copy(t, n, c).start()

            if size == 2:

                @pl.when(sec == 1)
                def _():
                    for n in range(2):
                        h_copy(t, n, c).start()

                @pl.when((sec == NSEC - 1) & (s == 0))
                def _():
                    for n in range(4):
                        m_copy(t, n, c).start()

    def task(t, carry):
        s = t // WAVES
        w = t % WAVES

        @pl.when(wide)
        def _():
            attend(t, 4)

        @pl.when(sec >= 1)
        def _():
            attend(t, 2)

        @pl.when((sec == 0) & (t == WAVES - 1))
        def _():
            for document in range(WAVES):
                for n in range(7):
                    token_copy(n, document).start()

        @pl.when(s == 1)
        def _():
            for k in range(width // 128):
                pool[w, k : k + 1, :] = pool_row[:, k * 128 : (k + 1) * 128]

            @pl.when(sec < NSEC - 1)
            def _():
                pool_copy(w).start()

            @pl.when(sec == NSEC - 1)
            def _():
                for index in range(NSEC - 1):
                    remote(
                        pool.at[w],
                        pool_in.at[index, w],
                        pool_send.at[w],
                        pool_recv.at[index, w],
                        where(0, tp, doc),
                    ).wait_recv()
                summed = pool[w] + pool_in[0, w] + pool_in[1, w] + pool_in[2, w]
                total[w] = summed

                @pl.when(w == 0)
                def _():
                    total_copy(0, 0).start()
                    total_copy(0, 2).start()

                @pl.when(w == 1)
                def _():
                    total_copy(1, 1).start()
                    cast[...] = summed

        return carry

    lax.fori_loop(0, SEGS * WAVES, task, 0)

    core = sec % 2
    base = sec - core
    n_docs = NY * NZ

    @pl.when(sec < NSEC - 1)
    def _():
        remote(
            total.at[0], cast, total_send.at[0, 0], total_recv, where(NSEC - 1, tp, doc)
        ).wait_recv()

    def cast_copy(k, which):
        to = base + core if which == 0 else base + 1 - core
        return remote(
            cast,
            out_ref.at[2 * doc + core],
            cast_send.at[which, k],
            cast_recv.at[core, doc],
            where(to, tp, (doc + k) % n_docs),
        )

    cast_copy(0, 1).start()

    def send_row(k, carry):
        cast_copy(k, 0).start()
        cast_copy(k, 1).start()
        return carry

    lax.fori_loop(1, n_docs, send_row, 0)
    out_ref[2 * doc + core] = cast[...]

    def row_arrival(c, d):
        return remote(
            cast, out_ref.at[2 * d + c], cast_send.at[0, 0], cast_recv.at[c, d], where(base + 1 - core, tp, doc)
        )

    row_arrival(1 - core, doc).wait_recv()

    def take_row(k, carry):
        d = (doc + k) % n_docs
        row_arrival(core, d).wait_recv()
        row_arrival(1 - core, d).wait_recv()
        return carry

    lax.fori_loop(1, n_docs, take_row, 0)

    cast_copy(0, 1).wait_send()

    def sent_row(k, carry):
        cast_copy(k, 0).wait_send()
        cast_copy(k, 1).wait_send()
        return carry

    lax.fori_loop(1, n_docs, sent_row, 0)

    @pl.when(sec > 0)
    def _():
        for s in range(SEGS):
            part_copy(s).wait_send()

    @pl.when(sec == 0)
    def _():
        for w in range(WAVES):
            for n in range(7):
                first_copy(n, w, 0).wait_send()
                first_copy(n, w, 1).wait_send()
                token_copy(n, w).wait_send()

    def sent_task(t, carry):
        @pl.when(wide)
        def _():
            for n in range(7):
                a_copy(t, n, 4).wait_send()

        @pl.when(sec >= 1)
        def _():
            for n in range(3):
                a_copy(t, n, 2).wait_send()

        @pl.when(near)
        def _():
            for n in range(4):
                b_copy(t, n, 0).wait_send()
                b_copy(t, n, 1).wait_send()

        @pl.when(sec == 1)
        def _():
            for n in range(2):
                h_copy(t, n, 0).wait_send()
                h_copy(t, n, 1).wait_send()

        @pl.when((sec == NSEC - 1) & (t < WAVES))
        def _():
            for n in range(4):
                m_copy(t, n, 0).wait_send()
                m_copy(t, n, 1).wait_send()

        @pl.when(sec == 2)
        def _():
            for n in range(2):
                forward(t, n, all_rows, 0).wait_send()
                forward(t, n, all_rows, 1).wait_send()

        @pl.when((sec == 0) & (t >= WAVES))
        def _():
            for n in range(4):
                forward(t, n, pl.ds(0, M), 0).wait_send()
                forward(t, n, pl.ds(0, M), 1).wait_send()

        return carry

    lax.fori_loop(0, SEGS * WAVES, sent_task, 0)

    @pl.when(sec < NSEC - 1)
    def _():
        for w in range(WAVES):
            pool_copy(w).wait_send()

    @pl.when(sec == NSEC - 1)
    def _():
        total_copy(0, 0).wait_send()
        total_copy(0, 2).wait_send()
        total_copy(1, 1).wait_send()


def body(
    token_ids,
    seg_lengths,
    emb_table,
    mem_init,
    norm_gain,
    w_query,
    w_key,
    w_value,
    w_out,
    layer_mix,
):
    doc_local = token_ids.shape[0]
    vocab_rows, width = emb_table.shape
    depth, head_cols = w_query.shape[1:]
    half, quarter = head_cols // 2, head_cols // 4
    n_tasks = SEGS * WAVES
    dma = pltpu.SemaphoreType.DMA
    bf16, f32 = jnp.bfloat16, jnp.float32
    any_space = pl.BlockSpec(memory_space=pl.ANY)
    vmem = pl.BlockSpec(memory_space=pltpu.VMEM)
    lanes = width // 128
    rows = pl.pallas_call(
        kernel,
        out_shape=jax.ShapeDtypeStruct((NY * NZ * WAVES, lanes, 128), f32),
        in_specs=[any_space] * 10,
        out_specs=vmem,
        scratch_shapes=[
            pltpu.VMEM((WAVES, SEGS, L), jnp.int32),
            pltpu.VMEM((vocab_rows, width), bf16),
            pltpu.VMEM((n_tasks * L, vocab_rows), bf16),
            pltpu.VMEM((M, width), bf16),
            pltpu.VMEM((2, 1, width), f32),
            pltpu.SMEM((doc_local, SEGS), jnp.int32),
            pltpu.SMEM((1,), f32),
            pltpu.VMEM((2 * width, 3 * half), bf16),
            pltpu.VMEM((2 * width, 3 * quarter), bf16),
            pltpu.VMEM((2 * head_cols, width), bf16),
            pltpu.VMEM((n_tasks, 2, NY, ROWS, width), bf16),
            pltpu.VMEM((4 * ROWS, width), bf16),
            pltpu.VMEM((3, 2 * ROWS, half), f32),
            pltpu.VMEM((3, 4 * ROWS, quarter), f32),
            pltpu.VMEM((3, 2 * ROWS, half), bf16),
            pltpu.VMEM((3, 4 * ROWS, quarter), bf16),
            pltpu.VMEM((n_tasks, 2, ROWS, half), bf16),
            pltpu.VMEM((n_tasks, 4, ROWS, quarter), bf16),
            pltpu.VMEM((n_tasks, ROWS, 2 * head_cols), bf16),
            pltpu.VMEM((ROWS, width), f32),
            pltpu.VMEM((n_tasks, ROWS, width), bf16),
            pltpu.VMEM((NSEC, SEGS, WAVES, L, width), bf16),
            pltpu.VMEM((NY, 8, 128), jnp.int32),
            pltpu.VMEM((1, width), f32),
            pltpu.VMEM((WAVES, lanes, 128), f32),
            pltpu.VMEM((NSEC - 1, WAVES, lanes, 128), f32),
            pltpu.VMEM((WAVES, lanes, 128), f32),
            pltpu.VMEM((lanes, 128), f32),
            dma((11,)),
            dma((3, 3)),
            dma((3, 3)),
            dma((2, 4, 2)),
            dma((2, 4, 2)),
            dma((8, 2)),
            dma((8, 2)),
            dma((3,)),
            dma((3,)),
            dma((SEGS,)),
            dma((NSEC - 1, SEGS)),
            dma((WAVES, 7, 2)),
            dma((WAVES, 7)),
            dma((WAVES, 8)),
            dma((n_tasks, 4, 2)),
            dma((n_tasks, 8, 2)),
            dma((n_tasks, 4, 2)),
            dma((n_tasks, 7)),
            dma((n_tasks, 8)),
            dma((WAVES,)),
            dma((NSEC - 1, WAVES)),
            dma((WAVES, 2)),
            dma,
            dma((2, NY * NZ)),
            dma((2, NY * NZ)),
            pltpu.SemaphoreType.REGULAR,
        ],
        compiler_params=pltpu.CompilerParams(
            has_side_effects=True, collective_id=0, vmem_limit_bytes=67000000
        ),
    )(
        token_ids,
        emb_table,
        mem_init,
        norm_gain,
        seg_lengths,
        layer_mix,
        w_query[0],
        w_key[0],
        w_value[0],
        w_out[0],
    )
    return rows.reshape(NY * NZ * WAVES, width)


def solution(mesh):
    return jax.shard_map(
        body,
        mesh=mesh,
        in_specs=(
            P("doc", None, None),
            P("doc", None),
            P("section", "tp"),
            P(None, "tp"),
            P("section", None),
            P("section", "doc", "tp"),
            P("section", "doc", "tp"),
            P("section", "doc", "tp"),
            P("section", None, "tp"),
            P("section"),
        ),
        out_specs=P(None, "tp"),
        check_vma=False,
    )
```

```python
import math

import jax
import jax.numpy as jnp
from jax import lax
from jax.experimental import pallas as pl
from jax.experimental.pallas import tpu as pltpu
from jax.sharding import PartitionSpec as P

HD = 128
M = 16
L = 32
SEGS = 2
ROWS = M + L
EPSILON = 1e-05
NEGATIVE = -1e30

NY = 4
NZ = 8
KEEP_EARLY = 96
KEEP_LATE = 80
WAVES = 2
NSEC = 4


def kernel(
    ids_hbm,
    table_hbm,
    mem_hbm,
    gain_hbm,
    len_hbm,
    mix_hbm,
    wq_ref,
    wk_ref,
    wv_ref,
    wo_ref,
    out_ref,
    ids_ref,
    table,
    picks,
    mem_ref,
    gain_ref,
    len_ref,
    mix_ref,
    weights2,
    weights4,
    w_out,
    blocks,
    scaled,
    sum2,
    sum4,
    qkv2,
    qkv4,
    mixed2,
    mixed4,
    heads,
    update,
    result,
    parts,
    lens,
    pool_row,
    pool,
    pool_in,
    total,
    cast,
    local_sem,
    y_send,
    y_recv,
    z_send,
    z_recv,
    f_send,
    f_recv,
    len_send,
    len_recv,
    part_send,
    part_recv,
    first_send,
    tok_send,
    tok_recv,
    x_send,
    x_recv,
    r_send,
    a_send,
    a_recv,
    pool_send,
    pool_recv,
    total_send,
    total_recv,
    cast_send,
    cast_recv,
    go_sem,
):
    sec = lax.axis_index("section")
    tp = lax.axis_index("tp")
    doc = lax.axis_index("doc")
    z = doc // NY
    y = doc % NY
    bit = y % 2
    y_mate = y + 1 - 2 * bit
    y_twin = NY - 1 - y
    y_far = NY - 1 - y_mate
    kind = ((y + 1) // 2) % 2
    width = blocks.shape[-1]
    depth = wq_ref.shape[0]
    slab = NY * depth
    pair = 2 * depth
    heads_cols = wq_ref.shape[1]

    def where(section, t, d):
        return {"section": section, "tp": t, "doc": d}

    def remote(src, dst, send, recv, to):
        return pltpu.make_async_remote_copy(
            src_ref=src,
            dst_ref=dst,
            send_sem=send,
            recv_sem=recv,
            device_id=to,
            device_id_type=pl.DeviceIdType.MESH,
        )

    def at_y(other):
        return where(sec, tp, z * NY + other)

    wide = sec == 0
    ring = [y, y_mate, y_twin, y_far]
    sources = (wq_ref, wk_ref, wv_ref)
    own_row = pl.multiple_of(doc * depth, depth)

    class Weights:
        def __init__(self, size, keep=KEEP_LATE):
            self.size = size
            self.keep = keep
            self.both = depth - keep
            self.per = heads_cols // size
            self.ref = weights4 if size == 4 else weights2

        def kind(self, other):
            return other if self.size == 4 else ((other + 1) // 2) % 2

        def column(self, other):
            return pl.ds(pl.multiple_of(self.kind(other) * self.per, self.per), self.per)

        def own_copies(self):
            return [
                pltpu.make_async_copy(
                    ref.at[:, self.column(y)],
                    self.ref.at[pl.ds(own_row, depth), pl.ds(j * self.per, self.per)],
                    local_sem.at[j],
                )
                for j, ref in enumerate(sources)
            ]

        def y_copies(self):
            out = []
            for n, other in enumerate(ring[1:]):
                for j, ref in enumerate(sources):
                    first, rows = 0, depth
                    if self.size == 2 and n > 0:
                        first, rows = pl.multiple_of((1 - bit) * self.keep, 16), self.both
                    src = ref.at[pl.ds(first, rows), self.column(other)]
                    dst = self.ref.at[
                        pl.ds(pl.multiple_of(own_row + first, 16), rows),
                        pl.ds(j * self.per, self.per),
                    ]
                    out.append(remote(src, dst, y_send.at[n, j], y_recv.at[n, j], at_y(other)))
            return out

        def rows(self, zz, part):
            if self.size == 4:
                return pl.ds(pl.multiple_of(zz * slab + part * pair, pair), pair)
            if part == 0:
                return pl.ds(pl.multiple_of(zz * slab + (y // 2) * pair, pair), pair)
            return pl.ds(pl.multiple_of(zz * slab + (1 - y // 2) * pair + self.keep, 16), 2 * self.both)

        def z_copy(self, way, step, part, arrival=False):
            ahead = step + 1 if arrival else step
            zz = (z + NZ - ahead) % NZ if way == 0 else (z + ahead) % NZ
            ref = self.ref.at[self.rows(zz, part)]
            to = (z + 1) % NZ if way == 0 else (z + NZ - 1) % NZ
            return remote(
                ref,
                ref,
                z_send.at[way, step, part],
                z_recv.at[way, step, part],
                where(sec, tp, to * NY + y),
            )

        def f_copies(self, slot, zz):
            if self.size == 4:
                return []
            base = zz * slab + (y // 2) * pair
            out = []
            for h, start in enumerate((base, base + pair - self.keep)):
                ref = self.ref.at[pl.ds(pl.multiple_of(start, 16), self.keep)]
                out.append(
                    remote(ref, ref, f_send.at[slot, h], f_recv.at[slot, h], at_y(y_twin))
                )
            return out

        def start_y(self):
            for copy in self.y_copies():
                copy.start()

        def start_z(self):
            for copy in self.own_copies():
                copy.wait()
            for copy in self.y_copies():
                copy.wait_recv()
            for part in range(2):
                for way in range(2):
                    self.z_copy(way, 0, part).start()
            for copy in self.f_copies(0, z):
                copy.start()

        def relay(self, step):
            for part in range(2):
                for way in range(2):
                    if z_sent(way, step, part):
                        self.z_copy(way, step, part, arrival=True).wait_recv()
                        if z_sent(way, step + 1, part):
                            self.z_copy(way, step + 1, part).start()
                        if part == 0:
                            ahead = step + 1
                            zz = (z + NZ - ahead) % NZ if way == 0 else (z + ahead) % NZ
                            for copy in self.f_copies(1 + step + 4 * way, zz):
                                copy.start()

        def finish(self):
            for step in range(4):
                for part in range(2):
                    for way in range(2):
                        if z_sent(way, step, part):
                            self.z_copy(way, step, part).wait_send()
            for k in range(8):
                for copy in self.f_copies(k, z):
                    copy.wait()
            for copy in self.y_copies():
                copy.wait_send()

    def z_sent(way, step, part):
        return step < 3 or (step == 3 and part == way)

    def each(condition, action):
        @pl.when(condition & wide)
        def _():
            action(Weights(4))

        @pl.when(condition & (sec == 1))
        def _():
            action(Weights(2, KEEP_EARLY))

        @pl.when(condition & (sec >= 2))
        def _():
            action(Weights(2))

    slot = tp * NY + y
    peers = [(t, other) for t in (tp, 1 - tp) for other in ring][1:]

    part_width = width // 2

    def part_cols(c):
        return pl.ds(c * part_width, part_width)

    def first_copy(n, w, c):
        t, other = peers[n]
        ref = blocks.at[w, tp, y, :, part_cols(c)]
        return remote(
            ref, ref, first_send.at[w, n, c], x_recv.at[w, slot, c], where(sec, t, z * NY + other)
        )

    def token_copy(n, w):
        t, other = peers[n]
        ref = blocks.at[WAVES + w, tp, y, pl.ds(M, L)]
        return remote(
            ref, ref, tok_send.at[w, n], tok_recv.at[w, slot], where(sec, t, z * NY + other)
        )

    def part_copy(s):
        index = jnp.maximum(sec - 1, 0)
        return remote(
            parts.at[NSEC - 1, s], parts.at[index, s], part_send.at[s], part_recv.at[index, s], where(0, tp, doc)
        )

    def len_copy(n, arrival=False):
        index = ring[n + 1] if arrival else y
        ref = lens.at[index]
        return remote(ref, ref, len_send.at[n], len_recv.at[n], at_y(ring[n + 1]))


    small_copies = [
        pltpu.make_async_copy(len_hbm, len_ref, local_sem.at[4]),
        pltpu.make_async_copy(mix_hbm, mix_ref, local_sem.at[5]),
        pltpu.make_async_copy(ids_hbm, ids_ref, local_sem.at[6]),
        pltpu.make_async_copy(mem_hbm, mem_ref, local_sem.at[7]),
        pltpu.make_async_copy(gain_hbm.at[:, pl.ds(0, width)], gain_ref.at[0], local_sem.at[8]),
        pltpu.make_async_copy(gain_hbm.at[:, pl.ds(width, width)], gain_ref.at[1], local_sem.at[9]),
    ]
    table_copy = pltpu.make_async_copy(table_hbm, table, local_sem.at[10])
    wo_copy = pltpu.make_async_copy(wo_ref, w_out, local_sem.at[3])
    for copy in small_copies:
        copy.start()
    for group in (Weights(4), Weights(2)):

        @pl.when(wide if group.size == 4 else sec >= 1)
        def _():
            for copy in group.own_copies():
                copy.start()


    next_sec = (sec + 1) % NSEC
    last_sec = (sec + NSEC - 1) % NSEC
    greeted = [where(sec, t, z * NY + other) for t, other in peers]
    greeted += [where(sec, tp, (z + step) % NZ * NY + y) for step in (1, NZ - 1)]
    greeted += [
        where(to, t, z * NY + other)
        for to in (next_sec, last_sec)
        for t in (tp, 1 - tp)
        for other in ring
    ]
    greeted += [where((sec + 2) % NSEC, tp, doc)]
    barrier = pltpu.get_barrier_semaphore()
    for to in greeted:
        pl.semaphore_signal(barrier, inc=1, device_id=to, device_id_type=pl.DeviceIdType.MESH)
    pl.semaphore_wait(barrier, len(greeted))

    each(sec >= 0, Weights.start_y)
    table_copy.start()
    for copy in small_copies:
        copy.wait()

    lane = lax.broadcasted_iota(jnp.int32, (1, 128), 1)
    mine = (lane >= bit * ROWS) & (lane < bit * ROWS + ROWS)
    for t in range(SEGS * WAVES):
        lens[y, t : t + 1, :] = jnp.where(mine, len_ref[t % WAVES, t // WAVES], 0)
    for t in range(SEGS * WAVES, 8):
        lens[y, t : t + 1, :] = jnp.zeros((1, 128), jnp.int32)
    for n in range(3):
        len_copy(n).start()

    even = sec % 2 == 0
    odd = sec % 2 == 1
    urgent = sec < 2
    each(sec <= 2, Weights.start_z)

    n_ids = SEGS * WAVES * L
    eye = lax.broadcasted_iota(jnp.int32, (L, L), 0) == lax.broadcasted_iota(jnp.int32, (L, L), 1)
    columns = [
        jnp.sum(
            jnp.where(eye, ids_ref[w, s : s + 1, :].astype(jnp.float32), 0.0), -1, keepdims=True
        )
        for s in range(SEGS)
        for w in range(WAVES)
    ]
    wanted = jnp.concatenate(columns, axis=0).astype(jnp.int32) - sec * table.shape[0]
    for k in range(0, table.shape[0], 512):
        place = lax.broadcasted_iota(jnp.int32, (n_ids, 512), 1) + k
        picks[:, k : k + 512] = jnp.where(place == wanted, 1.0, 0.0).astype(jnp.bfloat16)
    def let_go():
        pl.semaphore_signal(
            go_sem, inc=1, device_id=where(sec + 1, tp, doc), device_id_type=pl.DeviceIdType.MESH
        )

    each(urgent, lambda group: group.relay(0))
    table_copy.wait()
    wo_copy.start()

    def pick(j, carry):
        cols = pl.ds(pl.multiple_of(j * 512, 512), 512)
        rows = jnp.dot(picks[...], table[:, cols], preferred_element_type=jnp.float32)
        parts[NSEC - 1, :, :, :, cols] = rows.astype(jnp.bfloat16).reshape(SEGS, WAVES, L, 512)
        return carry

    lax.fori_loop(0, width // 1024, pick, 0)
    each(urgent, lambda group: group.relay(1))
    lax.fori_loop(width // 1024, width // 512, pick, 0)

    @pl.when(sec > 0)
    def _():
        for s in range(SEGS):
            part_copy(s).start()

    @pl.when(sec == 0)
    def _():
        for s in range(SEGS):
            for index in range(NSEC - 1):
                remote(
                    parts.at[NSEC - 1, s],
                    parts.at[index, s],
                    part_send.at[s],
                    part_recv.at[index, s],
                    where(1, tp, doc),
                ).wait_recv()
            for w in range(WAVES):
                rows = parts[0, s, w] + parts[1, s, w] + parts[2, s, w] + parts[3, s, w]
                blocks[s * WAVES + w, tp, y, M:, :] = rows
                if s == 0:
                    blocks[w, tp, y, :M, :] = mem_ref[...]
            for w in range(WAVES):
                for n in range(7):
                    if s == 0:
                        first_copy(n, w, 0).start()
                        first_copy(n, w, 1).start()

    @pl.when(sec == 0)
    def _():
        Weights(4).relay(2)

    @pl.when(sec == 2)
    def _():
        group = Weights(2)
        for step in range(3):
            group.relay(step)
        let_go()

    @pl.when(sec == 1)
    def _():
        Weights(2, KEEP_EARLY).relay(2)

    @pl.when(sec == 3)
    def _():
        pl.semaphore_wait(go_sem, 1)
        group = Weights(2)
        group.start_z()
        for step in range(3):
            group.relay(step)

    each(sec >= 0, lambda group: group.relay(3))
    each(sec >= 0, Weights.finish)
    wo_copy.wait()
    for n in range(3):
        len_copy(n).wait_send()
        len_copy(n, arrival=True).wait_recv()

    near = sec % 2 == 0

    def members(size):
        return ring if size == 4 else ring[:2]

    def b_copy(t, n, c):
        to_tp = tp if n < 2 else 1 - tp
        return remote(
            result.at[t, :, part_cols(c)],
            blocks.at[t, tp, y, :, part_cols(c)],
            x_send.at[t, n, c],
            x_recv.at[t, slot, c],
            where((sec + 1) % NSEC, to_tp, z * NY + ring[n % 2]),
        )

    def h_copy(t, n, c):
        return remote(
            result.at[t, :, part_cols(c)],
            blocks.at[t, tp, y, :, part_cols(c)],
            x_send.at[t, n, c],
            x_recv.at[t, slot, c],
            where((sec + 1) % NSEC, 1 - tp, z * NY + ring[n]),
        )

    def m_copy(t, n, c):
        return remote(
            result.at[t, pl.ds(0, M), part_cols(c)],
            blocks.at[t + WAVES, tp, y, pl.ds(0, M), part_cols(c)],
            x_send.at[t, n, c],
            x_recv.at[t + WAVES, slot, c],
            where(0, 1 - tp, z * NY + ring[n]),
        )

    def forward(t, n, rows, c):
        ref = blocks.at[t, 1 - tp, ring[n], rows, part_cols(c)]
        return remote(
            ref,
            ref,
            r_send.at[t, n, c],
            x_recv.at[t, (1 - tp) * NY + ring[n], c],
            where(sec, 1 - tp, doc),
        )

    def arrival(t, half, other, rows, c):
        ref = blocks.at[t, half, other, rows, part_cols(c)]
        sem = x_recv.at[t, half * NY + other, c]
        return remote(ref, ref, x_send.at[0, 0, 0], sem, at_y(y_mate))

    def token_arrival(t, half, other):
        ref = blocks.at[t, half, other, pl.ds(M, L)]
        sem = tok_recv.at[t - WAVES, half * NY + other]
        return remote(ref, ref, x_send.at[0, 0, 0], sem, at_y(y_mate))

    def head_cols(size, t, other):
        per = heads_cols // size
        start = t * heads_cols + Weights(size).kind(other) * per
        return pl.ds(pl.multiple_of(start, per), per)

    def a_peers(size):
        return [(t, other) for t in (tp, 1 - tp) for other in members(size)][1:]

    def mixed_rows(size, t, other):
        return mixed4.at[t, other] if size == 4 else mixed2.at[t, other % 2]

    def a_copy(t, n, size):
        to_tp, other = a_peers(size)[n]
        return remote(
            mixed_rows(size, t, other),
            heads.at[t, :, head_cols(size, tp, y)],
            a_send.at[t, n],
            a_recv.at[t, slot],
            where(sec, to_tp, z * NY + other),
        )

    def a_arrival(t, n, size):
        from_tp, other = a_peers(size)[n]
        return remote(
            mixed_rows(size, t, other),
            heads.at[t, :, head_cols(size, from_tp, other)],
            a_send.at[t, n],
            a_recv.at[t, from_tp * NY + other],
            at_y(y_mate),
        )

    def pool_copy(w):
        index = jnp.minimum(sec, NSEC - 2)
        return remote(
            pool.at[w], pool_in.at[index, w], pool_send.at[w], pool_recv.at[index, w], where(NSEC - 1, tp, doc)
        )

    def total_copy(w, to):
        return remote(
            total.at[w], cast, total_send.at[w, to // 2], total_recv, where(to, tp, doc)
        )

    all_rows = pl.ds(0, ROWS)
    scale = 1.0 / math.sqrt(HD)

    def attend(t, size):
        s = t // WAVES
        per = heads_cols // size
        docs = members(size)
        n_rows = size * ROWS
        group = Weights(size)
        far = near & ((sec > 0) | (s == 1))
        first = jnp.where(far, 1 - tp, tp)

        def wait_half(n):
            half = first if n == 0 else 1 - first

            def take(others, rows, onward):
                for c in range(2):
                    for k, other in enumerate(others):
                        arrival(t, half, other, rows, c).wait_recv()
                        if onward:
                            forward(t, k, rows, c).start()

            @pl.when(odd)
            def _():
                take(docs, all_rows, False)

            if size == 2:

                @pl.when(even)
                def _():
                    take(docs, all_rows, n == 0)

                return

            @pl.when(even & (s == 0))
            def _():
                take(docs[1 - n :], all_rows, False)

            @pl.when(even & (s == 1))
            def _():
                for other in docs[n:]:
                    token_arrival(t, half, other).wait_recv()
                take(docs, pl.ds(0, M), n == 0)

        step = 128
        total_sum = sum2 if size == 2 else sum4
        qkv = qkv2 if size == 2 else qkv4
        base = pl.multiple_of(y // 2 * 2, 2) if size == 2 else 0
        square = jnp.zeros((n_rows, step), jnp.float32)
        for n in range(2):
            half = first if n == 0 else 1 - first
            wait_half(n)
            for c in range(0, width, step):
                x = blocks[t, half, pl.ds(base, size), :, c : c + step]
                x = x.reshape(n_rows, step).astype(jnp.float32)
                square = square + x * x
                scaled[:n_rows, c : c + step] = (x * gain_ref[half, :, c : c + step]).astype(
                    jnp.bfloat16
                )
            if n == 1:
                mean_square = jnp.sum(square, -1, keepdims=True) * (1.0 / (2 * width))
                inverse = lax.rsqrt(mean_square + EPSILON)
            rows = pl.ds(pl.multiple_of(half * width, width), width)

            for j in range(3):
                cols = slice(j * per, (j + 1) * per)
                out = jnp.dot(
                    scaled[:n_rows, :], group.ref[rows, cols], preferred_element_type=jnp.float32
                )
                if n == 0:
                    total_sum[j] = out
                else:
                    qkv[j] = ((total_sum[j] + out) * inverse).astype(jnp.bfloat16)

        shape = (2 * ROWS, 2 * ROWS)
        row = lax.broadcasted_iota(jnp.int32, shape, 0)
        col = lax.broadcasted_iota(jnp.int32, shape, 1)
        row_doc = (row >= ROWS).astype(jnp.int32)
        col_doc = (col >= ROWS).astype(jnp.int32)
        i = row - ROWS * row_doc
        j = col - ROWS * col_doc
        ordered = (row_doc == col_doc) & ((j < M) | (i < M) | (j <= i))
        for p in range(size // 2):
            d = base + 2 * p
            lengths = (lens[d, pl.ds(t, 1), :] + lens[d + 1, pl.ds(t, 1), :])[:, : 2 * ROWS]
            allowed = ordered & ((j < M) | (j - M < lengths))
            own = slice(p * 2 * ROWS, (p + 1) * 2 * ROWS)
            for h in range(per // HD):
                cols = slice(h * HD, (h + 1) * HD)
                scores = (
                    lax.dot_general(
                        qkv[0, own, cols],
                        qkv[1, own, cols],
                        (((1,), (1,)), ((), ())),
                        preferred_element_type=jnp.float32,
                    )
                    * scale
                )
                scores = jnp.where(allowed, scores, NEGATIVE)
                exps = jnp.where(allowed, jnp.exp(scores), 0.0)
                probs = (exps / jnp.sum(exps, -1, keepdims=True)).astype(jnp.bfloat16)
                out = jnp.dot(probs, qkv[2, own, cols], preferred_element_type=jnp.float32)
                out = out.astype(jnp.bfloat16).reshape(2, ROWS, HD)
                if size == 4:
                    mixed4[t, 2 * p : 2 * p + 2, :, cols] = out
                else:
                    mixed2[t, :, :, cols] = out

        count = 2 * size - 1
        for n in reversed(range(count)):
            a_copy(t, n, size).start()
        heads[t, :, head_cols(size, tp, y)] = mixed4[t, y] if size == 4 else mixed2[t, bit]

    def output(t, size):
        s = t // WAVES
        count = 2 * size - 1
        update[...] = jnp.zeros_like(update)
        where_from = [(tp, y)] + a_peers(size)
        for n in range(count):
            own = head_cols(size, *where_from[n])
            update[...] += jnp.dot(
                heads[t, :, own], w_out[own, :], preferred_element_type=jnp.float32
            )
            a_arrival(t, n, size).wait_recv()
        last = head_cols(size, *where_from[count])

        w = t % WAVES
        length = len_ref[w, s]
        position = lax.broadcasted_iota(jnp.int32, (ROWS, 1), 0)
        token_ok = (position >= M) & (position - M < length)
        factor = mix_ref[0] / length.astype(jnp.float32)

        for c in range(2):
            for k in range(0, part_width, 512):
                cols = slice(c * part_width + k, c * part_width + k + 512)
                out = update[:, cols] + jnp.dot(
                    heads[t, :, last], w_out[last, cols], preferred_element_type=jnp.float32
                )
                out = (blocks[t, tp, y, :, cols].astype(jnp.float32) + out).astype(jnp.bfloat16)
                result[t, :, cols] = out
                summed = jnp.where(token_ok, out.astype(jnp.float32), 0.0)
                pool_row[:, cols] = jnp.sum(summed, 0, keepdims=True) * factor

            @pl.when(near)
            def _():
                for n in (3, 2, 1, 0):
                    b_copy(t, n, c).start()

            if size == 2:

                @pl.when(sec == 1)
                def _():
                    for n in range(2):
                        h_copy(t, n, c).start()

                @pl.when((sec == NSEC - 1) & (s == 0))
                def _():
                    for n in range(4):
                        m_copy(t, n, c).start()

    def mix(t, carry):
        @pl.when(wide)
        def _():
            attend(t, 4)

        @pl.when(sec >= 1)
        def _():
            attend(t, 2)

        return carry

    def close(t, carry):
        s = t // WAVES
        w = t % WAVES

        @pl.when(wide)
        def _():
            output(t, 4)

        @pl.when(sec >= 1)
        def _():
            output(t, 2)

        @pl.when((sec == 0) & (t == WAVES - 1))
        def _():
            for document in range(WAVES):
                for n in range(7):
                    token_copy(n, document).start()

        @pl.when(s == 1)
        def _():
            for k in range(width // 128):
                pool[w, k : k + 1, :] = pool_row[:, k * 128 : (k + 1) * 128]

            @pl.when(sec < NSEC - 1)
            def _():
                pool_copy(w).start()

            @pl.when(sec == NSEC - 1)
            def _():
                for index in range(NSEC - 1):
                    remote(
                        pool.at[w],
                        pool_in.at[index, w],
                        pool_send.at[w],
                        pool_recv.at[index, w],
                        where(0, tp, doc),
                    ).wait_recv()
                summed = pool[w] + pool_in[0, w] + pool_in[1, w] + pool_in[2, w]
                total[w] = summed

                @pl.when(w == 0)
                def _():
                    total_copy(0, 0).start()
                    total_copy(0, 2).start()

                @pl.when(w == 1)
                def _():
                    total_copy(1, 1).start()
                    cast[...] = summed

        return carry

    def segment(s, carry):
        lax.fori_loop(s * WAVES, (s + 1) * WAVES, mix, 0)
        lax.fori_loop(s * WAVES, (s + 1) * WAVES, close, 0)
        return carry

    lax.fori_loop(0, SEGS, segment, 0)

    core = sec % 2
    base = sec - core
    n_docs = NY * NZ

    @pl.when(sec < NSEC - 1)
    def _():
        remote(
            total.at[0], cast, total_send.at[0, 0], total_recv, where(NSEC - 1, tp, doc)
        ).wait_recv()

    def cast_copy(k, which):
        to = base + core if which == 0 else base + 1 - core
        return remote(
            cast,
            out_ref.at[2 * doc + core],
            cast_send.at[which, k],
            cast_recv.at[core, doc],
            where(to, tp, (doc + k) % n_docs),
        )

    cast_copy(0, 1).start()

    def send_row(k, carry):
        cast_copy(k, 0).start()
        cast_copy(k, 1).start()
        return carry

    lax.fori_loop(1, n_docs, send_row, 0)
    out_ref[2 * doc + core] = cast[...]

    def row_arrival(c, d):
        return remote(
            cast, out_ref.at[2 * d + c], cast_send.at[0, 0], cast_recv.at[c, d], where(base + 1 - core, tp, doc)
        )

    row_arrival(1 - core, doc).wait_recv()

    def take_row(k, carry):
        d = (doc + k) % n_docs
        row_arrival(core, d).wait_recv()
        row_arrival(1 - core, d).wait_recv()
        return carry

    lax.fori_loop(1, n_docs, take_row, 0)

    cast_copy(0, 1).wait_send()

    def sent_row(k, carry):
        cast_copy(k, 0).wait_send()
        cast_copy(k, 1).wait_send()
        return carry

    lax.fori_loop(1, n_docs, sent_row, 0)

    @pl.when(sec > 0)
    def _():
        for s in range(SEGS):
            part_copy(s).wait_send()

    @pl.when(sec == 0)
    def _():
        for w in range(WAVES):
            for n in range(7):
                first_copy(n, w, 0).wait_send()
                first_copy(n, w, 1).wait_send()
                token_copy(n, w).wait_send()

    def sent_task(t, carry):
        @pl.when(wide)
        def _():
            for n in range(7):
                a_copy(t, n, 4).wait_send()

        @pl.when(sec >= 1)
        def _():
            for n in range(3):
                a_copy(t, n, 2).wait_send()

        @pl.when(near)
        def _():
            for n in range(4):
                b_copy(t, n, 0).wait_send()
                b_copy(t, n, 1).wait_send()

        @pl.when(sec == 1)
        def _():
            for n in range(2):
                h_copy(t, n, 0).wait_send()
                h_copy(t, n, 1).wait_send()

        @pl.when((sec == NSEC - 1) & (t < WAVES))
        def _():
            for n in range(4):
                m_copy(t, n, 0).wait_send()
                m_copy(t, n, 1).wait_send()

        @pl.when(sec == 2)
        def _():
            for n in range(2):
                forward(t, n, all_rows, 0).wait_send()
                forward(t, n, all_rows, 1).wait_send()

        @pl.when((sec == 0) & (t >= WAVES))
        def _():
            for n in range(4):
                forward(t, n, pl.ds(0, M), 0).wait_send()
                forward(t, n, pl.ds(0, M), 1).wait_send()

        return carry

    lax.fori_loop(0, SEGS * WAVES, sent_task, 0)

    @pl.when(sec < NSEC - 1)
    def _():
        for w in range(WAVES):
            pool_copy(w).wait_send()

    @pl.when(sec == NSEC - 1)
    def _():
        total_copy(0, 0).wait_send()
        total_copy(0, 2).wait_send()
        total_copy(1, 1).wait_send()


def body(
    token_ids,
    seg_lengths,
    emb_table,
    mem_init,
    norm_gain,
    w_query,
    w_key,
    w_value,
    w_out,
    layer_mix,
):
    doc_local = token_ids.shape[0]
    vocab_rows, width = emb_table.shape
    depth, head_cols = w_query.shape[1:]
    half, quarter = head_cols // 2, head_cols // 4
    n_tasks = SEGS * WAVES
    dma = pltpu.SemaphoreType.DMA
    bf16, f32 = jnp.bfloat16, jnp.float32
    any_space = pl.BlockSpec(memory_space=pl.ANY)
    vmem = pl.BlockSpec(memory_space=pltpu.VMEM)
    lanes = width // 128
    rows = pl.pallas_call(
        kernel,
        out_shape=jax.ShapeDtypeStruct((NY * NZ * WAVES, lanes, 128), f32),
        in_specs=[any_space] * 10,
        out_specs=vmem,
        scratch_shapes=[
            pltpu.VMEM((WAVES, SEGS, L), jnp.int32),
            pltpu.VMEM((vocab_rows, width), bf16),
            pltpu.VMEM((n_tasks * L, vocab_rows), bf16),
            pltpu.VMEM((M, width), bf16),
            pltpu.VMEM((2, 1, width), f32),
            pltpu.SMEM((doc_local, SEGS), jnp.int32),
            pltpu.SMEM((1,), f32),
            pltpu.VMEM((2 * width, 3 * half), bf16),
            pltpu.VMEM((2 * width, 3 * quarter), bf16),
            pltpu.VMEM((2 * head_cols, width), bf16),
            pltpu.VMEM((n_tasks, 2, NY, ROWS, width), bf16),
            pltpu.VMEM((4 * ROWS, width), bf16),
            pltpu.VMEM((3, 2 * ROWS, half), f32),
            pltpu.VMEM((3, 4 * ROWS, quarter), f32),
            pltpu.VMEM((3, 2 * ROWS, half), bf16),
            pltpu.VMEM((3, 4 * ROWS, quarter), bf16),
            pltpu.VMEM((n_tasks, 2, ROWS, half), bf16),
            pltpu.VMEM((n_tasks, 4, ROWS, quarter), bf16),
            pltpu.VMEM((n_tasks, ROWS, 2 * head_cols), bf16),
            pltpu.VMEM((ROWS, width), f32),
            pltpu.VMEM((n_tasks, ROWS, width), bf16),
            pltpu.VMEM((NSEC, SEGS, WAVES, L, width), bf16),
            pltpu.VMEM((NY, 8, 128), jnp.int32),
            pltpu.VMEM((1, width), f32),
            pltpu.VMEM((WAVES, lanes, 128), f32),
            pltpu.VMEM((NSEC - 1, WAVES, lanes, 128), f32),
            pltpu.VMEM((WAVES, lanes, 128), f32),
            pltpu.VMEM((lanes, 128), f32),
            dma((11,)),
            dma((3, 3)),
            dma((3, 3)),
            dma((2, 4, 2)),
            dma((2, 4, 2)),
            dma((8, 2)),
            dma((8, 2)),
            dma((3,)),
            dma((3,)),
            dma((SEGS,)),
            dma((NSEC - 1, SEGS)),
            dma((WAVES, 7, 2)),
            dma((WAVES, 7)),
            dma((WAVES, 8)),
            dma((n_tasks, 4, 2)),
            dma((n_tasks, 8, 2)),
            dma((n_tasks, 4, 2)),
            dma((n_tasks, 7)),
            dma((n_tasks, 8)),
            dma((WAVES,)),
            dma((NSEC - 1, WAVES)),
            dma((WAVES, 2)),
            dma,
            dma((2, NY * NZ)),
            dma((2, NY * NZ)),
            pltpu.SemaphoreType.REGULAR,
        ],
        compiler_params=pltpu.CompilerParams(
            has_side_effects=True, collective_id=0, vmem_limit_bytes=67000000
        ),
    )(
        token_ids,
        emb_table,
        mem_init,
        norm_gain,
        seg_lengths,
        layer_mix,
        w_query[0],
        w_key[0],
        w_value[0],
        w_out[0],
    )
    return rows.reshape(NY * NZ * WAVES, width)


def solution(mesh):
    return jax.shard_map(
        body,
        mesh=mesh,
        in_specs=(
            P("doc", None, None),
            P("doc", None),
            P("section", "tp"),
            P(None, "tp"),
            P("section", None),
            P("section", "doc", "tp"),
            P("section", "doc", "tp"),
            P("section", "doc", "tp"),
            P("section", None, "tp"),
            P("section"),
        ),
        out_specs=P(None, "tp"),
        check_vma=False,
    )
```

```python
import math

import jax
import jax.numpy as jnp
from jax import lax
from jax.experimental import pallas as pl
from jax.experimental.pallas import tpu as pltpu
from jax.sharding import PartitionSpec as P

HD = 128
M = 16
L = 32
SEGS = 2
ROWS = M + L
EPSILON = 1e-05
NEGATIVE = -1e30

NY = 4
NZ = 8
KEEP_EARLY = 96
KEEP_LATE = 80
WAVES = 2
NSEC = 4


def kernel(
    ids_hbm,
    table_hbm,
    mem_hbm,
    gain_hbm,
    len_hbm,
    mix_hbm,
    wq_ref,
    wk_ref,
    wv_ref,
    wo_ref,
    out_ref,
    ids_ref,
    table,
    picks,
    mem_ref,
    gain_ref,
    len_ref,
    mix_ref,
    weights2,
    weights4,
    w_out,
    blocks,
    scaled,
    sum2,
    sum4,
    qkv2,
    qkv4,
    mixed2,
    mixed4,
    heads,
    update,
    result,
    parts,
    lens,
    pool_row,
    pool,
    pool_in,
    total,
    cast,
    local_sem,
    y_send,
    y_recv,
    z_send,
    z_recv,
    f_send,
    f_recv,
    len_send,
    len_recv,
    part_send,
    part_recv,
    first_send,
    tok_send,
    tok_recv,
    x_send,
    x_recv,
    r_send,
    a_send,
    a_recv,
    pool_send,
    pool_recv,
    total_send,
    total_recv,
    cast_send,
    cast_recv,
    go_sem,
):
    sec = lax.axis_index("section")
    tp = lax.axis_index("tp")
    doc = lax.axis_index("doc")
    z = doc // NY
    y = doc % NY
    bit = y % 2
    y_mate = y + 1 - 2 * bit
    y_twin = NY - 1 - y
    y_far = NY - 1 - y_mate
    kind = ((y + 1) // 2) % 2
    width = blocks.shape[-1]
    depth = wq_ref.shape[0]
    slab = NY * depth
    pair = 2 * depth
    heads_cols = wq_ref.shape[1]

    def where(section, t, d):
        return {"section": section, "tp": t, "doc": d}

    def remote(src, dst, send, recv, to):
        return pltpu.make_async_remote_copy(
            src_ref=src,
            dst_ref=dst,
            send_sem=send,
            recv_sem=recv,
            device_id=to,
            device_id_type=pl.DeviceIdType.MESH,
        )

    def at_y(other):
        return where(sec, tp, z * NY + other)

    wide = sec == 0
    ring = [y, y_mate, y_twin, y_far]
    sources = (wq_ref, wk_ref, wv_ref)
    own_row = pl.multiple_of(doc * depth, depth)

    class Weights:
        def __init__(self, size, keep=KEEP_LATE):
            self.size = size
            self.keep = keep
            self.both = depth - keep
            self.per = heads_cols // size
            self.ref = weights4 if size == 4 else weights2

        def kind(self, other):
            return other if self.size == 4 else ((other + 1) // 2) % 2

        def column(self, other):
            return pl.ds(pl.multiple_of(self.kind(other) * self.per, self.per), self.per)

        def own_copies(self):
            return [
                pltpu.make_async_copy(
                    ref.at[:, self.column(y)],
                    self.ref.at[pl.ds(own_row, depth), pl.ds(j * self.per, self.per)],
                    local_sem.at[j],
                )
                for j, ref in enumerate(sources)
            ]

        def y_copies(self):
            out = []
            for n, other in enumerate(ring[1:]):
                for j, ref in enumerate(sources):
                    first, rows = 0, depth
                    if self.size == 2 and n > 0:
                        first, rows = pl.multiple_of((1 - bit) * self.keep, 16), self.both
                    src = ref.at[pl.ds(first, rows), self.column(other)]
                    dst = self.ref.at[
                        pl.ds(pl.multiple_of(own_row + first, 16), rows),
                        pl.ds(j * self.per, self.per),
                    ]
                    out.append(remote(src, dst, y_send.at[n, j], y_recv.at[n, j], at_y(other)))
            return out

        def rows(self, zz, part):
            if self.size == 4:
                return pl.ds(pl.multiple_of(zz * slab + part * pair, pair), pair)
            if part == 0:
                return pl.ds(pl.multiple_of(zz * slab + (y // 2) * pair, pair), pair)
            return pl.ds(pl.multiple_of(zz * slab + (1 - y // 2) * pair + self.keep, 16), 2 * self.both)

        def z_copy(self, way, step, part, arrival=False):
            ahead = step + 1 if arrival else step
            zz = (z + NZ - ahead) % NZ if way == 0 else (z + ahead) % NZ
            ref = self.ref.at[self.rows(zz, part)]
            to = (z + 1) % NZ if way == 0 else (z + NZ - 1) % NZ
            return remote(
                ref,
                ref,
                z_send.at[way, step, part],
                z_recv.at[way, step, part],
                where(sec, tp, to * NY + y),
            )

        def f_copies(self, slot, zz):
            if self.size == 4:
                return []
            base = zz * slab + (y // 2) * pair
            out = []
            for h, start in enumerate((base, base + pair - self.keep)):
                ref = self.ref.at[pl.ds(pl.multiple_of(start, 16), self.keep)]
                out.append(
                    remote(ref, ref, f_send.at[slot, h], f_recv.at[slot, h], at_y(y_twin))
                )
            return out

        def start_y(self):
            for copy in self.y_copies():
                copy.start()

        def start_z(self):
            for copy in self.own_copies():
                copy.wait()
            for copy in self.y_copies():
                copy.wait_recv()
            for part in range(2):
                for way in range(2):
                    self.z_copy(way, 0, part).start()
            for copy in self.f_copies(0, z):
                copy.start()

        def relay(self, step):
            for part in range(2):
                for way in range(2):
                    if z_sent(way, step, part):
                        self.z_copy(way, step, part, arrival=True).wait_recv()
                        if z_sent(way, step + 1, part):
                            self.z_copy(way, step + 1, part).start()
                        if part == 0:
                            ahead = step + 1
                            zz = (z + NZ - ahead) % NZ if way == 0 else (z + ahead) % NZ
                            for copy in self.f_copies(1 + step + 4 * way, zz):
                                copy.start()

        def finish(self):
            for step in range(4):
                for part in range(2):
                    for way in range(2):
                        if z_sent(way, step, part):
                            self.z_copy(way, step, part).wait_send()
            for k in range(8):
                for copy in self.f_copies(k, z):
                    copy.wait()
            for copy in self.y_copies():
                copy.wait_send()

    def z_sent(way, step, part):
        return step < 3 or (step == 3 and part == way)

    def each(condition, action):
        @pl.when(condition & wide)
        def _():
            action(Weights(4))

        @pl.when(condition & (sec == 1))
        def _():
            action(Weights(2, KEEP_EARLY))

        @pl.when(condition & (sec >= 2))
        def _():
            action(Weights(2))

    slot = tp * NY + y
    peers = [(t, other) for t in (tp, 1 - tp) for other in ring][1:]

    part_width = width // 2

    def part_cols(c):
        return pl.ds(c * part_width, part_width)

    def first_copy(n, w, c):
        t, other = peers[n]
        ref = blocks.at[w, tp, y, :, part_cols(c)]
        return remote(
            ref, ref, first_send.at[w, n, c], x_recv.at[w, slot, c], where(sec, t, z * NY + other)
        )

    def token_copy(n, w):
        t, other = peers[n]
        ref = blocks.at[WAVES + w, tp, y, pl.ds(M, L)]
        return remote(
            ref, ref, tok_send.at[w, n], tok_recv.at[w, slot], where(sec, t, z * NY + other)
        )

    def part_copy(s):
        index = jnp.maximum(sec - 1, 0)
        return remote(
            parts.at[NSEC - 1, s], parts.at[index, s], part_send.at[s], part_recv.at[index, s], where(0, tp, doc)
        )

    def len_copy(n, arrival=False):
        index = ring[n + 1] if arrival else y
        ref = lens.at[index]
        return remote(ref, ref, len_send.at[n], len_recv.at[n], at_y(ring[n + 1]))


    small_copies = [
        pltpu.make_async_copy(len_hbm, len_ref, local_sem.at[4]),
        pltpu.make_async_copy(mix_hbm, mix_ref, local_sem.at[5]),
        pltpu.make_async_copy(ids_hbm, ids_ref, local_sem.at[6]),
        pltpu.make_async_copy(mem_hbm, mem_ref, local_sem.at[7]),
        pltpu.make_async_copy(gain_hbm.at[:, pl.ds(0, width)], gain_ref.at[0], local_sem.at[8]),
        pltpu.make_async_copy(gain_hbm.at[:, pl.ds(width, width)], gain_ref.at[1], local_sem.at[9]),
    ]
    table_copy = pltpu.make_async_copy(table_hbm, table, local_sem.at[10])
    wo_copy = pltpu.make_async_copy(wo_ref, w_out, local_sem.at[3])
    for copy in small_copies:
        copy.start()
    for group in (Weights(4), Weights(2)):

        @pl.when(wide if group.size == 4 else sec >= 1)
        def _():
            for copy in group.own_copies():
                copy.start()


    next_sec = (sec + 1) % NSEC
    last_sec = (sec + NSEC - 1) % NSEC
    greeted = [where(sec, t, z * NY + other) for t, other in peers]
    greeted += [where(sec, tp, (z + step) % NZ * NY + y) for step in (1, NZ - 1)]
    greeted += [
        where(to, t, z * NY + other)
        for to in (next_sec, last_sec)
        for t in (tp, 1 - tp)
        for other in ring
    ]
    greeted += [where((sec + 2) % NSEC, tp, doc)]
    barrier = pltpu.get_barrier_semaphore()
    for to in greeted:
        pl.semaphore_signal(barrier, inc=1, device_id=to, device_id_type=pl.DeviceIdType.MESH)
    pl.semaphore_wait(barrier, len(greeted))

    each(sec >= 0, Weights.start_y)
    table_copy.start()
    for copy in small_copies:
        copy.wait()

    lane = lax.broadcasted_iota(jnp.int32, (1, 128), 1)
    mine = (lane >= bit * ROWS) & (lane < bit * ROWS + ROWS)
    for t in range(SEGS * WAVES):
        lens[y, t : t + 1, :] = jnp.where(mine, len_ref[t % WAVES, t // WAVES], 0)
    for t in range(SEGS * WAVES, 8):
        lens[y, t : t + 1, :] = jnp.zeros((1, 128), jnp.int32)
    for n in range(3):
        len_copy(n).start()

    even = sec % 2 == 0
    odd = sec % 2 == 1
    urgent = sec < 2
    each(sec <= 2, Weights.start_z)

    n_ids = SEGS * WAVES * L
    eye = lax.broadcasted_iota(jnp.int32, (L, L), 0) == lax.broadcasted_iota(jnp.int32, (L, L), 1)
    columns = [
        jnp.sum(
            jnp.where(eye, ids_ref[w, s : s + 1, :].astype(jnp.float32), 0.0), -1, keepdims=True
        )
        for s in range(SEGS)
        for w in range(WAVES)
    ]
    wanted = jnp.concatenate(columns, axis=0).astype(jnp.int32) - sec * table.shape[0]
    for k in range(0, table.shape[0], 512):
        place = lax.broadcasted_iota(jnp.int32, (n_ids, 512), 1) + k
        picks[:, k : k + 512] = jnp.where(place == wanted, 1.0, 0.0).astype(jnp.bfloat16)
    def let_go():
        pl.semaphore_signal(
            go_sem, inc=1, device_id=where(sec + 1, tp, doc), device_id_type=pl.DeviceIdType.MESH
        )

    each(urgent, lambda group: group.relay(0))
    table_copy.wait()
    wo_copy.start()

    def pick(j, carry):
        cols = pl.ds(pl.multiple_of(j * 512, 512), 512)
        rows = jnp.dot(picks[...], table[:, cols], preferred_element_type=jnp.float32)
        parts[NSEC - 1, :, :, :, cols] = rows.astype(jnp.bfloat16).reshape(SEGS, WAVES, L, 512)
        return carry

    lax.fori_loop(0, width // 1024, pick, 0)
    each(urgent, lambda group: group.relay(1))
    lax.fori_loop(width // 1024, width // 512, pick, 0)

    @pl.when(sec > 0)
    def _():
        for s in range(SEGS):
            part_copy(s).start()

    @pl.when(sec == 0)
    def _():
        for s in range(SEGS):
            for index in range(NSEC - 1):
                remote(
                    parts.at[NSEC - 1, s],
                    parts.at[index, s],
                    part_send.at[s],
                    part_recv.at[index, s],
                    where(1, tp, doc),
                ).wait_recv()
            for w in range(WAVES):
                rows = parts[0, s, w] + parts[1, s, w] + parts[2, s, w] + parts[3, s, w]
                blocks[s * WAVES + w, tp, y, M:, :] = rows
                if s == 0:
                    blocks[w, tp, y, :M, :] = mem_ref[...]
            for w in range(WAVES):
                for n in range(7):
                    if s == 0:
                        first_copy(n, w, 0).start()
                        first_copy(n, w, 1).start()

    @pl.when(sec == 0)
    def _():
        Weights(4).relay(2)

    @pl.when(sec == 2)
    def _():
        group = Weights(2)
        for step in range(3):
            group.relay(step)
        let_go()

    @pl.when(sec == 1)
    def _():
        Weights(2, KEEP_EARLY).relay(2)

    @pl.when(sec == 3)
    def _():
        pl.semaphore_wait(go_sem, 1)
        group = Weights(2)
        group.start_z()
        for step in range(3):
            group.relay(step)

    each(sec >= 0, lambda group: group.relay(3))
    each(sec >= 0, Weights.finish)
    wo_copy.wait()
    for n in range(3):
        len_copy(n).wait_send()
        len_copy(n, arrival=True).wait_recv()

    near = sec % 2 == 0

    def members(size):
        return ring if size == 4 else ring[:2]

    def b_copy(t, n, c):
        to_tp = tp if n < 2 else 1 - tp
        return remote(
            result.at[t, :, part_cols(c)],
            blocks.at[t, tp, y, :, part_cols(c)],
            x_send.at[t, n, c],
            x_recv.at[t, slot, c],
            where((sec + 1) % NSEC, to_tp, z * NY + ring[n % 2]),
        )

    def h_copy(t, n, c):
        return remote(
            result.at[t, :, part_cols(c)],
            blocks.at[t, tp, y, :, part_cols(c)],
            x_send.at[t, n, c],
            x_recv.at[t, slot, c],
            where((sec + 1) % NSEC, 1 - tp, z * NY + ring[n]),
        )

    def m_copy(t, n, c):
        return remote(
            result.at[t, pl.ds(0, M), part_cols(c)],
            blocks.at[t + WAVES, tp, y, pl.ds(0, M), part_cols(c)],
            x_send.at[t, n, c],
            x_recv.at[t + WAVES, slot, c],
            where(0, 1 - tp, z * NY + ring[n]),
        )

    def forward(t, n, rows, c):
        ref = blocks.at[t, 1 - tp, ring[n], rows, part_cols(c)]
        return remote(
            ref,
            ref,
            r_send.at[t, n, c],
            x_recv.at[t, (1 - tp) * NY + ring[n], c],
            where(sec, 1 - tp, doc),
        )

    def arrival(t, half, other, rows, c):
        ref = blocks.at[t, half, other, rows, part_cols(c)]
        sem = x_recv.at[t, half * NY + other, c]
        return remote(ref, ref, x_send.at[0, 0, 0], sem, at_y(y_mate))

    def token_arrival(t, half, other):
        ref = blocks.at[t, half, other, pl.ds(M, L)]
        sem = tok_recv.at[t - WAVES, half * NY + other]
        return remote(ref, ref, x_send.at[0, 0, 0], sem, at_y(y_mate))

    def head_cols(size, t, other):
        per = heads_cols // size
        start = t * heads_cols + Weights(size).kind(other) * per
        return pl.ds(pl.multiple_of(start, per), per)

    def a_peers(size):
        return [(t, other) for t in (tp, 1 - tp) for other in members(size)][1:]

    def mixed_rows(size, t, other):
        return mixed4.at[t, other] if size == 4 else mixed2.at[t, other % 2]

    def a_copy(t, n, size):
        to_tp, other = a_peers(size)[n]
        return remote(
            mixed_rows(size, t, other),
            heads.at[t, :, head_cols(size, tp, y)],
            a_send.at[t, n],
            a_recv.at[t, slot],
            where(sec, to_tp, z * NY + other),
        )

    def a_arrival(t, n, size):
        from_tp, other = a_peers(size)[n]
        return remote(
            mixed_rows(size, t, other),
            heads.at[t, :, head_cols(size, from_tp, other)],
            a_send.at[t, n],
            a_recv.at[t, from_tp * NY + other],
            at_y(y_mate),
        )

    def pool_copy(w):
        index = jnp.minimum(sec, NSEC - 2)
        return remote(
            pool.at[w], pool_in.at[index, w], pool_send.at[w], pool_recv.at[index, w], where(NSEC - 1, tp, doc)
        )

    def total_copy(w, to):
        return remote(
            total.at[w], cast, total_send.at[w, to // 2], total_recv, where(to, tp, doc)
        )

    all_rows = pl.ds(0, ROWS)
    scale = 1.0 / math.sqrt(HD)

    def attend(t, size):
        s = t // WAVES
        per = heads_cols // size
        docs = members(size)
        n_rows = size * ROWS
        group = Weights(size)
        far = near & ((sec > 0) | (s == 1))
        first = jnp.where(far, 1 - tp, tp)

        def wait_half(n):
            half = first if n == 0 else 1 - first

            def take(others, rows, onward):
                for c in range(2):
                    for k, other in enumerate(others):
                        arrival(t, half, other, rows, c).wait_recv()
                        if onward:
                            forward(t, k, rows, c).start()

            @pl.when(odd)
            def _():
                take(docs, all_rows, False)

            if size == 2:

                @pl.when(even)
                def _():
                    take(docs, all_rows, n == 0)

                return

            @pl.when(even & (s == 0))
            def _():
                take(docs[1 - n :], all_rows, False)

            @pl.when(even & (s == 1))
            def _():
                for other in docs[n:]:
                    token_arrival(t, half, other).wait_recv()
                take(docs, pl.ds(0, M), n == 0)

        step = 128
        total_sum = sum2 if size == 2 else sum4
        qkv = qkv2 if size == 2 else qkv4
        base = pl.multiple_of(y // 2 * 2, 2) if size == 2 else 0
        square = jnp.zeros((n_rows, step), jnp.float32)
        for n in range(2):
            half = first if n == 0 else 1 - first
            wait_half(n)
            for c in range(0, width, step):
                x = blocks[t, half, pl.ds(base, size), :, c : c + step]
                x = x.reshape(n_rows, step).astype(jnp.float32)
                square = square + x * x
                scaled[:n_rows, c : c + step] = (x * gain_ref[half, :, c : c + step]).astype(
                    jnp.bfloat16
                )
            if n == 1:
                mean_square = jnp.sum(square, -1, keepdims=True) * (1.0 / (2 * width))
                inverse = lax.rsqrt(mean_square + EPSILON)
            rows = pl.ds(pl.multiple_of(half * width, width), width)

            for j in range(3):
                cols = slice(j * per, (j + 1) * per)
                out = jnp.dot(
                    scaled[:n_rows, :], group.ref[rows, cols], preferred_element_type=jnp.float32
                )
                if n == 0:
                    total_sum[j] = out
                else:
                    qkv[j] = ((total_sum[j] + out) * inverse).astype(jnp.bfloat16)

        shape = (2 * ROWS, 2 * ROWS)
        row = lax.broadcasted_iota(jnp.int32, shape, 0)
        col = lax.broadcasted_iota(jnp.int32, shape, 1)
        row_doc = (row >= ROWS).astype(jnp.int32)
        col_doc = (col >= ROWS).astype(jnp.int32)
        i = row - ROWS * row_doc
        j = col - ROWS * col_doc
        ordered = (row_doc == col_doc) & ((j < M) | (i < M) | (j <= i))
        for p in range(size // 2):
            d = base + 2 * p
            lengths = (lens[d, pl.ds(t, 1), :] + lens[d + 1, pl.ds(t, 1), :])[:, : 2 * ROWS]
            allowed = ordered & ((j < M) | (j - M < lengths))
            own = slice(p * 2 * ROWS, (p + 1) * 2 * ROWS)
            for h in range(per // HD):
                cols = slice(h * HD, (h + 1) * HD)
                scores = (
                    lax.dot_general(
                        qkv[0, own, cols],
                        qkv[1, own, cols],
                        (((1,), (1,)), ((), ())),
                        preferred_element_type=jnp.float32,
                    )
                    * scale
                )
                scores = jnp.where(allowed, scores, NEGATIVE)
                exps = jnp.where(allowed, jnp.exp(scores), 0.0)
                probs = (exps / jnp.sum(exps, -1, keepdims=True)).astype(jnp.bfloat16)
                out = jnp.dot(probs, qkv[2, own, cols], preferred_element_type=jnp.float32)
                out = out.astype(jnp.bfloat16).reshape(2, ROWS, HD)
                if size == 4:
                    mixed4[t, 2 * p : 2 * p + 2, :, cols] = out
                else:
                    mixed2[t, :, :, cols] = out

        count = 2 * size - 1
        for n in reversed(range(count)):
            a_copy(t, n, size).start()
        heads[t, :, head_cols(size, tp, y)] = mixed4[t, y] if size == 4 else mixed2[t, bit]
        where_from = [(tp, y)] + a_peers(size)
        for n in range(count):
            own = head_cols(size, *where_from[n])
            product = jnp.dot(heads[t, :, own], w_out[own, :], preferred_element_type=jnp.float32)
            update[...] = product if n == 0 else update[...] + product
            a_arrival(t, n, size).wait_recv()
        last = head_cols(size, *where_from[count])

        w = t % WAVES
        length = len_ref[w, s]
        position = lax.broadcasted_iota(jnp.int32, (ROWS, 1), 0)
        token_ok = (position >= M) & (position - M < length)
        factor = mix_ref[0] / length.astype(jnp.float32)

        for c in range(2):
            for k in range(0, part_width, 512):
                cols = slice(c * part_width + k, c * part_width + k + 512)
                out = update[:, cols] + jnp.dot(
                    heads[t, :, last], w_out[last, cols], preferred_element_type=jnp.float32
                )
                out = (blocks[t, tp, y, :, cols].astype(jnp.float32) + out).astype(jnp.bfloat16)
                result[t, :, cols] = out
                summed = jnp.where(token_ok, out.astype(jnp.float32), 0.0)
                pool_row[:, cols] = jnp.sum(summed, 0, keepdims=True) * factor

            @pl.when(near)
            def _():
                for n in (3, 2, 1, 0):
                    b_copy(t, n, c).start()

            if size == 2:

                @pl.when(sec == 1)
                def _():
                    for n in range(2):
                        h_copy(t, n, c).start()

                @pl.when((sec == NSEC - 1) & (s == 0))
                def _():
                    for n in range(4):
                        m_copy(t, n, c).start()

    def task(t, carry):
        s = t // WAVES
        w = t % WAVES

        @pl.when(wide)
        def _():
            attend(t, 4)

        @pl.when(sec >= 1)
        def _():
            attend(t, 2)

        @pl.when((sec == 0) & (t == WAVES - 1))
        def _():
            for document in range(WAVES):
                for n in range(7):
                    token_copy(n, document).start()

        @pl.when(s == 1)
        def _():
            for k in range(width // 128):
                pool[w, k : k + 1, :] = pool_row[:, k * 128 : (k + 1) * 128]

            @pl.when(sec < NSEC - 1)
            def _():
                pool_copy(w).start()

            @pl.when(sec == NSEC - 1)
            def _():
                for index in range(NSEC - 1):
                    remote(
                        pool.at[w],
                        pool_in.at[index, w],
                        pool_send.at[w],
                        pool_recv.at[index, w],
                        where(0, tp, doc),
                    ).wait_recv()
                summed = pool[w] + pool_in[0, w] + pool_in[1, w] + pool_in[2, w]
                total[w] = summed

                @pl.when(w == 0)
                def _():
                    total_copy(0, 0).start()
                    total_copy(0, 2).start()

                @pl.when(w == 1)
                def _():
                    total_copy(1, 1).start()
                    cast[...] = summed

        return carry

    lax.fori_loop(0, SEGS * WAVES, task, 0)

    core = sec % 2
    base = sec - core
    n_docs = NY * NZ

    @pl.when(sec < NSEC - 1)
    def _():
        remote(
            total.at[0], cast, total_send.at[0, 0], total_recv, where(NSEC - 1, tp, doc)
        ).wait_recv()

    def cast_copy(k, which):
        to = base + core if which == 0 else base + 1 - core
        return remote(
            cast,
            out_ref.at[2 * doc + core],
            cast_send.at[which, k],
            cast_recv.at[core, doc],
            where(to, tp, (doc + k) % n_docs),
        )

    cast_copy(0, 1).start()

    def send_row(k, carry):
        cast_copy(k, 0).start()
        cast_copy(k, 1).start()
        return carry

    far = n_docs // 2
    lax.fori_loop(far - NY, far + NY + 1, send_row, 0)
    lax.fori_loop(1, far - NY, send_row, 0)
    lax.fori_loop(far + NY + 1, n_docs, send_row, 0)
    out_ref[2 * doc + core] = cast[...]

    def row_arrival(c, d):
        return remote(
            cast, out_ref.at[2 * d + c], cast_send.at[0, 0], cast_recv.at[c, d], where(base + 1 - core, tp, doc)
        )

    row_arrival(1 - core, doc).wait_recv()

    def take_row(k, carry):
        d = (doc + k) % n_docs
        row_arrival(core, d).wait_recv()
        row_arrival(1 - core, d).wait_recv()
        return carry

    lax.fori_loop(1, n_docs, take_row, 0)

    cast_copy(0, 1).wait_send()

    def sent_row(k, carry):
        cast_copy(k, 0).wait_send()
        cast_copy(k, 1).wait_send()
        return carry

    lax.fori_loop(1, n_docs, sent_row, 0)

    @pl.when(sec > 0)
    def _():
        for s in range(SEGS):
            part_copy(s).wait_send()

    @pl.when(sec == 0)
    def _():
        for w in range(WAVES):
            for n in range(7):
                first_copy(n, w, 0).wait_send()
                first_copy(n, w, 1).wait_send()
                token_copy(n, w).wait_send()

    def sent_task(t, carry):
        @pl.when(wide)
        def _():
            for n in range(7):
                a_copy(t, n, 4).wait_send()

        @pl.when(sec >= 1)
        def _():
            for n in range(3):
                a_copy(t, n, 2).wait_send()

        @pl.when(near)
        def _():
            for n in range(4):
                b_copy(t, n, 0).wait_send()
                b_copy(t, n, 1).wait_send()

        @pl.when(sec == 1)
        def _():
            for n in range(2):
                h_copy(t, n, 0).wait_send()
                h_copy(t, n, 1).wait_send()

        @pl.when((sec == NSEC - 1) & (t < WAVES))
        def _():
            for n in range(4):
                m_copy(t, n, 0).wait_send()
                m_copy(t, n, 1).wait_send()

        @pl.when(sec == 2)
        def _():
            for n in range(2):
                forward(t, n, all_rows, 0).wait_send()
                forward(t, n, all_rows, 1).wait_send()

        @pl.when((sec == 0) & (t >= WAVES))
        def _():
            for n in range(4):
                forward(t, n, pl.ds(0, M), 0).wait_send()
                forward(t, n, pl.ds(0, M), 1).wait_send()

        return carry

    lax.fori_loop(0, SEGS * WAVES, sent_task, 0)

    @pl.when(sec < NSEC - 1)
    def _():
        for w in range(WAVES):
            pool_copy(w).wait_send()

    @pl.when(sec == NSEC - 1)
    def _():
        total_copy(0, 0).wait_send()
        total_copy(0, 2).wait_send()
        total_copy(1, 1).wait_send()


def body(
    token_ids,
    seg_lengths,
    emb_table,
    mem_init,
    norm_gain,
    w_query,
    w_key,
    w_value,
    w_out,
    layer_mix,
):
    doc_local = token_ids.shape[0]
    vocab_rows, width = emb_table.shape
    depth, head_cols = w_query.shape[1:]
    half, quarter = head_cols // 2, head_cols // 4
    n_tasks = SEGS * WAVES
    dma = pltpu.SemaphoreType.DMA
    bf16, f32 = jnp.bfloat16, jnp.float32
    any_space = pl.BlockSpec(memory_space=pl.ANY)
    vmem = pl.BlockSpec(memory_space=pltpu.VMEM)
    lanes = width // 128
    rows = pl.pallas_call(
        kernel,
        out_shape=jax.ShapeDtypeStruct((NY * NZ * WAVES, lanes, 128), f32),
        in_specs=[any_space] * 10,
        out_specs=vmem,
        scratch_shapes=[
            pltpu.VMEM((WAVES, SEGS, L), jnp.int32),
            pltpu.VMEM((vocab_rows, width), bf16),
            pltpu.VMEM((n_tasks * L, vocab_rows), bf16),
            pltpu.VMEM((M, width), bf16),
            pltpu.VMEM((2, 1, width), f32),
            pltpu.SMEM((doc_local, SEGS), jnp.int32),
            pltpu.SMEM((1,), f32),
            pltpu.VMEM((2 * width, 3 * half), bf16),
            pltpu.VMEM((2 * width, 3 * quarter), bf16),
            pltpu.VMEM((2 * head_cols, width), bf16),
            pltpu.VMEM((n_tasks, 2, NY, ROWS, width), bf16),
            pltpu.VMEM((4 * ROWS, width), bf16),
            pltpu.VMEM((3, 2 * ROWS, half), f32),
            pltpu.VMEM((3, 4 * ROWS, quarter), f32),
            pltpu.VMEM((3, 2 * ROWS, half), bf16),
            pltpu.VMEM((3, 4 * ROWS, quarter), bf16),
            pltpu.VMEM((n_tasks, 2, ROWS, half), bf16),
            pltpu.VMEM((n_tasks, 4, ROWS, quarter), bf16),
            pltpu.VMEM((n_tasks, ROWS, 2 * head_cols), bf16),
            pltpu.VMEM((ROWS, width), f32),
            pltpu.VMEM((n_tasks, ROWS, width), bf16),
            pltpu.VMEM((NSEC, SEGS, WAVES, L, width), bf16),
            pltpu.VMEM((NY, 8, 128), jnp.int32),
            pltpu.VMEM((1, width), f32),
            pltpu.VMEM((WAVES, lanes, 128), f32),
            pltpu.VMEM((NSEC - 1, WAVES, lanes, 128), f32),
            pltpu.VMEM((WAVES, lanes, 128), f32),
            pltpu.VMEM((lanes, 128), f32),
            dma((11,)),
            dma((3, 3)),
            dma((3, 3)),
            dma((2, 4, 2)),
            dma((2, 4, 2)),
            dma((8, 2)),
            dma((8, 2)),
            dma((3,)),
            dma((3,)),
            dma((SEGS,)),
            dma((NSEC - 1, SEGS)),
            dma((WAVES, 7, 2)),
            dma((WAVES, 7)),
            dma((WAVES, 8)),
            dma((n_tasks, 4, 2)),
            dma((n_tasks, 8, 2)),
            dma((n_tasks, 4, 2)),
            dma((n_tasks, 7)),
            dma((n_tasks, 8)),
            dma((WAVES,)),
            dma((NSEC - 1, WAVES)),
            dma((WAVES, 2)),
            dma,
            dma((2, NY * NZ)),
            dma((2, NY * NZ)),
            pltpu.SemaphoreType.REGULAR,
        ],
        compiler_params=pltpu.CompilerParams(
            has_side_effects=True, collective_id=0, vmem_limit_bytes=67000000
        ),
    )(
        token_ids,
        emb_table,
        mem_init,
        norm_gain,
        seg_lengths,
        layer_mix,
        w_query[0],
        w_key[0],
        w_value[0],
        w_out[0],
    )
    return rows.reshape(NY * NZ * WAVES, width)


def solution(mesh):
    return jax.shard_map(
        body,
        mesh=mesh,
        in_specs=(
            P("doc", None, None),
            P("doc", None),
            P("section", "tp"),
            P(None, "tp"),
            P("section", None),
            P("section", "doc", "tp"),
            P("section", "doc", "tp"),
            P("section", "doc", "tp"),
            P("section", None, "tp"),
            P("section"),
        ),
        out_specs=P(None, "tp"),
        check_vma=False,
    )
```
